32 devices in a mesh: rep: 8 (over y, x, core), shard: 4 (over z).
Axes of the slice: x: 2, y: 2, z: 4, core: 2. Of those that a mesh axis runs over, the one named last changes fastest.
Arguments:
- inputs: bfloat16 [16, 1024, 1280], P('rep', 'shard'), may hold values from -6 to 6
- lengths: int32 [16], P('rep'), may hold values from 256 to 1024, as said below
- cotangent: bfloat16 [16, 1024, 1280], P('rep', 'shard'), may hold values from -6 to 6
- attn_gain: bfloat16 [2, 1280], P(None, 'shard'), may hold values from 0.5 to 1.5
- attn_shift: bfloat16 [2, 1280], P(None, 'shard'), may hold values from -1.25 to 1.25
- query_weight: bfloat16 [2, 1280, 1280], P(None, 'shard'), may hold values from -0.15625 to 0.15625
- query_bias: bfloat16 [2, 1280], P(None, 'shard'), may hold values from -1.25 to 1.25
- key_weight: bfloat16 [2, 1280, 1280], P(None, 'shard'), may hold values from -0.15625 to 0.15625
- value_weight: bfloat16 [2, 1280, 1280], P(None, 'shard'), may hold values from -0.15625 to 0.15625
- value_bias: bfloat16 [2, 1280], P(None, 'shard'), may hold values from -1.25 to 1.25
- out_weight: bfloat16 [2, 1280, 1280], P(None, 'shard'), may hold values from -2.5 to 2.5
- out_bias: bfloat16 [2, 1280], P(None, 'shard'), may hold values from -1.25 to 1.25
- mlp_gain: bfloat16 [2, 1280], P(None, 'shard'), may hold values from 0.5 to 1.5
- mlp_shift: bfloat16 [2, 1280], P(None, 'shard'), may hold values from -1.25 to 1.25
- up_weight: bfloat16 [2, 1280, 5120], P(None, 'shard'), may hold values from -0.15625 to 0.15625
- up_bias: bfloat16 [2, 5120], P(None, 'shard'), may hold values from -1.25 to 1.25
- down_weight: bfloat16 [2, 5120, 1280], P(None, 'shard'), may hold values from -0.078125 to 0.078125
- down_bias: bfloat16 [2, 1280], P(None, 'shard'), may hold values from -1.25 to 1.25
Outputs:
- output: bfloat16 [16, 1024, 1280], P('rep', 'shard')
- input_grad: float32 [16, 1024, 1280], P('rep', 'shard')
- attn_gain_grad: float32 [2, 1280], P(None, 'shard')
- attn_shift_grad: float32 [2, 1280], P(None, 'shard')
- query_weight_grad: float32 [2, 1280, 1280], P(None, 'shard')
- query_bias_grad: float32 [2, 1280], P(None, 'shard')
- key_weight_grad: float32 [2, 1280, 1280], P(None, 'shard')
- value_weight_grad: float32 [2, 1280, 1280], P(None, 'shard')
- value_bias_grad: float32 [2, 1280], P(None, 'shard')
- out_weight_grad: float32 [2, 1280, 1280], P(None, 'shard')
- out_bias_grad: float32 [2, 1280], P(None, 'shard')
- mlp_gain_grad: float32 [2, 1280], P(None, 'shard')
- mlp_shift_grad: float32 [2, 1280], P(None, 'shard')
- up_weight_grad: float32 [2, 1280, 5120], P(None, 'shard')
- up_bias_grad: float32 [2, 5120], P(None, 'shard')
- down_weight_grad: float32 [2, 5120, 1280], P(None, 'shard')
- down_bias_grad: float32 [2, 1280], P(None, 'shard')
The draws below stay inside these ranges and needn't reach their ends.
Inputs may be any that keep to these rules, and one draw needn't show every extreme that they name: `lengths`: of the 2 clips on one index of rep, one (which, drawn from the seed) has all 1024 tokens valid.
All inputs are finite; a program needn't handle non-finite values.
Results may differ from the reference program's by a relative error of at most 0.02.
Values may be sent and summed in bfloat16 or wider, within the bound.
A program may use at most 576 MiB of HBM per device.

```python
import jax
import jax.numpy as jnp
from jax import lax

D = 1280
H = 16
HD = 80
FF = 5120
LEN = 1024
LAYERS = 2
CLIP_GRP = 2
CLIPS = 16
N_REP = 8


def draw_lengths(key, part):
    key_length, key_choose = jax.random.split(jax.random.fold_in(key, 7))
    count = CLIP_GRP * N_REP
    drawn = jax.random.randint(key_length, (count,), LEN // 4, LEN + 1)
    chosen = jax.random.randint(key_choose, (N_REP,), 0, CLIP_GRP)
    position = jnp.arange(count, dtype=jnp.int32)
    full_clip = position % CLIP_GRP == chosen[position // CLIP_GRP]
    return jnp.where(full_clip, LEN, drawn).astype(jnp.int32)


def block_levels(own_key, extent, cuts, least, high):
    def one(axis_at, blocks):
        draws = jax.random.uniform(jax.random.fold_in(jax.random.fold_in(own_key, 6), axis_at), (blocks,), jnp.float32, least / len(cuts), high / len(cuts))
        return jnp.repeat(jnp.exp(draws), extent[axis_at] // blocks).reshape((-1,) + (1,) * (len(extent) - axis_at - 1))

    loudness = one(*cuts[0])
    for cut in cuts[1:]:
        loudness = loudness * one(*cut)
    return loudness


def scatter_about(rng, dims, width, bound, pieces=(), held_as=jnp.bfloat16):
    gain = block_levels(rng, dims, pieces, -0.22, 0.18) if pieces else 1.0
    values = jax.random.normal(rng, dims, jnp.float32) * width * gain
    return jnp.minimum(jnp.maximum(values, -bound), bound).astype(held_as)


def setup_inputs(seed: int = 0) -> dict:
    streams_of = jax.random.split(jax.random.key(seed), 19)
    inputs = scatter_about(streams_of[0], (CLIPS, LEN, D), 1.0, 6.0, ((0, 8), (1, 4)))
    lengths = draw_lengths(jax.random.fold_in(streams_of[18], 71), 0)
    cotangent = scatter_about(streams_of[2], (CLIPS, LEN, D), 1.0, 6.0, ((0, 8), (1, 4)))
    attn_gain = jnp.clip(1.0 + 0.1 * jax.random.normal(streams_of[3], (LAYERS, D), jnp.float32), 0.5, 1.5).astype(jnp.bfloat16)
    attn_shift = scatter_about(streams_of[4], (LAYERS, D), 0.2, 1.25, ((1, 4),))
    query_weight = scatter_about(streams_of[5], (LAYERS, D, D), D ** -0.5, 0.15625, ((1, 4),))
    query_bias = scatter_about(streams_of[6], (LAYERS, D), 0.2, 1.25, ((1, 4),))
    key_weight = scatter_about(streams_of[7], (LAYERS, D, D), D ** -0.5, 0.15625, ((1, 4),))
    value_weight = scatter_about(streams_of[8], (LAYERS, D, D), D ** -0.5, 0.15625, ((1, 4),))
    value_bias = scatter_about(streams_of[9], (LAYERS, D), 0.2, 1.25, ((1, 4),))
    out_weight = scatter_about(streams_of[10], (LAYERS, D, D), (max(1, D // 256)) ** -0.5, 2.5, ((1, 4),))
    out_bias = scatter_about(streams_of[11], (LAYERS, D), 0.2, 1.25, ((1, 4),))
    mlp_gain = jnp.clip(1.0 + 0.1 * jax.random.normal(streams_of[12], (LAYERS, D), jnp.float32), 0.5, 1.5).astype(jnp.bfloat16)
    mlp_shift = scatter_about(streams_of[13], (LAYERS, D), 0.2, 1.25, ((1, 4),))
    up_weight = scatter_about(streams_of[14], (LAYERS, D, FF), D ** -0.5, 0.15625, ((1, 4),))
    up_bias = scatter_about(streams_of[15], (LAYERS, FF), 0.2, 1.25, ((1, 4),))
    down_weight = scatter_about(streams_of[16], (LAYERS, FF, D), FF ** -0.5, 0.078125, ((1, 4),))
    down_bias = scatter_about(streams_of[17], (LAYERS, D), 0.2, 1.25, ((1, 4),))
    return dict(inputs=inputs, lengths=lengths, cotangent=cotangent, attn_gain=attn_gain, attn_shift=attn_shift, query_weight=query_weight, query_bias=query_bias, key_weight=key_weight, value_weight=value_weight, value_bias=value_bias, out_weight=out_weight, out_bias=out_bias, mlp_gain=mlp_gain, mlp_shift=mlp_shift, up_weight=up_weight, up_bias=up_bias, down_weight=down_weight, down_bias=down_bias)


EPSILON = 1e-05
NEGATIVE = -1e+30

@jax.custom_vjp
def low(v):
    return lax.optimization_barrier(v.astype(jnp.bfloat16)).astype(jnp.float32)

@jax.custom_vjp
def low_back(v):
    return v

def low_keep(v):
    return (low(v), None)

def low_pass(kept, grad):
    return (grad,)

def back_keep(v):
    return (v, None)

def back_low(kept, grad):
    return (low(grad),)
low.defvjp(low_keep, low_pass)
low_back.defvjp(back_keep, back_low)

def norm_affine(values, norm_gain, norm_shift):
    center = values - lax.optimization_barrier(jnp.mean(values, axis=-1, keepdims=True))
    spread = lax.optimization_barrier(jnp.mean(center * center, axis=-1, keepdims=True))
    return center * lax.rsqrt(spread + EPSILON) * norm_gain + norm_shift

def gelu_exact(values):
    return jax.nn.gelu(values, approximate=False)

def matmul_high(left_operand, right_operand):
    return jnp.dot(left_operand, right_operand, precision=lax.Precision.HIGHEST, preferred_element_type=jnp.float32)

def attend(query_low, key_low, value_low, clip_length):
    block = min(512, LEN)
    query_blocks = query_low.reshape(LEN // block, block, H, HD)
    key_heads = key_low.reshape(LEN, H, HD)
    value_heads = value_low.reshape(LEN, H, HD)
    valid_keys = jnp.arange(LEN, dtype=jnp.int32) < clip_length

    def one_block(query_block):
        scores = low_back(jnp.einsum('qhd,khd->hqk', query_block, key_heads, precision=lax.Precision.HIGHEST))
        scores = jnp.where(valid_keys[None, None, :], scores, NEGATIVE)
        attention = low(jax.nn.softmax(scores, axis=-1))
        return jnp.einsum('hqk,khd->qhd', attention, value_heads, precision=lax.Precision.HIGHEST)
    context = lax.map(jax.checkpoint(one_block), query_blocks)
    return context.reshape(LEN, H * HD)

def layer_forward(hidden_state, layer_params, clip_length):
    attn_gain, attn_shift, query_weight, query_bias, key_weight, value_weight, value_bias, out_weight, out_bias, mlp_gain, mlp_shift, up_weight, up_bias, down_weight, down_bias = layer_params
    query_scale = float(HD) ** (-0.5)
    normed = low(norm_affine(hidden_state, attn_gain, attn_shift))
    query_low = low(low_back((matmul_high(normed, query_weight) + query_bias) * query_scale))
    key_low = low(low_back(matmul_high(normed, key_weight)))
    value_low = low(low_back(matmul_high(normed, value_weight) + value_bias))
    context = low(low_back(attend(query_low, key_low, value_low, clip_length)))
    middle = hidden_state + low_back(matmul_high(context, out_weight) + out_bias)
    hidden_in = low(norm_affine(middle, mlp_gain, mlp_shift))
    pre_gelu = low_back(matmul_high(hidden_in, up_weight) + up_bias)
    active = low(gelu_exact(pre_gelu))
    return middle + low_back(matmul_high(active, down_weight) + down_bias)

def reference(inputs, lengths, cotangent, attn_gain, attn_shift, query_weight, query_bias, key_weight, value_weight, value_bias, out_weight, out_bias, mlp_gain, mlp_shift, up_weight, up_bias, down_weight, down_bias):
    params = tuple((weight_array.astype(jnp.float32) for weight_array in (attn_gain, attn_shift, query_weight, query_bias, key_weight, value_weight, value_bias, out_weight, out_bias, mlp_gain, mlp_shift, up_weight, up_bias, down_weight, down_bias)))

    def one_clip(totals, clip_data):
        clip_inputs, clip_cotangent, clip_length = clip_data
        row_mask = (jnp.arange(LEN, dtype=jnp.int32) < clip_length).astype(jnp.float32)[:, None]

        def forward(clip_values, all_params):
            hidden_state = clip_values
            for layer_index in range(LAYERS):
                layer_params = tuple((weight_array[layer_index] for weight_array in all_params))
                hidden_state = layer_forward(hidden_state, layer_params, clip_length)
            return hidden_state
        result, pull_back = jax.vjp(forward, clip_inputs.astype(jnp.float32), params)
        grad_inputs, grad_params = pull_back(clip_cotangent.astype(jnp.float32) * row_mask)
        totals = tuple((running + addend for running, addend in zip(totals, grad_params)))
        return (totals, (result.astype(jnp.bfloat16), grad_inputs))
    zeros = tuple((jnp.zeros_like(weight_array) for weight_array in params))
    totals, stacked = lax.scan(one_clip, zeros, (inputs, cotangent, lengths))
    outputs, input_grads = stacked
    return (outputs, input_grads, totals[0], totals[1], totals[2], totals[3], totals[4], totals[5], totals[6], totals[7], totals[8], totals[9], totals[10], totals[11], totals[12], totals[13], totals[14])
```

```python
import functools
import math

import jax
import jax.numpy as jnp
from jax import lax
from jax.experimental import pallas as pl
from jax.experimental.pallas import tpu as pltpu
from jax.sharding import PartitionSpec as P

H = 16
EPSILON = 1e-05
NEGATIVE = -1e30
BF16 = jnp.bfloat16
F32 = jnp.float32
BOTH = ("rep", "shard")


def norm_affine(values, norm_gain, norm_shift):
    center = values - jnp.mean(values, axis=-1, keepdims=True)
    spread = jnp.mean(center * center, axis=-1, keepdims=True)
    return center * lax.rsqrt(spread + EPSILON) * norm_gain + norm_shift


def gelu_exact(values):
    return jax.nn.gelu(values, approximate=False)


def project(left_operand, right_operand):
    return jnp.einsum(
        "csa,ab->csb", left_operand, right_operand, preferred_element_type=jnp.float32
    )


def project_back(left_operand, right_operand):
    return jnp.einsum(
        "csb,ab->csa", left_operand, right_operand, preferred_element_type=jnp.float32
    )


def weight_grad(left_operand, right_operand):
    return jnp.einsum(
        "csa,csb->ab", left_operand, right_operand, preferred_element_type=jnp.float32
    )


def column_sum(values):
    return jnp.sum(values.astype(jnp.float32), axis=(0, 1))


def layer_slice(params, layer_index):
    return tuple((weight_array[layer_index] for weight_array in params))


def fetch_forward(local_params):
    return (
        lax.all_gather(local_params[0], "shard", axis=0, tiled=True),
        lax.all_gather(local_params[1], "shard", axis=0, tiled=True),
        lax.all_gather(local_params[2], "shard", axis=0, tiled=True),
        lax.all_gather(local_params[3], "shard", axis=0, tiled=True),
        lax.all_gather(local_params[4], "shard", axis=0, tiled=True),
        lax.all_gather(local_params[5], "shard", axis=0, tiled=True),
        lax.all_gather(local_params[6], "shard", axis=0, tiled=True),
        lax.all_gather(local_params[7], "shard", axis=0, tiled=True),
        lax.all_gather(local_params[8], "shard", axis=0, tiled=True),
        lax.all_gather(local_params[9], "shard", axis=0, tiled=True),
        lax.all_gather(local_params[10], "shard", axis=0, tiled=True),
        lax.all_gather(local_params[11], "shard", axis=0, tiled=True),
        lax.all_gather(local_params[12], "shard", axis=0, tiled=True),
        lax.all_gather(local_params[13], "shard", axis=0, tiled=True),
        lax.all_gather(local_params[14], "shard", axis=0, tiled=True),
    )


def fetch_again(local_params):
    return (
        lax.all_gather(local_params[0], "shard", axis=0, tiled=True),
        lax.all_gather(local_params[1], "shard", axis=0, tiled=True),
        lax.all_gather(local_params[2], "shard", axis=0, tiled=True),
        lax.all_gather(local_params[3], "shard", axis=0, tiled=True),
        lax.all_gather(local_params[4], "shard", axis=0, tiled=True),
        lax.all_gather(local_params[5], "shard", axis=0, tiled=True),
        lax.all_gather(local_params[6], "shard", axis=0, tiled=True),
        lax.all_gather(local_params[7], "shard", axis=0, tiled=True),
        lax.all_gather(local_params[8], "shard", axis=0, tiled=True),
        lax.all_gather(local_params[9], "shard", axis=0, tiled=True),
        lax.all_gather(local_params[10], "shard", axis=0, tiled=True),
        lax.all_gather(local_params[11], "shard", axis=0, tiled=True),
        lax.all_gather(local_params[12], "shard", axis=0, tiled=True),
        lax.all_gather(local_params[13], "shard", axis=0, tiled=True),
        lax.all_gather(local_params[14], "shard", axis=0, tiled=True),
    )


def forward_layer(hidden_state, weights, lengths):
    (
        attn_gain,
        attn_shift,
        query_weight,
        query_bias,
        key_weight,
        value_weight,
        value_bias,
        out_weight,
        out_bias,
        mlp_gain,
        mlp_shift,
        up_weight,
        up_bias,
        down_weight,
        down_bias,
    ) = weights
    clip_count, row_count, model_width = hidden_state.shape
    head_size = model_width // H
    query_scale = float(head_size) ** (-0.5)
    normed = norm_affine(
        hidden_state, attn_gain.astype(jnp.float32), attn_shift.astype(jnp.float32)
    ).astype(jnp.bfloat16)
    query_low = (
        (project(normed, query_weight) + query_bias.astype(jnp.float32)) * query_scale
    ).astype(jnp.bfloat16)
    key_low = project(normed, key_weight).astype(jnp.bfloat16)
    value_low = (project(normed, value_weight) + value_bias.astype(jnp.float32)).astype(
        jnp.bfloat16
    )
    key_all, value_all = (
        lax.all_gather(key_low, "shard", axis=1, tiled=True),
        lax.all_gather(value_low, "shard", axis=1, tiled=True),
    )
    length_all = key_all.shape[1]
    valid_keys = jnp.arange(length_all, dtype=jnp.int32)[None, :] < lengths[:, None]
    query_heads = query_low.reshape(clip_count, row_count, H, head_size)
    key_heads = key_all.reshape(clip_count, length_all, H, head_size)
    value_heads = value_all.reshape(clip_count, length_all, H, head_size)
    scores = jnp.einsum(
        "cqhd,ckhd->chqk", query_heads, key_heads, preferred_element_type=jnp.float32
    )
    scores = jnp.where(valid_keys[:, None, None, :], scores, NEGATIVE)
    attention = jax.nn.softmax(scores, axis=-1)
    attention_low = attention.astype(jnp.bfloat16)
    context = jnp.einsum(
        "chqk,ckhd->cqhd", attention_low, value_heads, preferred_element_type=jnp.float32
    )
    context_low = context.reshape(clip_count, row_count, model_width).astype(jnp.bfloat16)
    middle = hidden_state + project(context_low, out_weight) + out_bias.astype(jnp.float32)
    hidden_in = norm_affine(
        middle, mlp_gain.astype(jnp.float32), mlp_shift.astype(jnp.float32)
    ).astype(jnp.bfloat16)
    pre_gelu = project(hidden_in, up_weight) + up_bias.astype(jnp.float32)
    active_low = gelu_exact(pre_gelu).astype(jnp.bfloat16)
    result = middle + project(active_low, down_weight) + down_bias.astype(jnp.float32)
    kept_values = (
        normed,
        query_heads,
        key_heads,
        value_heads,
        attention,
        attention_low,
        context_low,
        middle,
        hidden_in,
        pre_gelu,
        active_low,
    )
    return (result, kept_values)


def backward_layer(hidden_state, grad_after, weights, lengths):
    (
        attn_gain,
        attn_shift,
        query_weight,
        query_bias,
        key_weight,
        value_weight,
        value_bias,
        out_weight,
        out_bias,
        mlp_gain,
        mlp_shift,
        up_weight,
        up_bias,
        down_weight,
        down_bias,
    ) = weights
    unused, kept_values = forward_layer(hidden_state, weights, lengths)
    (
        normed,
        query_heads,
        key_heads,
        value_heads,
        attention,
        attention_low,
        context_low,
        middle,
        hidden_in,
        pre_gelu,
        active_low,
    ) = kept_values
    clip_count, row_count, model_width = hidden_state.shape
    length_all = key_heads.shape[1]
    head_size = model_width // H
    query_scale = float(head_size) ** (-0.5)
    grad_low = grad_after.astype(jnp.bfloat16)
    grad_active = project_back(grad_low, down_weight)
    unused, gelu_pull = jax.vjp(gelu_exact, pre_gelu)
    grad_pre = gelu_pull(grad_active)[0].astype(jnp.bfloat16)
    grad_hidden = project_back(grad_pre, up_weight)
    unused, mlp_pull = jax.vjp(
        norm_affine, middle, mlp_gain.astype(jnp.float32), mlp_shift.astype(jnp.float32)
    )
    grad_middle_norm, grad_mlp_gain, grad_mlp_shift = mlp_pull(grad_hidden)
    grad_middle = grad_after + grad_middle_norm
    middle_low = grad_middle.astype(jnp.bfloat16)
    grad_context = project_back(middle_low, out_weight).astype(jnp.bfloat16)
    grad_context = grad_context.reshape(clip_count, row_count, H, head_size)
    grad_attention = jnp.einsum(
        "cqhd,ckhd->chqk", grad_context, value_heads, preferred_element_type=jnp.float32
    )
    value_part = jnp.einsum(
        "chqk,cqhd->ckhd", attention_low, grad_context, preferred_element_type=jnp.float32
    )
    grad_scores = attention * (
        grad_attention - jnp.sum(attention * grad_attention, axis=-1, keepdims=True)
    )
    scores_low = grad_scores.astype(jnp.bfloat16)
    grad_query = jnp.einsum(
        "chqk,ckhd->cqhd", scores_low, key_heads, preferred_element_type=jnp.float32
    )
    grad_query = grad_query.reshape(clip_count, row_count, model_width).astype(jnp.bfloat16)
    key_part = jnp.einsum(
        "chqk,cqhd->ckhd", scores_low, query_heads, preferred_element_type=jnp.float32
    )
    key_summed, value_summed = (
        lax.psum_scatter(
            key_part.reshape(clip_count, length_all, model_width).astype(jnp.bfloat16),
            "shard",
            scatter_dimension=1,
            tiled=True,
        ).astype(jnp.float32),
        lax.psum_scatter(
            value_part.reshape(clip_count, length_all, model_width).astype(jnp.bfloat16),
            "shard",
            scatter_dimension=1,
            tiled=True,
        ).astype(jnp.float32),
    )
    key_grad_low = key_summed.astype(jnp.bfloat16)
    value_grad_low = value_summed.astype(jnp.bfloat16)
    grad_normed = (
        project_back(grad_query, query_weight) * query_scale
        + project_back(key_grad_low, key_weight)
        + project_back(value_grad_low, value_weight)
    )
    unused, attn_pull = jax.vjp(
        norm_affine, hidden_state, attn_gain.astype(jnp.float32), attn_shift.astype(jnp.float32)
    )
    grad_input_norm, grad_attn_gain, grad_attn_shift = attn_pull(grad_normed)
    grad_before = grad_middle + grad_input_norm
    grad_down = weight_grad(active_low, grad_low)
    grad_down_bias = column_sum(grad_low)
    grad_up = weight_grad(hidden_in, grad_pre)
    grad_up_bias = column_sum(grad_pre)
    grad_out_weight = weight_grad(context_low, middle_low)
    grad_out_bias = column_sum(middle_low)
    grad_query_weight = weight_grad(normed, grad_query) * query_scale
    grad_query_bias = column_sum(grad_query) * query_scale
    grad_key_weight = weight_grad(normed, key_grad_low)
    grad_value_weight = weight_grad(normed, value_grad_low)
    grad_value_bias = column_sum(value_grad_low)
    owned_grads = (
        lax.psum_scatter(
            grad_attn_gain.astype(jnp.bfloat16), "shard", scatter_dimension=0, tiled=True
        ).astype(jnp.float32),
        lax.psum_scatter(
            grad_attn_shift.astype(jnp.bfloat16), "shard", scatter_dimension=0, tiled=True
        ).astype(jnp.float32),
        lax.psum_scatter(
            grad_query_weight.astype(jnp.bfloat16), "shard", scatter_dimension=0, tiled=True
        ).astype(jnp.float32),
        lax.psum_scatter(
            grad_query_bias.astype(jnp.bfloat16), "shard", scatter_dimension=0, tiled=True
        ).astype(jnp.float32),
        lax.psum_scatter(
            grad_key_weight.astype(jnp.bfloat16), "shard", scatter_dimension=0, tiled=True
        ).astype(jnp.float32),
        lax.psum_scatter(
            grad_value_weight.astype(jnp.bfloat16), "shard", scatter_dimension=0, tiled=True
        ).astype(jnp.float32),
        lax.psum_scatter(
            grad_value_bias.astype(jnp.bfloat16), "shard", scatter_dimension=0, tiled=True
        ).astype(jnp.float32),
        lax.psum_scatter(
            grad_out_weight.astype(jnp.bfloat16), "shard", scatter_dimension=0, tiled=True
        ).astype(jnp.float32),
        lax.psum_scatter(
            grad_out_bias.astype(jnp.bfloat16), "shard", scatter_dimension=0, tiled=True
        ).astype(jnp.float32),
        lax.psum_scatter(
            grad_mlp_gain.astype(jnp.bfloat16), "shard", scatter_dimension=0, tiled=True
        ).astype(jnp.float32),
        lax.psum_scatter(
            grad_mlp_shift.astype(jnp.bfloat16), "shard", scatter_dimension=0, tiled=True
        ).astype(jnp.float32),
        lax.psum_scatter(
            grad_up.astype(jnp.bfloat16), "shard", scatter_dimension=0, tiled=True
        ).astype(jnp.float32),
        lax.psum_scatter(
            grad_up_bias.astype(jnp.bfloat16), "shard", scatter_dimension=0, tiled=True
        ).astype(jnp.float32),
        lax.psum_scatter(
            grad_down.astype(jnp.bfloat16), "shard", scatter_dimension=0, tiled=True
        ).astype(jnp.float32),
        lax.psum_scatter(
            grad_down_bias.astype(jnp.bfloat16), "shard", scatter_dimension=0, tiled=True
        ).astype(jnp.float32),
    )
    return (grad_before, owned_grads)


def replica_layer(owned_grads):
    return (
        lax.psum(owned_grads[0].astype(jnp.bfloat16), "rep").astype(jnp.float32),
        lax.psum(owned_grads[1].astype(jnp.bfloat16), "rep").astype(jnp.float32),
        lax.psum(owned_grads[2].astype(jnp.bfloat16), "rep").astype(jnp.float32),
        lax.psum(owned_grads[3].astype(jnp.bfloat16), "rep").astype(jnp.float32),
        lax.psum(owned_grads[4].astype(jnp.bfloat16), "rep").astype(jnp.float32),
        lax.psum(owned_grads[5].astype(jnp.bfloat16), "rep").astype(jnp.float32),
        lax.psum(owned_grads[6].astype(jnp.bfloat16), "rep").astype(jnp.float32),
        lax.psum(owned_grads[7].astype(jnp.bfloat16), "rep").astype(jnp.float32),
        lax.psum(owned_grads[8].astype(jnp.bfloat16), "rep").astype(jnp.float32),
        lax.psum(owned_grads[9].astype(jnp.bfloat16), "rep").astype(jnp.float32),
        lax.psum(owned_grads[10].astype(jnp.bfloat16), "rep").astype(jnp.float32),
        lax.psum(owned_grads[11].astype(jnp.bfloat16), "rep").astype(jnp.float32),
        lax.psum(owned_grads[12].astype(jnp.bfloat16), "rep").astype(jnp.float32),
        lax.psum(owned_grads[13].astype(jnp.bfloat16), "rep").astype(jnp.float32),
        lax.psum(owned_grads[14].astype(jnp.bfloat16), "rep").astype(jnp.float32),
    )


def general_shards(
    inputs,
    lengths,
    cotangent,
    attn_gain,
    attn_shift,
    query_weight,
    query_bias,
    key_weight,
    value_weight,
    value_bias,
    out_weight,
    out_bias,
    mlp_gain,
    mlp_shift,
    up_weight,
    up_bias,
    down_weight,
    down_bias,
):
    params = (
        attn_gain,
        attn_shift,
        query_weight,
        query_bias,
        key_weight,
        value_weight,
        value_bias,
        out_weight,
        out_bias,
        mlp_gain,
        mlp_shift,
        up_weight,
        up_bias,
        down_weight,
        down_bias,
    )
    layers = attn_gain.shape[0]
    hidden_state = inputs.astype(jnp.float32)
    kept_inputs = []
    kept_weights = []
    for layer_index in range(layers):
        gathered = fetch_forward(layer_slice(params, layer_index))
        kept_inputs.append(hidden_state)
        kept_weights.append(gathered)
        hidden_state, unused = forward_layer(hidden_state, gathered, lengths)
    output = hidden_state.astype(jnp.bfloat16)
    row_count = inputs.shape[1]
    first_row = lax.axis_index("shard") * row_count
    positions = first_row + jnp.arange(row_count, dtype=jnp.int32)
    row_mask = (positions[None, :] < lengths[:, None]).astype(jnp.float32)
    grad_state = cotangent.astype(jnp.float32) * row_mask[:, :, None]
    owned_list = [None] * layers
    for layer_index in reversed(range(layers)):
        gathered = fetch_again(layer_slice(params, layer_index))
        grad_state, owned_grads = backward_layer(
            kept_inputs[layer_index], grad_state, gathered, lengths
        )
        owned_grads = replica_layer(owned_grads)
        owned_list[layer_index] = owned_grads
    stacked = tuple(
        (
            jnp.stack([owned_list[layer_index][member] for layer_index in range(layers)])
            for member in range(15)
        )
    )
    return (
        output,
        grad_state,
        stacked[0],
        stacked[1],
        stacked[2],
        stacked[3],
        stacked[4],
        stacked[5],
        stacked[6],
        stacked[7],
        stacked[8],
        stacked[9],
        stacked[10],
        stacked[11],
        stacked[12],
        stacked[13],
        stacked[14],
    )


def device_index(a, b, core, z):
    return ((a * 2 + b) * 2 + core) * 4 + z


def make_pairs(target):
    return [
        (device_index(a, b, core, z), device_index(*target(a, b, core, z)))
        for a in range(2)
        for b in range(2)
        for core in range(2)
        for z in range(4)
    ]


PAIRS = {
    "a": make_pairs(lambda a, b, c, z: (1 - a, b, c, z)),
    "b": make_pairs(lambda a, b, c, z: (a, 1 - b, c, z)),
    "ab": make_pairs(lambda a, b, c, z: (1 - a, 1 - b, c, z)),
    "core": make_pairs(lambda a, b, c, z: (a, b, 1 - c, z)),
    "z1": make_pairs(lambda a, b, c, z: (a, b, c, (z + 1) % 4)),
    "z2": make_pairs(lambda a, b, c, z: (a, b, c, (z + 2) % 4)),
    "z3": make_pairs(lambda a, b, c, z: (a, b, c, (z + 3) % 4)),
}
for step in range(2):
    PAIRS["in%d" % step] = make_pairs(
        lambda a, b, c, z, step=step: (a, b, z // 2, 2 * c + (z + step) % 2)
    )
    PAIRS["out%d" % step] = [(target, source) for source, target in PAIRS["in%d" % step]]


def send(values, way):
    return lax.ppermute(values, BOTH, PAIRS[way])


def pick(values, index, axis=0):
    return lax.dynamic_index_in_dim(values, index, axis, keepdims=False)


def place():
    rep = lax.axis_index("rep")
    return rep // 4, (rep // 2) % 2, rep % 2, lax.axis_index("shard")


def after(values, *others):
    return lax.optimization_barrier((values,) + others)[0]


def own_piece(kind, shards):
    a, b, core, z = place()
    chip = a * 2 + b
    if kind == "attn":
        stacked = jnp.stack(shards)
        return lax.dynamic_slice(stacked, (0, chip * 80, core * 640), (4, 80, 640))
    if kind == "up":
        part = lax.dynamic_slice(shards[0], (chip * 80, core * 2560), (80, 2560))
        return jnp.stack([part[:, :1280], part[:, 1280:]])
    part = lax.dynamic_slice(shards[0], (chip * 320, core * 640), (320, 640))
    return part.reshape(2, 160, 640)


def assemble_kernel(kind, count, *refs):
    shards, refs = refs[:count], refs[count:]
    sources, refs = refs[:10], refs[10:]
    outs, sem = refs[:-1], refs[-1]
    rep = lax.axis_index("rep")
    a, b, core, z = rep // 4, (rep // 2) % 2, rep % 2, lax.axis_index("shard")
    copies = []
    rows = shards[0].shape[0]
    for shard, out in zip(shards, outs):
        at = pl.ds(pl.multiple_of(z * rows, rows), rows)
        copies.append(pltpu.make_async_copy(shard, out.at[at, :], sem))
    for number, source in enumerate(sources):
        place_core = core if number < 5 else 1 - core
        which = number % 5
        chip_a = a if which in (0, 1) else 1 - a
        chip_b = b if which in (0, 2) else 1 - b
        chip = chip_a * 2 + chip_b
        first = 0
        if which == 4:
            first = 2 if kind == "attn" else 1
        for s in range(3):
            from_z = lax.rem(z + 3 - s, 4)
            for part in range(source.shape[1]):
                unit = first + part
                if kind == "attn":
                    out = outs[unit]
                    row, height = from_z * 320 + chip * 80, 80
                    column, width = place_core * 640, 640
                elif kind == "up":
                    out = outs[0]
                    row, height = from_z * 320 + chip * 80, 80
                    column, width = place_core * 2560 + unit * 1280, 1280
                else:
                    out = outs[0]
                    row, height = from_z * 1280 + chip * 320 + unit * 160, 160
                    column, width = place_core * 640, 640
                at = (
                    pl.ds(pl.multiple_of(row, 16), height),
                    pl.ds(pl.multiple_of(column, 128), width),
                )
                copies.append(pltpu.make_async_copy(source.at[s, part], out.at[at], sem))
    for copy in copies:
        copy.start()
    for copy in copies:
        copy.wait()


def assemble(kind, shards, sources):
    shape = {"attn": (1280, 1280), "up": (1280, 5120), "down": (5120, 1280)}[kind]
    count = len(shards)
    size = 2 * count * shape[0] * shape[1]
    return pl.pallas_call(
        functools.partial(assemble_kernel, kind, count),
        out_shape=tuple(jax.ShapeDtypeStruct(shape, BF16) for _ in shards),
        in_specs=[pl.BlockSpec(memory_space=pl.ANY)] * (count + 10),
        out_specs=tuple(pl.BlockSpec(memory_space=pl.ANY) for _ in shards),
        scratch_shapes=[pltpu.SemaphoreType.DMA],
        cost_estimate=pl.CostEstimate(flops=0, bytes_accessed=2 * size, transcendentals=0),
        name="assemble_" + kind,
    )(*shards, *sources)


def fetch(kind, shards, gate):
    piece = own_piece(kind, shards)
    if gate is not None:
        piece = after(piece, gate)
    far = jnp.stack([send(piece, "z1"), send(piece, "z2"), send(piece, "z3")])
    half = far.shape[1] // 2
    from_b, from_a = send(far, "b"), send(far, "a")
    first, second = send(from_b[:, :half], "a"), send(from_a[:, half:], "b")
    mine = (far, from_b, from_a, first, second)
    other = tuple(send(part, "core") for part in mine)
    return assemble(kind, shards, mine + other), far


def attend_kernel(q, k0, k1, v0, v1, m0, m1, out, lse):
    contract = (((0,), (0,)), ((), ()))
    query = q[...]
    s0 = lax.dot_general(k0[...], query, contract, preferred_element_type=F32) + m0[...]
    s1 = lax.dot_general(k1[...], query, contract, preferred_element_type=F32) + m1[...]
    top = jnp.maximum(jnp.max(s0, axis=0, keepdims=True), jnp.max(s1, axis=0, keepdims=True))
    e0, e1 = jnp.exp(s0 - top), jnp.exp(s1 - top)
    total = jnp.sum(e0, axis=0, keepdims=True) + jnp.sum(e1, axis=0, keepdims=True)
    context = jnp.dot(v0[...], e0.astype(BF16), preferred_element_type=F32)
    context += jnp.dot(v1[...], e1.astype(BF16), preferred_element_type=F32)
    out[...] = (context / total).astype(BF16)
    lse[0] = top + jnp.log(total)


def head_spec(rows, columns):
    return pl.BlockSpec((rows, columns), lambda h: (h, 0))


def whole_spec(rows, columns):
    return pl.BlockSpec((rows, columns), lambda h: (0, 0))


def attend(query, key, value, far_key, far_value, mask, far_mask):
    width, count = query.shape
    size = width // H
    heads = head_spec(size, count)
    masks = whole_spec(count, 1)
    return pl.pallas_call(
        attend_kernel,
        grid=(H,),
        out_shape=(
            jax.ShapeDtypeStruct((width, count), BF16),
            jax.ShapeDtypeStruct((H, 1, count), F32),
        ),
        in_specs=[heads] * 5 + [masks] * 2,
        out_specs=(heads, pl.BlockSpec((1, 1, count), lambda h: (h, 0, 0))),
        compiler_params=pltpu.CompilerParams(vmem_limit_bytes=48 << 20),
        cost_estimate=pl.CostEstimate(
            flops=8 * width * count * count * 3,
            bytes_accessed=12 * width * count,
            transcendentals=2 * H * count * count,
        ),
        name="attend",
    )(query, key, far_key, value, far_value, mask, far_mask)


def attend_back_kernel(q, k0, k1, v0, v1, m0, m1, lse, g, gq, gk0, gk1, gv0, gv1):
    outer = (((0,), (0,)), ((), ()))
    inner = (((1,), (1,)), ((), ()))
    query, grad, norm = q[...], g[...], lse[0]
    halves = []
    delta = None
    for k, v, m, gv in ((k0, v0, m0, gv0), (k1, v1, m1, gv1)):
        s = lax.dot_general(k[...], query, outer, preferred_element_type=F32) + m[...]
        p = jnp.exp(s - norm)
        dp = lax.dot_general(v[...], grad, outer, preferred_element_type=F32)
        part = jnp.sum(p * dp, axis=0, keepdims=True)
        delta = part if delta is None else delta + part
        gv[...] = lax.dot_general(
            grad, p.astype(BF16), inner, preferred_element_type=F32
        ).astype(BF16)
        halves.append((p, dp))
    total = None
    for (p, dp), k, gk in zip(halves, (k0, k1), (gk0, gk1)):
        ds = (p * (dp - delta)).astype(BF16)
        part = jnp.dot(k[...], ds, preferred_element_type=F32)
        total = part if total is None else total + part
        gk[...] = lax.dot_general(query, ds, inner, preferred_element_type=F32).astype(BF16)
    gq[...] = total.astype(BF16)


def attend_back(query, key, value, far_key, far_value, mask, far_mask, lse, grad):
    width, count = query.shape
    size = width // H
    heads = head_spec(size, count)
    masks = whole_spec(count, 1)
    stats = pl.BlockSpec((1, 1, count), lambda h: (h, 0, 0))
    return pl.pallas_call(
        attend_back_kernel,
        grid=(H,),
        out_shape=tuple(jax.ShapeDtypeStruct((width, count), BF16) for _ in range(5)),
        in_specs=[heads] * 5 + [masks] * 2 + [stats, heads],
        out_specs=tuple(heads for _ in range(5)),
        compiler_params=pltpu.CompilerParams(vmem_limit_bytes=48 << 20),
        cost_estimate=pl.CostEstimate(
            flops=20 * width * count * count * 3,
            bytes_accessed=22 * width * count,
            transcendentals=2 * H * count * count,
        ),
        name="attend_back",
    )(query, key, far_key, value, far_value, mask, far_mask, lse, grad)


def add(*parts):
    total = parts[0].astype(F32)
    for part in parts[1:]:
        total = total + part.astype(F32)
    return total.astype(BF16)


def reduce_blocks(blocks, cut):
    a, b, core, z = place()
    first, second = blocks[..., :cut], blocks[..., cut:]
    got = send(pick(first, 1 - b, 2), "b")
    first = add(pick(first, b, 2), got)
    got = send(pick(second, 1 - a, 1), "a")
    second = add(pick(second, a, 1), got)
    got = send(pick(first, 1 - a, 1), "a")
    first = add(pick(first, a, 1), got)
    got = send(pick(second, 1 - b, 1), "b")
    second = add(pick(second, b, 1), got)
    both = jnp.concatenate([first, second], axis=-1)
    got = [send(pick(both, (z + s) % 4), "z%d" % s) for s in (1, 2, 3)]
    return add(pick(both, z), *got)


def spread(piece):
    a, b, core, z = place()
    parts = jnp.stack([piece, send(piece, "b"), send(piece, "a"), send(piece, "ab")])
    other = send(parts, "core")
    me = core * 4 + a * 2 + b
    every = jnp.concatenate([parts, other])
    ordered = jnp.stack([pick(every, jnp.bitwise_xor(me, i)) for i in range(8)])
    return ordered.reshape(2, 4, *piece.shape)


def product(left, right, spec):
    return jnp.einsum(spec, left, right, preferred_element_type=F32)


def half_columns(values, core):
    size = values.shape[1] // 2
    return lax.dynamic_slice_in_dim(values, core * size, size, 1)


def half_rows(values, core):
    size = values.shape[0] // 2
    return lax.dynamic_slice_in_dim(values, core * size, size, 0)


def normalize(values):
    center = values - jnp.mean(values, axis=-1, keepdims=True)
    scale = lax.rsqrt(jnp.mean(center * center, axis=-1, keepdims=True) + EPSILON)
    return center * scale, scale


def norm_back(grad, gain, unit, scale):
    e = grad * gain
    return scale * (
        e
        - jnp.mean(e, axis=-1, keepdims=True)
        - unit * jnp.mean(e * unit, axis=-1, keepdims=True)
    )


ROOT_HALF = math.sqrt(0.5)
ROOT_TWO_PI = math.sqrt(2.0 * math.pi)


def forward_fast(state, weights, vectors, masks):
    query_weight, key_weight, value_weight, out_weight, up_weight, down_weight = weights
    (attn_gain, attn_shift, query_bias, value_bias, out_bias, mlp_gain, mlp_shift, down_bias,
     up_bias) = vectors
    scale = float(state.shape[1] // H) ** (-0.5)
    unit, _ = normalize(state)
    normed = (unit * attn_gain + attn_shift).astype(BF16)
    key = product(key_weight, normed, "df,sd->fs").astype(BF16)
    value = (product(value_weight, normed, "df,sd->fs") + value_bias[:, None]).astype(BF16)
    far_key, far_value = send(key, "core"), send(value, "core")
    query = ((product(query_weight, normed, "df,sd->fs") + query_bias[:, None]) * scale).astype(BF16)
    context, lse = attend(query, key, value, far_key, far_value, *masks)
    middle = state + product(context, out_weight, "fs,fd->sd") + out_bias
    unit, _ = normalize(middle)
    hidden_in = (unit * mlp_gain + mlp_shift).astype(BF16)
    pre_gelu = product(hidden_in, up_weight, "sd,df->sf") + up_bias
    active = (pre_gelu * (0.5 * (1.0 + lax.erf(pre_gelu * ROOT_HALF)))).astype(BF16)
    result = middle + product(active, down_weight, "sf,fd->sd") + down_bias
    kept = (normed, query, key, value, far_key, far_value, lse, context, middle, hidden_in, pre_gelu,
            active)
    return result, kept


def two(own, core, cut):
    return jnp.concatenate([cut(own, core), send(cut(own, 1 - core), "core")], axis=0)


def backward_fast(state, grad_after, weights, vectors, masks, kept):
    query_weight, key_weight, value_weight, out_weight, up_weight, down_weight = weights
    (attn_gain, attn_shift, query_bias, value_bias, out_bias, mlp_gain, mlp_shift, down_bias,
     up_bias) = vectors
    (normed, query, key, value, far_key, far_value, lse, context, middle, hidden_in, pre_gelu,
     active) = kept
    a, b, core, z = place()
    scale = float(state.shape[1] // H) ** (-0.5)
    count = state.shape[0]

    def whole(values):
        return jnp.concatenate([values, send(values, "core")], axis=0)

    def active_part(values, which):
        return pick(values.reshape(count, 4, 2, 640), which, 2).reshape(count, 2560)

    grad_f = grad_after.astype(BF16)
    active_both = two(active, core, active_part)
    grad_f_both = whole(grad_f)
    grad_down = product(active_both, grad_f_both, "sa,sb->ab").astype(BF16)
    grad_down = spread(reduce_blocks(grad_down.reshape(4, 2, 2, 160, 1280), 640))
    grad_down = grad_down.reshape(1280, 1280)

    grad_active = product(grad_f, down_weight, "sd,fd->sf")
    slope = 0.5 * (1.0 + lax.erf(pre_gelu * ROOT_HALF)) + pre_gelu * jnp.exp(
        -0.5 * pre_gelu * pre_gelu
    ) * (1.0 / ROOT_TWO_PI)
    grad_pre = (grad_active * slope).astype(BF16)
    grad_pre_both = two(grad_pre, core, half_columns)
    hidden_both = whole(hidden_in)
    grad_up = product(hidden_both, grad_pre_both, "sa,sb->ab").astype(BF16)
    grad_up = spread(reduce_blocks(grad_up.reshape(4, 2, 2, 80, 2560), 1280))
    grad_up = grad_up.transpose(1, 2, 0, 3).reshape(320, 5120)

    grad_hidden = product(grad_pre, up_weight, "sf,df->sd")
    unit, spread_scale = normalize(middle)
    grad_middle = grad_after + norm_back(grad_hidden, mlp_gain, unit, spread_scale)
    grad_o = grad_middle.astype(BF16)
    mlp_gain_grad, mlp_shift_grad = jnp.sum(grad_hidden * unit, 0), jnp.sum(grad_hidden, 0)

    context_both = jnp.concatenate([context, send(context, "core")], axis=1)
    grad_o_both = two(grad_o, core, half_columns)
    grad_out = product(context_both, grad_o_both, "as,sb->ab").astype(BF16)
    grad_out = spread(reduce_blocks(grad_out.reshape(4, 2, 2, 80, 640), 384))
    grad_out = grad_out.transpose(1, 2, 0, 3).reshape(320, 1280)

    grad_context = product(out_weight, grad_o, "fd,sd->fs").astype(BF16)
    grad_query, grad_key, far_grad_key, grad_value, far_grad_value = attend_back(
        query, key, value, far_key, far_value, *masks, lse, grad_context
    )
    grad_key = add(grad_key, send(far_grad_key, "core"))
    grad_value = add(grad_value, send(far_grad_value, "core"))
    normed_both = whole(normed)
    parts = jnp.concatenate(
        [
            jnp.concatenate([half_rows(g, core), send(half_rows(g, 1 - core), "core")], axis=1)
            for g in (grad_query, grad_key, grad_value)
        ],
        axis=0,
    )
    grad_qkv = product(normed_both, parts, "sa,bs->ab")
    columns = jnp.arange(1920) < 640
    grad_qkv = (grad_qkv * jnp.where(columns, scale, 1.0)).astype(BF16)
    grad_qkv = spread(reduce_blocks(grad_qkv.reshape(4, 2, 2, 80, 1920), 1024))
    grad_qkv = grad_qkv.reshape(2, 4, 80, 3, 640).transpose(3, 1, 2, 0, 4).reshape(3, 320, 1280)

    grad_normed = (
        product(grad_query, query_weight, "fs,df->sd") * scale
        + product(grad_key, key_weight, "fs,df->sd")
        + product(grad_value, value_weight, "fs,df->sd")
    )
    unit, spread_scale = normalize(state)
    attn_gain_grad, attn_shift_grad = jnp.sum(grad_normed * unit, 0), jnp.sum(grad_normed, 0)
    grad_before = grad_middle + norm_back(grad_normed, attn_gain, unit, spread_scale)

    def rows(values):
        return jnp.sum(values.astype(F32), axis=0)

    small = jnp.concatenate(
        [
            attn_gain_grad,
            attn_shift_grad,
            jnp.sum(grad_query.astype(F32), axis=1) * scale,
            jnp.sum(grad_value.astype(F32), axis=1),
            rows(grad_o),
            mlp_gain_grad,
            mlp_shift_grad,
            rows(grad_f),
            rows(grad_pre),
        ]
    )
    return grad_before, (grad_qkv, grad_out, grad_up, grad_down), small


def plane_shards(
    inputs, lengths, cotangent, attn_gain, attn_shift, query_weight, query_bias, key_weight,
    value_weight, value_bias, out_weight, out_bias, mlp_gain, mlp_shift, up_weight, up_bias,
    down_weight, down_bias,
):
    a, b, core, z = place()
    layers = attn_gain.shape[0]
    block = inputs.shape[1]

    def gather_tokens(values):
        return jnp.concatenate(
            [send(pick(values, (z + step) % 2), "in%d" % step) for step in range(2)], axis=0
        )

    def return_tokens(values):
        got = [send(values[step * block : (step + 1) * block], "out%d" % step) for step in range(2)]
        got = jnp.stack(got)
        return jnp.stack([pick(got, (z + clip) % 2) for clip in range(2)])

    packed = jnp.concatenate(
        [attn_gain, attn_shift, query_bias, value_bias, out_bias, mlp_gain, mlp_shift, down_bias,
         up_bias], axis=1,
    )
    pieces = jnp.stack([packed] + [send(packed, "z%d" % s) for s in (1, 2, 3)])
    pieces = jnp.stack([pick(pieces, (z + 4 - from_z) % 4) for from_z in range(4)]).astype(F32)
    vectors = []
    for layer in range(layers):
        row = [pieces[:, layer, i * 320 : (i + 1) * 320].reshape(1280) for i in range(8)]
        row.append(pieces[:, layer, 2560:].reshape(5120))
        vectors.append(tuple(row))

    state = gather_tokens(inputs).astype(F32)

    far_lengths = send(lengths, "core")
    four = jnp.where(core == 0, jnp.concatenate([lengths, far_lengths]),
                     jnp.concatenate([far_lengths, lengths]))
    length = pick(four, z)

    def positions(which):
        return jnp.concatenate(
            [(2 * which + (z + step) % 2) * block + jnp.arange(block) for step in range(2)]
        )

    def mask_of(which):
        return jnp.where(positions(which) < length, 0.0, NEGATIVE).astype(F32)[:, None]

    masks = (mask_of(core), mask_of(1 - core))

    weights = []
    gate = None
    for layer in range(layers):
        attn, gate = fetch(
            "attn", (query_weight[layer], key_weight[layer], value_weight[layer], out_weight[layer]), gate
        )
        up, gate = fetch("up", (up_weight[layer],), gate)
        down, gate = fetch("down", (down_weight[layer],), gate)
        weights.append(attn + up + down)

    states, kept = [], []
    for layer in range(layers):
        states.append(state)
        state, values = forward_fast(state, weights[layer], vectors[layer], masks)
        kept.append(values)
    output = return_tokens(state.astype(BF16))

    row_mask = (positions(core) < length).astype(F32)
    grad = gather_tokens(cotangent).astype(F32) * row_mask[:, None]
    small, large = [None] * layers, [None] * layers
    for layer in reversed(range(layers)):
        grad, large[layer], small[layer] = backward_fast(
            states[layer], grad, weights[layer], vectors[layer], masks, kept[layer]
        )
    input_grad = return_tokens(grad.astype(BF16)).astype(F32)

    total = lax.psum(jnp.stack(small), BOTH)
    vec = pick(total[:, :10240].reshape(layers, 8, 4, 320), z, 2)
    up_bias_grad = pick(total[:, 10240:].reshape(layers, 4, 1280), z, 1)

    def stack(parts):
        return jnp.stack([part.astype(F32) for part in parts])

    query_grad = stack([g[0][0] for g in large])
    key_grad = stack([g[0][1] for g in large])
    value_grad = stack([g[0][2] for g in large])
    out_grad = stack([g[1] for g in large])
    up_grad = stack([g[2] for g in large])
    down_grad = stack([g[3] for g in large])
    return (
        output, input_grad, vec[:, 0], vec[:, 1], query_grad, vec[:, 2], key_grad, value_grad,
        vec[:, 3], out_grad, vec[:, 4], vec[:, 5], vec[:, 6], up_grad, up_bias_grad, down_grad,
        vec[:, 7],
    )


def pick_body(mesh):
    if mesh.shape["rep"] == 8 and mesh.shape["shard"] == 4:
        return plane_shards
    return general_shards


def solution(mesh):
    body = pick_body(mesh)
    placed = (
        P("rep", "shard", None),
        P("rep"),
        P("rep", "shard", None),
        P(None, "shard"),
        P(None, "shard"),
        P(None, "shard", None),
        P(None, "shard"),
        P(None, "shard", None),
        P(None, "shard", None),
        P(None, "shard"),
        P(None, "shard", None),
        P(None, "shard"),
        P(None, "shard"),
        P(None, "shard"),
        P(None, "shard", None),
        P(None, "shard"),
        P(None, "shard", None),
        P(None, "shard"),
    )
    return jax.shard_map(
        body,
        mesh=mesh,
        in_specs=placed,
        out_specs=(
            P("rep", "shard", None),
            P("rep", "shard", None),
            P(None, "shard"),
            P(None, "shard"),
            P(None, "shard", None),
            P(None, "shard"),
            P(None, "shard", None),
            P(None, "shard", None),
            P(None, "shard"),
            P(None, "shard", None),
            P(None, "shard"),
            P(None, "shard"),
            P(None, "shard"),
            P(None, "shard", None),
            P(None, "shard"),
            P(None, "shard", None),
            P(None, "shard"),
        ),
        check_vma=False,
    )
```

```python
import functools
import math

import jax
import jax.numpy as jnp
from jax import lax
from jax.experimental import pallas as pl
from jax.experimental.pallas import tpu as pltpu
from jax.sharding import PartitionSpec as P

H = 16
EPSILON = 1e-05
NEGATIVE = -1e30
BF16 = jnp.bfloat16
F32 = jnp.float32
BOTH = ("rep", "shard")


def norm_affine(values, norm_gain, norm_shift):
    center = values - jnp.mean(values, axis=-1, keepdims=True)
    spread = jnp.mean(center * center, axis=-1, keepdims=True)
    return center * lax.rsqrt(spread + EPSILON) * norm_gain + norm_shift


def gelu_exact(values):
    return jax.nn.gelu(values, approximate=False)


def project(left_operand, right_operand):
    return jnp.einsum(
        "csa,ab->csb", left_operand, right_operand, preferred_element_type=jnp.float32
    )


def project_back(left_operand, right_operand):
    return jnp.einsum(
        "csb,ab->csa", left_operand, right_operand, preferred_element_type=jnp.float32
    )


def weight_grad(left_operand, right_operand):
    return jnp.einsum(
        "csa,csb->ab", left_operand, right_operand, preferred_element_type=jnp.float32
    )


def column_sum(values):
    return jnp.sum(values.astype(jnp.float32), axis=(0, 1))


def layer_slice(params, layer_index):
    return tuple((weight_array[layer_index] for weight_array in params))


def fetch_forward(local_params):
    return (
        lax.all_gather(local_params[0], "shard", axis=0, tiled=True),
        lax.all_gather(local_params[1], "shard", axis=0, tiled=True),
        lax.all_gather(local_params[2], "shard", axis=0, tiled=True),
        lax.all_gather(local_params[3], "shard", axis=0, tiled=True),
        lax.all_gather(local_params[4], "shard", axis=0, tiled=True),
        lax.all_gather(local_params[5], "shard", axis=0, tiled=True),
        lax.all_gather(local_params[6], "shard", axis=0, tiled=True),
        lax.all_gather(local_params[7], "shard", axis=0, tiled=True),
        lax.all_gather(local_params[8], "shard", axis=0, tiled=True),
        lax.all_gather(local_params[9], "shard", axis=0, tiled=True),
        lax.all_gather(local_params[10], "shard", axis=0, tiled=True),
        lax.all_gather(local_params[11], "shard", axis=0, tiled=True),
        lax.all_gather(local_params[12], "shard", axis=0, tiled=True),
        lax.all_gather(local_params[13], "shard", axis=0, tiled=True),
        lax.all_gather(local_params[14], "shard", axis=0, tiled=True),
    )


def fetch_again(local_params):
    return (
        lax.all_gather(local_params[0], "shard", axis=0, tiled=True),
        lax.all_gather(local_params[1], "shard", axis=0, tiled=True),
        lax.all_gather(local_params[2], "shard", axis=0, tiled=True),
        lax.all_gather(local_params[3], "shard", axis=0, tiled=True),
        lax.all_gather(local_params[4], "shard", axis=0, tiled=True),
        lax.all_gather(local_params[5], "shard", axis=0, tiled=True),
        lax.all_gather(local_params[6], "shard", axis=0, tiled=True),
        lax.all_gather(local_params[7], "shard", axis=0, tiled=True),
        lax.all_gather(local_params[8], "shard", axis=0, tiled=True),
        lax.all_gather(local_params[9], "shard", axis=0, tiled=True),
        lax.all_gather(local_params[10], "shard", axis=0, tiled=True),
        lax.all_gather(local_params[11], "shard", axis=0, tiled=True),
        lax.all_gather(local_params[12], "shard", axis=0, tiled=True),
        lax.all_gather(local_params[13], "shard", axis=0, tiled=True),
        lax.all_gather(local_params[14], "shard", axis=0, tiled=True),
    )


def forward_layer(hidden_state, weights, lengths):
    (
        attn_gain,
        attn_shift,
        query_weight,
        query_bias,
        key_weight,
        value_weight,
        value_bias,
        out_weight,
        out_bias,
        mlp_gain,
        mlp_shift,
        up_weight,
        up_bias,
        down_weight,
        down_bias,
    ) = weights
    clip_count, row_count, model_width = hidden_state.shape
    head_size = model_width // H
    query_scale = float(head_size) ** (-0.5)
    normed = norm_affine(
        hidden_state, attn_gain.astype(jnp.float32), attn_shift.astype(jnp.float32)
    ).astype(jnp.bfloat16)
    query_low = (
        (project(normed, query_weight) + query_bias.astype(jnp.float32)) * query_scale
    ).astype(jnp.bfloat16)
    key_low = project(normed, key_weight).astype(jnp.bfloat16)
    value_low = (project(normed, value_weight) + value_bias.astype(jnp.float32)).astype(
        jnp.bfloat16
    )
    key_all, value_all = (
        lax.all_gather(key_low, "shard", axis=1, tiled=True),
        lax.all_gather(value_low, "shard", axis=1, tiled=True),
    )
    length_all = key_all.shape[1]
    valid_keys = jnp.arange(length_all, dtype=jnp.int32)[None, :] < lengths[:, None]
    query_heads = query_low.reshape(clip_count, row_count, H, head_size)
    key_heads = key_all.reshape(clip_count, length_all, H, head_size)
    value_heads = value_all.reshape(clip_count, length_all, H, head_size)
    scores = jnp.einsum(
        "cqhd,ckhd->chqk", query_heads, key_heads, preferred_element_type=jnp.float32
    )
    scores = jnp.where(valid_keys[:, None, None, :], scores, NEGATIVE)
    attention = jax.nn.softmax(scores, axis=-1)
    attention_low = attention.astype(jnp.bfloat16)
    context = jnp.einsum(
        "chqk,ckhd->cqhd", attention_low, value_heads, preferred_element_type=jnp.float32
    )
    context_low = context.reshape(clip_count, row_count, model_width).astype(jnp.bfloat16)
    middle = hidden_state + project(context_low, out_weight) + out_bias.astype(jnp.float32)
    hidden_in = norm_affine(
        middle, mlp_gain.astype(jnp.float32), mlp_shift.astype(jnp.float32)
    ).astype(jnp.bfloat16)
    pre_gelu = project(hidden_in, up_weight) + up_bias.astype(jnp.float32)
    active_low = gelu_exact(pre_gelu).astype(jnp.bfloat16)
    result = middle + project(active_low, down_weight) + down_bias.astype(jnp.float32)
    kept_values = (
        normed,
        query_heads,
        key_heads,
        value_heads,
        attention,
        attention_low,
        context_low,
        middle,
        hidden_in,
        pre_gelu,
        active_low,
    )
    return (result, kept_values)


def backward_layer(hidden_state, grad_after, weights, lengths):
    (
        attn_gain,
        attn_shift,
        query_weight,
        query_bias,
        key_weight,
        value_weight,
        value_bias,
        out_weight,
        out_bias,
        mlp_gain,
        mlp_shift,
        up_weight,
        up_bias,
        down_weight,
        down_bias,
    ) = weights
    unused, kept_values = forward_layer(hidden_state, weights, lengths)
    (
        normed,
        query_heads,
        key_heads,
        value_heads,
        attention,
        attention_low,
        context_low,
        middle,
        hidden_in,
        pre_gelu,
        active_low,
    ) = kept_values
    clip_count, row_count, model_width = hidden_state.shape
    length_all = key_heads.shape[1]
    head_size = model_width // H
    query_scale = float(head_size) ** (-0.5)
    grad_low = grad_after.astype(jnp.bfloat16)
    grad_active = project_back(grad_low, down_weight)
    unused, gelu_pull = jax.vjp(gelu_exact, pre_gelu)
    grad_pre = gelu_pull(grad_active)[0].astype(jnp.bfloat16)
    grad_hidden = project_back(grad_pre, up_weight)
    unused, mlp_pull = jax.vjp(
        norm_affine, middle, mlp_gain.astype(jnp.float32), mlp_shift.astype(jnp.float32)
    )
    grad_middle_norm, grad_mlp_gain, grad_mlp_shift = mlp_pull(grad_hidden)
    grad_middle = grad_after + grad_middle_norm
    middle_low = grad_middle.astype(jnp.bfloat16)
    grad_context = project_back(middle_low, out_weight).astype(jnp.bfloat16)
    grad_context = grad_context.reshape(clip_count, row_count, H, head_size)
    grad_attention = jnp.einsum(
        "cqhd,ckhd->chqk", grad_context, value_heads, preferred_element_type=jnp.float32
    )
    value_part = jnp.einsum(
        "chqk,cqhd->ckhd", attention_low, grad_context, preferred_element_type=jnp.float32
    )
    grad_scores = attention * (
        grad_attention - jnp.sum(attention * grad_attention, axis=-1, keepdims=True)
    )
    scores_low = grad_scores.astype(jnp.bfloat16)
    grad_query = jnp.einsum(
        "chqk,ckhd->cqhd", scores_low, key_heads, preferred_element_type=jnp.float32
    )
    grad_query = grad_query.reshape(clip_count, row_count, model_width).astype(jnp.bfloat16)
    key_part = jnp.einsum(
        "chqk,cqhd->ckhd", scores_low, query_heads, preferred_element_type=jnp.float32
    )
    key_summed, value_summed = (
        lax.psum_scatter(
            key_part.reshape(clip_count, length_all, model_width).astype(jnp.bfloat16),
            "shard",
            scatter_dimension=1,
            tiled=True,
        ).astype(jnp.float32),
        lax.psum_scatter(
            value_part.reshape(clip_count, length_all, model_width).astype(jnp.bfloat16),
            "shard",
            scatter_dimension=1,
            tiled=True,
        ).astype(jnp.float32),
    )
    key_grad_low = key_summed.astype(jnp.bfloat16)
    value_grad_low = value_summed.astype(jnp.bfloat16)
    grad_normed = (
        project_back(grad_query, query_weight) * query_scale
        + project_back(key_grad_low, key_weight)
        + project_back(value_grad_low, value_weight)
    )
    unused, attn_pull = jax.vjp(
        norm_affine, hidden_state, attn_gain.astype(jnp.float32), attn_shift.astype(jnp.float32)
    )
    grad_input_norm, grad_attn_gain, grad_attn_shift = attn_pull(grad_normed)
    grad_before = grad_middle + grad_input_norm
    grad_down = weight_grad(active_low, grad_low)
    grad_down_bias = column_sum(grad_low)
    grad_up = weight_grad(hidden_in, grad_pre)
    grad_up_bias = column_sum(grad_pre)
    grad_out_weight = weight_grad(context_low, middle_low)
    grad_out_bias = column_sum(middle_low)
    grad_query_weight = weight_grad(normed, grad_query) * query_scale
    grad_query_bias = column_sum(grad_query) * query_scale
    grad_key_weight = weight_grad(normed, key_grad_low)
    grad_value_weight = weight_grad(normed, value_grad_low)
    grad_value_bias = column_sum(value_grad_low)
    owned_grads = (
        lax.psum_scatter(
            grad_attn_gain.astype(jnp.bfloat16), "shard", scatter_dimension=0, tiled=True
        ).astype(jnp.float32),
        lax.psum_scatter(
            grad_attn_shift.astype(jnp.bfloat16), "shard", scatter_dimension=0, tiled=True
        ).astype(jnp.float32),
        lax.psum_scatter(
            grad_query_weight.astype(jnp.bfloat16), "shard", scatter_dimension=0, tiled=True
        ).astype(jnp.float32),
        lax.psum_scatter(
            grad_query_bias.astype(jnp.bfloat16), "shard", scatter_dimension=0, tiled=True
        ).astype(jnp.float32),
        lax.psum_scatter(
            grad_key_weight.astype(jnp.bfloat16), "shard", scatter_dimension=0, tiled=True
        ).astype(jnp.float32),
        lax.psum_scatter(
            grad_value_weight.astype(jnp.bfloat16), "shard", scatter_dimension=0, tiled=True
        ).astype(jnp.float32),
        lax.psum_scatter(
            grad_value_bias.astype(jnp.bfloat16), "shard", scatter_dimension=0, tiled=True
        ).astype(jnp.float32),
        lax.psum_scatter(
            grad_out_weight.astype(jnp.bfloat16), "shard", scatter_dimension=0, tiled=True
        ).astype(jnp.float32),
        lax.psum_scatter(
            grad_out_bias.astype(jnp.bfloat16), "shard", scatter_dimension=0, tiled=True
        ).astype(jnp.float32),
        lax.psum_scatter(
            grad_mlp_gain.astype(jnp.bfloat16), "shard", scatter_dimension=0, tiled=True
        ).astype(jnp.float32),
        lax.psum_scatter(
            grad_mlp_shift.astype(jnp.bfloat16), "shard", scatter_dimension=0, tiled=True
        ).astype(jnp.float32),
        lax.psum_scatter(
            grad_up.astype(jnp.bfloat16), "shard", scatter_dimension=0, tiled=True
        ).astype(jnp.float32),
        lax.psum_scatter(
            grad_up_bias.astype(jnp.bfloat16), "shard", scatter_dimension=0, tiled=True
        ).astype(jnp.float32),
        lax.psum_scatter(
            grad_down.astype(jnp.bfloat16), "shard", scatter_dimension=0, tiled=True
        ).astype(jnp.float32),
        lax.psum_scatter(
            grad_down_bias.astype(jnp.bfloat16), "shard", scatter_dimension=0, tiled=True
        ).astype(jnp.float32),
    )
    return (grad_before, owned_grads)


def replica_layer(owned_grads):
    return (
        lax.psum(owned_grads[0].astype(jnp.bfloat16), "rep").astype(jnp.float32),
        lax.psum(owned_grads[1].astype(jnp.bfloat16), "rep").astype(jnp.float32),
        lax.psum(owned_grads[2].astype(jnp.bfloat16), "rep").astype(jnp.float32),
        lax.psum(owned_grads[3].astype(jnp.bfloat16), "rep").astype(jnp.float32),
        lax.psum(owned_grads[4].astype(jnp.bfloat16), "rep").astype(jnp.float32),
        lax.psum(owned_grads[5].astype(jnp.bfloat16), "rep").astype(jnp.float32),
        lax.psum(owned_grads[6].astype(jnp.bfloat16), "rep").astype(jnp.float32),
        lax.psum(owned_grads[7].astype(jnp.bfloat16), "rep").astype(jnp.float32),
        lax.psum(owned_grads[8].astype(jnp.bfloat16), "rep").astype(jnp.float32),
        lax.psum(owned_grads[9].astype(jnp.bfloat16), "rep").astype(jnp.float32),
        lax.psum(owned_grads[10].astype(jnp.bfloat16), "rep").astype(jnp.float32),
        lax.psum(owned_grads[11].astype(jnp.bfloat16), "rep").astype(jnp.float32),
        lax.psum(owned_grads[12].astype(jnp.bfloat16), "rep").astype(jnp.float32),
        lax.psum(owned_grads[13].astype(jnp.bfloat16), "rep").astype(jnp.float32),
        lax.psum(owned_grads[14].astype(jnp.bfloat16), "rep").astype(jnp.float32),
    )


def general_shards(
    inputs,
    lengths,
    cotangent,
    attn_gain,
    attn_shift,
    query_weight,
    query_bias,
    key_weight,
    value_weight,
    value_bias,
    out_weight,
    out_bias,
    mlp_gain,
    mlp_shift,
    up_weight,
    up_bias,
    down_weight,
    down_bias,
):
    params = (
        attn_gain,
        attn_shift,
        query_weight,
        query_bias,
        key_weight,
        value_weight,
        value_bias,
        out_weight,
        out_bias,
        mlp_gain,
        mlp_shift,
        up_weight,
        up_bias,
        down_weight,
        down_bias,
    )
    layers = attn_gain.shape[0]
    hidden_state = inputs.astype(jnp.float32)
    kept_inputs = []
    kept_weights = []
    for layer_index in range(layers):
        gathered = fetch_forward(layer_slice(params, layer_index))
        kept_inputs.append(hidden_state)
        kept_weights.append(gathered)
        hidden_state, unused = forward_layer(hidden_state, gathered, lengths)
    output = hidden_state.astype(jnp.bfloat16)
    row_count = inputs.shape[1]
    first_row = lax.axis_index("shard") * row_count
    positions = first_row + jnp.arange(row_count, dtype=jnp.int32)
    row_mask = (positions[None, :] < lengths[:, None]).astype(jnp.float32)
    grad_state = cotangent.astype(jnp.float32) * row_mask[:, :, None]
    owned_list = [None] * layers
    for layer_index in reversed(range(layers)):
        gathered = fetch_again(layer_slice(params, layer_index))
        grad_state, owned_grads = backward_layer(
            kept_inputs[layer_index], grad_state, gathered, lengths
        )
        owned_grads = replica_layer(owned_grads)
        owned_list[layer_index] = owned_grads
    stacked = tuple(
        (
            jnp.stack([owned_list[layer_index][member] for layer_index in range(layers)])
            for member in range(15)
        )
    )
    return (
        output,
        grad_state,
        stacked[0],
        stacked[1],
        stacked[2],
        stacked[3],
        stacked[4],
        stacked[5],
        stacked[6],
        stacked[7],
        stacked[8],
        stacked[9],
        stacked[10],
        stacked[11],
        stacked[12],
        stacked[13],
        stacked[14],
    )


def device_index(a, b, core, z):
    return ((a * 2 + b) * 2 + core) * 4 + z


def make_pairs(target):
    return [
        (device_index(a, b, core, z), device_index(*target(a, b, core, z)))
        for a in range(2)
        for b in range(2)
        for core in range(2)
        for z in range(4)
    ]


PAIRS = {
    "a": make_pairs(lambda a, b, c, z: (1 - a, b, c, z)),
    "b": make_pairs(lambda a, b, c, z: (a, 1 - b, c, z)),
    "ab": make_pairs(lambda a, b, c, z: (1 - a, 1 - b, c, z)),
    "core": make_pairs(lambda a, b, c, z: (a, b, 1 - c, z)),
    "z1": make_pairs(lambda a, b, c, z: (a, b, c, (z + 1) % 4)),
    "z2": make_pairs(lambda a, b, c, z: (a, b, c, (z + 2) % 4)),
    "z3": make_pairs(lambda a, b, c, z: (a, b, c, (z + 3) % 4)),
}
for step in range(2):
    PAIRS["in%d" % step] = make_pairs(
        lambda a, b, c, z, step=step: (a, b, z // 2, 2 * c + (z + step) % 2)
    )
    PAIRS["out%d" % step] = [(target, source) for source, target in PAIRS["in%d" % step]]


def send(values, way):
    return lax.ppermute(values, BOTH, PAIRS[way])


def pick(values, index, axis=0):
    return lax.dynamic_index_in_dim(values, index, axis, keepdims=False)


def place():
    rep = lax.axis_index("rep")
    return rep // 4, (rep // 2) % 2, rep % 2, lax.axis_index("shard")


def after(values, *others):
    return lax.optimization_barrier((values,) + others)[0]


MESH = pl.DeviceIdType.MESH

def device(a, b, core, z):
    return ((a * 2 + b) * 2 + core, z)


class Net:
    def __init__(self, sent, arrived):
        self.sent, self.arrived = sent, arrived
        self.copies, self.count = [], 0
    def push(self, source, target_ref, target, sent=None):
        copy = pltpu.make_async_remote_copy(
            src_ref=source, dst_ref=target_ref, send_sem=self.sent if sent is None else sent,
            recv_sem=self.arrived.at[self.count], device_id=target, device_id_type=MESH)
        copy.start()
        self.count += 1
        if sent is None:
            self.copies.append(copy)
        return copy

    def drain(self):
        for copy in self.copies:
            copy.wait_send()

def greet(targets):
    barrier = pltpu.get_barrier_semaphore()
    for target in targets:
        pl.semaphore_signal(barrier, inc=1, device_id=target, device_id_type=MESH)
    pl.semaphore_wait(barrier, len(targets))

def gather_regions(index, zs, chip, core):
    part = chip * 2 + core
    def rows(base, size):
        return pl.ds(pl.multiple_of(base, 8), size)
    if index < 2:
        return 0, (pl.ds(2 * index, 2), rows(zs * 320 + part * 40, 40), slice(None))
    if index < 4:
        return 1, (rows(zs * 320 + part * 40, 40), pl.ds((index - 2) * 2560, 2560))
    return 2, (rows(zs * 1280 + part * 160 + (index - 4) * 80, 80), slice(None))


NN = (((1,), (0,)), ((), ()))
TN = (((0,), (0,)), ((), ()))
NT = (((1,), (1,)), ((), ()))
TOKENS = 512
ROOT_HALF = math.sqrt(0.5)
ROOT_TWO_PI = math.sqrt(2.0 * math.pi)

def dot(left, right, numbers=NN):
    return lax.dot_general(left, right, numbers, preferred_element_type=F32)


def tile(i, size):
    return pl.ds(pl.multiple_of(i * size, size), size)


def stream(count, copy, body):
    copy(0, 0).start()

    @pl.loop(0, count)
    def _(i):
        slot = i % 2

        @pl.when(i + 1 < count)
        def _():
            copy(i + 1, 1 - slot).start()

        copy(i, slot).wait()
        body(i, slot)


def transpose_into(target, source, rows):
    @pl.loop(0, rows // 128)
    def _(i):
        target[tile(i, 128), :] = source[:, tile(i, 128)].T


def gather_program(net, layers, shards, outs, copies, local):
    a, b, core, z = place()
    behind = [lax.rem(z + 4 - s, 4) for s in range(4)]
    to_z = [device(a, b, core, lax.rem(z + s, 4)) for s in range(4)]
    to_a, to_b, to_core = device(1 - a, b, core, z), device(a, 1 - b, core, z), device(a, b, 1 - core, z)
    count = 6 * layers
    twin = [[] for _ in range(count)]

    def refs_at(index, zs, pa, pb, whose):
        which, at = gather_regions(index % 6, zs, pa * 2 + pb, core)
        return whose[which].at[index // 6].at[at]

    def start(index):
        return [net.push(refs_at(index, 0, a, b, shards), refs_at(index, z, a, b, outs), to_z[s]) for s in (1, 2, 3)]

    def on(index, s, pa, pb, target):
        ref = refs_at(index, behind[s], pa, pb, outs)
        copy = net.push(ref, ref, target)
        if target is to_core:
            twin[index].append(copy)
        return copy

    def own_copies(step):
        layer, which = step // 3, step % 3
        shard, out = shards[which].at[layer], outs[which].at[layer]
        ins, back = [], []
        for i in range(4):
            if which == 0:
                source, target = shard.at[i], out.at[i, pl.ds(pl.multiple_of(z * 320, 8), 320), :]
            elif which == 1:
                source = shard.at[:, pl.ds(i * 1280, 1280)]
                target = out.at[pl.ds(pl.multiple_of(z * 320, 8), 320), pl.ds(i * 1280, 1280)]
            else:
                source = shard.at[pl.ds(i * 320, 320), :]
                target = out.at[pl.ds(pl.multiple_of(z * 1280 + i * 320, 8), 320), :]
            ins.append(pltpu.make_async_copy(source, copies.at[i], local))
            back.append(pltpu.make_async_copy(copies.at[i], target, local))
        for copy in ins:
            copy.start()
        for copy in ins:
            copy.wait()
        for copy in back:
            copy.start()
        for copy in back:
            copy.wait()

    zed, mid, diag = {}, {}, {}
    zed[0] = start(0)
    zed[1] = start(1)
    own_copies(0)
    yield twin
    for t in range(count + 2):
        if t < count:
            mid[t] = {}
            for s in (1, 2, 3):
                zed[t][s - 1].wait_recv()
                mid[t][s] = (on(t, s, a, b, to_b), on(t, s, a, b, to_a))
                on(t, s, a, b, to_core)
            if t + 2 < count:
                zed[t + 2] = start(t + 2)
        if 0 <= t - 1 < count:
            k = t - 1
            diag[k] = {}
            for s in (1, 2, 3):
                via_b, via_a = mid[k][s]
                via_b.wait_recv()
                on(k, s, a, 1 - b, to_core)
                if (s + k) % 2 == 0:
                    diag[k][s] = on(k, s, a, 1 - b, to_a)
                via_a.wait_recv()
                on(k, s, 1 - a, b, to_core)
                if (s + k) % 2 == 1:
                    diag[k][s] = on(k, s, 1 - a, b, to_b)
        if 0 <= t - 2 < count:
            k = t - 2
            for s in (1, 2, 3):
                diag[k][s].wait_recv()
                on(k, s, 1 - a, 1 - b, to_core)
        if t + 1 < 3 * layers:
            own_copies(t + 1)
        yield twin


def normalize_rows(source, target, gain, shift, rows=64):
    @pl.loop(0, TOKENS // rows)
    def _(i):
        values = source[tile(i, rows), :]
        center = values - jnp.mean(values, axis=-1, keepdims=True)
        scale = lax.rsqrt(jnp.mean(center * center, axis=-1, keepdims=True) + EPSILON)
        target[tile(i, rows), :] = (center * scale * gain + shift).astype(BF16)


def attend_heads(first, last, query, key, value, far, masks, context, lse):
    @pl.loop(first, last)
    def _(h):
        at = pl.ds(pl.multiple_of(h * 80, 16), 80)
        q = query[at, :]
        s0 = dot(key[at, :], q, TN) + masks[0]
        s1 = dot(far[0, at, :], q, TN) + masks[1]
        top = jnp.maximum(jnp.max(s0, axis=0, keepdims=True), jnp.max(s1, axis=0, keepdims=True))
        e0, e1 = jnp.exp(s0 - top), jnp.exp(s1 - top)
        total = jnp.sum(e0, axis=0, keepdims=True) + jnp.sum(e1, axis=0, keepdims=True)
        out = dot(value[at, :], e0.astype(BF16)) + dot(far[1, at, :], e1.astype(BF16))
        context[at, :] = (out / total).astype(BF16)
        lse[h] = top + jnp.log(total)


def forward_kernel(layers, *refs):
    (tokens, attn, up, down, vectors, masks,
     attn_full, up_full, down_full, keep_normed, keep_qkv, keep_far, keep_lse, keep_context, keep_middle,
     keep_hidden, keep_slope, keep_active, states,
     state, middle, normed, normed_t, hidden_t, qkv, far, context_t, context, active, active_t, slope, lse,
     small_w, up_w, down_w, copies, product,
     local, wsem, saved, swapped, sent, arrived) = refs
    a, b, core, z = place()
    to_core = device(a, b, 1 - core, z)
    greet([device(a, b, core, lax.rem(z + s, 4)) for s in (1, 2, 3)]
          + [device(1 - a, b, core, z), device(a, 1 - b, core, z), to_core])
    net = Net(sent, arrived)
    load = pltpu.make_async_copy(tokens, state, local)
    load.start()
    load.wait()
    ticks = gather_program(net, layers, (attn, up, down), (attn_full, up_full, down_full), copies, local)
    twin = next(ticks)
    clock = [-1]

    def pump(until):
        while clock[0] < until:
            next(ticks)
            clock[0] += 1

    def ready(*chunks):
        pump(max(chunks) + 2)
        for chunk in chunks:
            for copy in twin[chunk]:
                copy.wait_recv()

    saves = []

    def save(source, target):
        copy = pltpu.make_async_copy(source, target, saved)
        copy.start()
        saves.append(copy)

    scale = float(80) ** (-0.5)
    for layer in range(layers):
        base = 6 * layer
        vec = vectors.at[layer]

        def row(i):
            return vec[i : i + 1, :]

        weights = attn_full.at[layer]
        save(state, states.at[layer])
        normalize_rows(state, normed, row(0), row(1))
        transpose_into(normed_t, normed, 1280)
        save(normed_t, keep_normed.at[layer])
        ready(base, base + 1)

        def project(which, bias, factor, target):
            def copy(i, slot):
                return pltpu.make_async_copy(weights.at[which, :, tile(i, 256)], small_w.at[slot], wsem.at[slot])

            def body(i, slot):
                out = dot(normed[...], small_w[slot])
                if bias is not None:
                    out = out + vec[bias : bias + 1, tile(i, 256)]
                if factor != 1.0:
                    out = out * factor
                target[tile(i, 256), :] = out.astype(BF16).T

            stream(5, copy, body)

        project(1, None, 1.0, qkv.at[1])
        project(2, 3, 1.0, qkv.at[2])
        swap = net.push(qkv.at[pl.ds(1, 2)], far.at[layer], to_core, swapped)
        project(0, 2, scale, qkv.at[0])
        pump(base + 4)
        swap.wait()
        for part in range(4):
            if part == 2:
                pump(base + 5)
            attend_heads(4 * part, 4 * part + 4, qkv.at[0], qkv.at[1], qkv.at[2], far.at[layer], masks, context_t, lse)
        save(qkv, keep_qkv.at[layer])
        save(far.at[layer], keep_far.at[layer])
        save(lse, keep_lse.at[layer])
        save(context_t, keep_context.at[layer])

        @pl.loop(0, 10)
        def _(i):
            context[:, tile(i, 128)] = context_t[tile(i, 128), :].T

        def copy_out(i, slot):
            return pltpu.make_async_copy(weights.at[3, :, tile(i, 256)], small_w.at[slot], wsem.at[slot])

        def body_out(i, slot):
            at = tile(i, 256)
            middle[:, at] = state[:, at] + dot(context[...], small_w[slot]) + vec[4:5, at]

        stream(5, copy_out, body_out)
        save(middle, keep_middle.at[layer])
        normalize_rows(middle, normed, row(5), row(6))
        transpose_into(hidden_t, normed, 1280)
        save(hidden_t, keep_hidden.at[layer])
        pump(base + 6)
        ready(base + 2, base + 3)

        def copy_up(i, slot):
            return pltpu.make_async_copy(up_full.at[layer, :, tile(i, 512)], up_w.at[slot], wsem.at[slot])

        def body_up(i, slot):
            at = tile(i, 512)
            product[...] = dot(normed[...], up_w[slot])
            bias = vec[pl.ds(8 + i, 1), :512]

            @pl.loop(0, 16)
            def _(j):
                u = product[tile(j, 32), :] + bias
                half = 0.5 * (1.0 + lax.erf(u * ROOT_HALF))
                active[tile(j, 32), at] = (u * half).astype(BF16)
                slope[tile(j, 32), at] = (half + u * jnp.exp(-0.5 * u * u) * (1.0 / ROOT_TWO_PI)).astype(BF16)

            active_t[at, :] = active[:, at].T

        stream(10, copy_up, body_up)
        save(slope, keep_slope.at[layer])
        save(active_t, keep_active.at[layer])
        ready(base + 4, base + 5)

        def copy_down(i, slot):
            return pltpu.make_async_copy(down_full.at[layer, :, tile(i, 256)], down_w.at[slot], wsem.at[slot])

        for copy in saves:
            copy.wait()
        saves.clear()

        def body_down(i, slot):
            at = tile(i, 256)
            state[:, at] = middle[:, at] + dot(active[...], down_w[slot]) + vec[7:8, at]

        stream(5, copy_down, body_down)
    save(state, states.at[layers])
    for copy in saves:
        copy.wait()
    net.drain()


def forward_all(tokens, attn, up, down, vectors, masks):
    any_ = pl.BlockSpec(memory_space=pl.ANY)
    vmem = pl.BlockSpec(memory_space=pltpu.VMEM)
    layers = up.shape[0]
    t = TOKENS

    def hbm(shape, dtype=BF16):
        return jax.ShapeDtypeStruct((layers,) + shape, dtype)

    out_shape = (
        hbm((4, 1280, 1280)), hbm((1280, 5120)), hbm((5120, 1280)),
        hbm((1280, t)), hbm((3, 1280, t)), hbm((2, 1280, t)), hbm((H, 1, t), F32), hbm((1280, t)), hbm((t, 1280), F32),
        hbm((1280, t)), hbm((t, 5120)), hbm((5120, t)), jax.ShapeDtypeStruct((layers + 1, t, 1280), F32),
    )
    v = pltpu.VMEM
    return pl.pallas_call(
        functools.partial(forward_kernel, layers),
        out_shape=out_shape,
        in_specs=[any_] * 4 + [vmem] * 2,
        out_specs=(any_,) * len(out_shape),
        scratch_shapes=[
            v((t, 1280), F32), v((t, 1280), F32), v((t, 1280), BF16), v((1280, t), BF16), v((1280, t), BF16),
            v((3, 1280, t), BF16), v((layers, 2, 1280, t), BF16), v((1280, t), BF16), v((t, 1280), BF16),
            v((t, 5120), BF16), v((5120, t), BF16), v((t, 5120), BF16), v((H, 1, t), F32),
            v((2, 1280, 256), BF16), v((2, 1280, 512), BF16), v((2, 5120, 256), BF16), v((4, 320, 1280), BF16),
            v((t, 512), F32),
            pltpu.SemaphoreType.DMA, pltpu.SemaphoreType.DMA((2,)), pltpu.SemaphoreType.DMA,
            pltpu.SemaphoreType.DMA, pltpu.SemaphoreType.DMA, pltpu.SemaphoreType.DMA((6 * layers * 24 + layers,)),
        ],
        compiler_params=pltpu.CompilerParams(collective_id=1, has_side_effects=True, vmem_limit_bytes=63 << 20),
        name="forward_all",
    )(tokens, attn, up, down, vectors, masks)


def add(*parts):
    total = parts[0].astype(F32)
    for part in parts[1:]:
        total = total + part.astype(F32)
    return total.astype(BF16)


ITEMS_A_LAYER = 12
RING, XRING = 8, 4


def streams(count, copies, body):
    for copy in copies(0, 0):
        copy.start()

    @pl.loop(0, count)
    def _(i):
        slot = i % 2

        @pl.when(i + 1 < count)
        def _():
            for copy in copies(i + 1, 1 - slot):
                copy.start()

        for copy in copies(i, slot):
            copy.wait()
        body(i, slot)


def add_blocks(blocks, target, parts):
    @pl.loop(0, blocks * 5)
    def _(i):
        block = i // 5
        at = pl.ds(pl.multiple_of((i % 5) * 16, 16), 16)
        refs = [part(block) for part in parts]
        sums = refs[0][at, :].astype(F32)
        for ref in refs[1:]:
            sums = sums + ref[at, :].astype(F32)
        target(block)[at, :] = sums.astype(BF16)


def backward_kernel(layers, *refs):
    (cotangent, attn_full, up_full, down_full, normed_t, qkv, far, lse_all, context_t, middles, hidden_t, slopes,
     active_t, states, vectors, masks,
     grad_out, down_out, up_out, out_out, qkv_out, sums,
     active_far, hidden_far, context_far, normed_far, grad_f_far, grad_pre_far, grad_o_far, grad_far, grad_kv_far,
     g, low, gp, gs, gh, rows_in, big, dfar, heads_in, far_in, lse, wide_w, slope_in, left_in,
     xs, got1s, got2s, got3s, finals,
     local, lsem, swapped, item_sent, item_local, sent, arrived) = refs
    a, b, core, z = place()
    to_z = [device(a, b, core, lax.rem(z + s, 4)) for s in range(4)]
    to_a, to_b, to_core = device(1 - a, b, core, z), device(a, 1 - b, core, z), device(a, b, 1 - core, z)
    greet(to_z[1:] + [to_a, to_b, to_core])
    net = Net(sent, arrived)
    scale = float(80) ** (-0.5)
    side = {"a": (a, to_a), "b": (b, to_b)}

    def program(number, order, spot):
        slot = number % RING
        x, got1, got2, got3, final = (
            xs.at[number % XRING], got1s.at[slot], got2s.at[slot], got3s.at[slot], finals.at[slot])
        target = side[order[0]][1]
        other, other_target = side["b" if order[0] == "a" else "a"]

        def push(source, target_ref, target, stage):
            return net.push(source, target_ref, target, item_sent.at[slot, stage])

        first = push(x.at[1], got1, target, 0)
        yield
        first.wait()
        add_blocks(8, lambda i: got1.at[i // 2, i % 2],
                   [lambda i: got1.at[i // 2, i % 2], lambda i: x.at[0, i // 2, i % 2]])
        if order[1] == "z":
            nexts = [push(got1.at[lax.rem(z + s, 4)], got2.at[pl.ds(2 * s - 2, 2)], to_z[s], 1) for s in (1, 2, 3)]
        else:
            nexts = [push(got1.at[:, 1 - other], got2.at[pl.ds(0, 4)], other_target, 1)]
        yield
        for copy in nexts:
            copy.wait()
        if order[1] == "z":
            add_blocks(2, lambda i: got1.at[z, i],
                       [lambda i: got1.at[z, i]] + [lambda i, s=s: got2.at[2 * s + i] for s in range(3)])
            nexts = [push(got1.at[z, 1 - other], got3.at[0], other_target, 2)]
        else:
            add_blocks(4, lambda i: got2.at[i], [lambda i: got2.at[i], lambda i: got1.at[i, other]])
            nexts = [push(got2.at[lax.rem(z + s, 4)], got3.at[s - 1], to_z[s], 2) for s in (1, 2, 3)]
        yield
        for copy in nexts:
            copy.wait()
        if order[1] == "z":
            add_blocks(1, lambda i: final, [lambda i: got1.at[z, other], lambda i: got3.at[0]])
        else:
            add_blocks(1, lambda i: final, [lambda i: got2.at[z]] + [lambda i, s=s: got3.at[s] for s in range(3)])
        mine = pltpu.make_async_copy(final, spot(core, a, b), item_local.at[slot])
        mine.start()
        via = [push(final, spot(core, a, b), target, 3) for target in (to_a, to_b, to_core)]
        yield
        mine.wait()
        for copy in via:
            copy.wait()

        def on(pa, pb, target):
            return net.push(spot(core, pa, pb), spot(core, pa, pb), target)

        diag = on(1 - a, b, to_b) if number % 2 == 0 else on(a, 1 - b, to_a)
        twin = [on(1 - a, b, to_core), on(a, 1 - b, to_core)]
        yield
        diag.wait_recv()
        twin.append(on(1 - a, 1 - b, to_core))
        yield
        for copy in twin:
            copy.wait_recv()
        yield

    programs, stage, age = [], [], []

    def advance(number):
        next(programs[number])
        stage[number] += 1

    def round_(lead=1):
        for number in range(len(programs)):
            age[number] += 1
            if stage[number] < 7 and (stage[number] > 1 or age[number] >= lead):
                advance(number)

    def room(extra):
        while any(stage[i] < 2 for i in range(max(0, len(programs) + extra - XRING))):
            round_()
        while any(stage[i] < 5 for i in range(max(0, len(programs) + extra - RING))):
            round_()

    def send_item(order, spot):
        number = len(programs)
        programs.append(program(number, order, spot))
        stage.append(0)
        age.append(0)
        advance(number)

    def weight_gradient(height, own, far_, parts):
        base = len(programs)

        def copies(i, slot):
            return [
                pltpu.make_async_copy(own(i), left_in.at[slot, 0, pl.ds(0, height), :], lsem.at[slot]),
                pltpu.make_async_copy(far_(i), left_in.at[slot, 1, pl.ds(0, height), :], lsem.at[slot]),
            ]

        def body(i, slot):
            for right, far_right, factor, targets in parts:
                out = dot(left_in[slot, 0, :height, :], right()) + dot(left_in[slot, 1, :height, :], far_right())
                if factor != 1.0:
                    out = out * factor
                out = out.astype(BF16)
                for item, order, first in targets:
                    x = xs.at[(base + item) % XRING]
                    for pa in range(2):
                        for pb in range(2):
                            row = (pa * 2 + pb) * (height // 4) + first
                            block = out[row : row + 80, :]
                            if order[0] == "a":
                                x[lax.rem(pa + a, 2), i, pb] = block
                            else:
                                x[lax.rem(pb + b, 2), i, pa] = block

        streams(4, copies, body)

    def fetch(*pairs):
        copies = [pltpu.make_async_copy(x, y, local) for x, y in pairs]
        for copy in copies:
            copy.start()
        for copy in copies:
            copy.wait()

    def norm_back(source, gain, gain_at, layer, lowered):
        def copies(i, slot):
            return [pltpu.make_async_copy(source.at[tile(i, 64), :], rows_in.at[slot], lsem.at[slot])]

        def body(i, slot):
            at = tile(i, 64)
            values = rows_in[slot]
            center = values - jnp.mean(values, axis=-1, keepdims=True)
            s = lax.rsqrt(jnp.mean(center * center, axis=-1, keepdims=True) + EPSILON)
            unit = center * s
            grad = gh[at, :]
            e = grad * gain
            out = g[at, :] + s * (
                e - jnp.mean(e, axis=-1, keepdims=True) - unit * jnp.mean(e * unit, axis=-1, keepdims=True))
            g[at, :] = out
            sums[layer, pl.ds(gain_at, 1), :] += jnp.sum(grad * unit, axis=0, keepdims=True)
            sums[layer, pl.ds(gain_at + 1, 1), :] += jnp.sum(grad, axis=0, keepdims=True)
            if lowered:
                small = out.astype(BF16)
                low[0, at, :] = small
                sums[layer, pl.ds(4, 1), :] += jnp.sum(small.astype(F32), axis=0, keepdims=True)

        streams(8, copies, body)

    swaps = {}
    for layer in reversed(range(layers)):
        swaps[layer] = [
            net.push(active_t.at[layer, :, 1 - core], active_far.at[layer], to_core),
            net.push(hidden_t.at[layer], hidden_far.at[layer], to_core),
            net.push(context_t.at[layer], context_far.at[layer], to_core),
            net.push(normed_t.at[layer], normed_far.at[layer], to_core),
        ]
    fetch((cotangent, g))
    sums[...] = jnp.zeros_like(sums)

    for layer in reversed(range(layers)):
        vec = vectors.at[layer]

        @pl.loop(0, 8)
        def _(i):
            at = tile(i, 64)
            small = g[at, :].astype(BF16)
            low[0, at, :] = small
            sums[layer, pl.ds(7, 1), :] += jnp.sum(small.astype(F32), axis=0, keepdims=True)

        swap = net.push(low.at[0], grad_f_far.at[layer], to_core, swapped)
        swap.wait()
        fetch((grad_f_far.at[layer], low.at[1]))
        for copy in swaps[layer]:
            copy.wait_recv()

        def down_spot(half, column):
            def spot(pc, pa, pb):
                row = pc * 640 + (pa * 2 + pb) * 160 + half * 80
                return down_out.at[layer, pl.ds(pl.multiple_of(row, 16), 80), pl.ds(column * 640, 640)]
            return spot

        for column in range(2):
            room(2)
            weight_gradient(
                640, lambda i: active_t.at[layer, i, core], lambda i: active_far.at[layer, i],
                [(lambda column=column: low[0, :, column * 640 : column * 640 + 640],
                  lambda column=column: low[1, :, column * 640 : column * 640 + 640], 1.0,
                  [(0, "azb", 0), (1, "bza", 80)])],
            )
            send_item("azb", down_spot(0, column))
            send_item("bza", down_spot(1, column))
            if column == 0:
                round_()

        def copies_down(i, slot):
            return [
                pltpu.make_async_copy(down_full.at[layer, tile(i, 512), :], wide_w.at[slot], lsem.at[slot]),
                pltpu.make_async_copy(slopes.at[layer, :, tile(i, 512)], slope_in.at[slot], lsem.at[slot]),
            ]

        def body_down(i, slot):
            at = tile(i, 512)
            gh[:, :512] = dot(low[0], wide_w[slot], NT)

            @pl.loop(0, 8)
            def _(j):
                rows = tile(j, 64)
                small = (gh[rows, :512] * slope_in[slot, rows, :].astype(F32)).astype(BF16)
                gp[rows, at] = small
                sums[layer, pl.ds(8 + i, 1), :512] += jnp.sum(small.astype(F32), axis=0, keepdims=True)

        streams(10, copies_down, body_down)
        swap = net.push(gp.at[:, pl.ds(pl.multiple_of((1 - core) * 2560, 128), 2560)], grad_pre_far.at[layer], to_core,
                        swapped)
        round_()
        swap.wait()
        fetch((grad_pre_far.at[layer], gs))

        def up_spot(unit):
            def spot(pc, pa, pb):
                return up_out.at[layer, pl.ds(pl.multiple_of((pa * 2 + pb) * 80, 16), 80),
                                 pl.ds(pl.multiple_of(pc * 2560 + unit * 640, 128), 640)]
            return spot

        def rows_of(values, i):
            return values.at[layer, pl.ds(pl.multiple_of(i * 320, 16), 320), :]

        for pair in range(2):
            room(2)
            weight_gradient(
                320, lambda i: rows_of(hidden_t, i), lambda i: rows_of(hidden_far, i),
                [(lambda unit=unit: gp[:, pl.ds(pl.multiple_of(core * 2560 + unit * 640, 128), 640)],
                  lambda unit=unit: gs[:, unit * 640 : unit * 640 + 640], 1.0,
                  [(unit % 2, ("azb", "bza")[unit % 2], 0)]) for unit in (2 * pair, 2 * pair + 1)],
            )
            send_item("azb", up_spot(2 * pair))
            send_item("bza", up_spot(2 * pair + 1))
            if pair == 0:
                round_()

        def copies_up(i, slot):
            return [
                pltpu.make_async_copy(up_full.at[layer, tile(i, 256), pl.ds(k * 512, 512)],
                                      big.at[pl.ds(pl.multiple_of(slot * 2560 + k * 256, 256), 256), :], lsem.at[slot])
                for k in range(10)
            ]

        def body_up(i, slot):
            total_ = None
            for k in range(10):
                part = dot(gp[:, k * 512 : k * 512 + 512],
                           big[pl.ds(pl.multiple_of(slot * 2560 + k * 256, 256), 256), :], NT)
                total_ = part if total_ is None else total_ + part
            gh[:, tile(i, 256)] = total_

        streams(5, copies_up, body_up)
        round_()
        norm_back(middles.at[layer], vec[5:6, :], 5, layer, True)
        swap = net.push(low.at[0, :, pl.ds(pl.multiple_of((1 - core) * 640, 128), 640)], grad_o_far.at[layer], to_core,
                        swapped)

        def copies_out(i, slot):
            return [pltpu.make_async_copy(attn_full.at[layer, 3, tile(i, 256), :], wide_w.at[slot, pl.ds(0, 256), :],
                                          lsem.at[slot])]

        def body_out(i, slot):
            big[pl.ds(pl.multiple_of(3840 + i * 256, 256), 256), :] = dot(
                wide_w[slot, :256, :], low[0], NT).astype(BF16)

        streams(5, copies_out, body_out)
        swap.wait()
        fetch((grad_o_far.at[layer], low.at[1, :, pl.ds(0, 640)]), (lse_all.at[layer], lse))

        def small_spot(whole):
            def spot(pc, pa, pb):
                return whole.at[pl.ds(pl.multiple_of((pa * 2 + pb) * 80, 16), 80),
                                pl.ds(pl.multiple_of(pc * 640, 128), 640)]
            return spot

        room(1)
        weight_gradient(
            320, lambda i: rows_of(context_t, i), lambda i: rows_of(context_far, i),
            [(lambda: low[0, :, pl.ds(pl.multiple_of(core * 640, 128), 640)], lambda: low[1, :, :640], 1.0,
              [(0, "abz", 0)])],
        )
        send_item("abz", small_spot(out_out.at[layer]))
        round_()

        def copies_head(h, slot):
            at = pl.ds(pl.multiple_of(h * 80, 16), 80)
            return [
                pltpu.make_async_copy(qkv.at[layer, :, at, :], heads_in.at[slot, pl.ds(0, 3)], lsem.at[slot]),
                pltpu.make_async_copy(far.at[layer, :, at, :], heads_in.at[slot, pl.ds(3, 2)], lsem.at[slot]),
            ]

        def body_head(h, slot):
            at = pl.ds(pl.multiple_of(h * 80, 16), 80)
            at_k = pl.ds(pl.multiple_of(1280 + h * 80, 16), 80)
            at_v = pl.ds(pl.multiple_of(2560 + h * 80, 16), 80)
            query, norm = heads_in[slot, 0], lse[h]
            grad = big[pl.ds(pl.multiple_of(3840 + h * 80, 16), 80), :]
            halves, delta = [], None
            for k, v, mask, target in ((1, 2, 0, big.at[at_v, :]), (3, 4, 1, dfar.at[1, at, :])):
                p = jnp.exp(dot(heads_in[slot, k], query, TN) + masks[mask] - norm)
                dp = dot(heads_in[slot, v], grad, TN)
                part = jnp.sum(p * dp, axis=0, keepdims=True)
                delta = part if delta is None else delta + part
                target[...] = dot(grad, p.astype(BF16), NT).astype(BF16)
                halves.append((p, dp))
            total_ = None
            for (p, dp), k, target in zip(halves, (1, 3), (big.at[at_k, :], dfar.at[0, at, :])):
                ds = (p * (dp - delta)).astype(BF16)
                part = dot(heads_in[slot, k], ds)
                total_ = part if total_ is None else total_ + part
                target[...] = dot(query, ds, NT).astype(BF16)
            big[at, :] = total_.astype(BF16)

        for part in range(2):
            streams(8, lambda i, slot: copies_head(i + 8 * part, slot), lambda i, slot: body_head(i + 8 * part, slot))
            round_()
        swap = net.push(dfar, grad_kv_far.at[layer], to_core, swapped)
        swap.wait()

        def copies_far(i, slot):
            return [pltpu.make_async_copy(grad_kv_far.at[layer, :, tile(i, 128), :], far_in.at[slot], lsem.at[slot])]

        def body_far(i, slot):
            at = tile(i, 128)
            query = big[at, :].T
            gp[:, at] = query
            sums[layer, 2:3, at] = jnp.sum(query.astype(F32), axis=0, keepdims=True) * scale
            for which in range(2):
                rows = pl.ds(pl.multiple_of(1280 + which * 1280 + i * 128, 128), 128)
                both = (big[rows, :].astype(F32) + far_in[slot, which].astype(F32)).astype(BF16).T
                gp[:, pl.ds(pl.multiple_of(1280 + which * 1280 + i * 128, 128), 128)] = both
                if which == 1:
                    sums[layer, 3:4, at] = jnp.sum(both.astype(F32), axis=0, keepdims=True)

        streams(10, copies_far, body_far)
        swap = [
            net.push(gp.at[:, pl.ds(pl.multiple_of(t * 1280 + (1 - core) * 640, 128), 640)], grad_far.at[layer, t],
                     to_core, swapped)
            for t in range(3)
        ]
        for copy in swap:
            copy.wait()
        fetch(*[(grad_far.at[layer, t], gs.at[:, pl.ds(t * 640, 640)]) for t in range(3)])
        for group in ((0, 1), (2,)):
            room(len(group))
            weight_gradient(
                320, lambda i: rows_of(normed_t, i), lambda i: rows_of(normed_far, i),
                [(lambda t=t: gp[:, pl.ds(pl.multiple_of(t * 1280 + core * 640, 128), 640)],
                  lambda t=t: gs[:, t * 640 : t * 640 + 640], scale if t == 0 else 1.0,
                  [(t % 2, ("baz", "abz")[t % 2], 0)]) for t in group],
            )
            for t in group:
                send_item(("baz", "abz")[t % 2], small_spot(qkv_out.at[layer, t]))
            if len(group) == 2:
                round_()

        def copies_back(i, slot):
            return [pltpu.make_async_copy(attn_full.at[layer, i // 5, tile(i % 5, 256), :],
                                          wide_w.at[slot, pl.ds(0, 256), :], lsem.at[slot])]

        def body_back(i, slot):
            at = tile(i % 5, 256)
            out = dot(gp[:, pl.ds(pl.multiple_of((i // 5) * 1280, 128), 1280)], wide_w[slot, :256, :], NT)

            @pl.when(i < 5)
            def _():
                gh[:, at] = out * scale

            @pl.when(i >= 5)
            def _():
                gh[:, at] += out

        streams(15, copies_back, body_back)
        round_()
        norm_back(states.at[layer], vec[0:1, :], 0, layer, False)
        if layer > 0:
            round_()
    store = pltpu.make_async_copy(g, grad_out, local)
    store.start()
    while any(s < 7 for s in stage):
        round_()
    store.wait()
    net.drain()


def backward_all(cotangent, weights, kept, vectors, masks):
    any_ = pl.BlockSpec(memory_space=pl.ANY)
    vmem = pl.BlockSpec(memory_space=pltpu.VMEM)
    layers = vectors.shape[0]
    t = TOKENS

    def hbm(shape, dtype=BF16):
        return jax.ShapeDtypeStruct((layers,) + shape, dtype)

    out_shape = (
        jax.ShapeDtypeStruct((t, 1280), F32), hbm((1280, 1280)), hbm((320, 5120)), hbm((320, 1280)), hbm((3, 320, 1280)),
        hbm((24, 1280), F32),
        hbm((4, 640, t)), hbm((1280, t)), hbm((1280, t)), hbm((1280, t)), hbm((t, 1280)), hbm((t, 2560)), hbm((t, 640)),
        hbm((3, t, 640)), hbm((2, 1280, t)),
    )
    v = pltpu.VMEM
    items = ITEMS_A_LAYER * layers
    return pl.pallas_call(
        functools.partial(backward_kernel, layers),
        out_shape=out_shape,
        in_specs=[any_] * 14 + [vmem] * 2,
        out_specs=(any_,) * 5 + (vmem,) + (any_,) * 9,
        scratch_shapes=[
            v((t, 1280), F32), v((2, t, 1280), BF16), v((t, 5120), BF16), v((t, 2560), BF16), v((t, 1280), F32),
            v((2, 64, 1280), F32), v((5120, t), BF16), v((2, 1280, t), BF16), v((2, 5, 80, t), BF16), v((2, 2, 128, t), BF16),
            v((H, 1, t), F32), v((2, 512, 1280), BF16), v((2, t, 512), BF16), v((2, 2, 640, t), BF16),
            v((XRING, 2, 4, 2, 80, 640), BF16), v((RING, 4, 2, 80, 640), BF16), v((RING, 6, 80, 640), BF16),
            v((RING, 3, 80, 640), BF16), v((RING, 80, 640), BF16),
            pltpu.SemaphoreType.DMA, pltpu.SemaphoreType.DMA((2,)), pltpu.SemaphoreType.DMA,
            pltpu.SemaphoreType.DMA((RING, 4)), pltpu.SemaphoreType.DMA((RING,)), pltpu.SemaphoreType.DMA,
            pltpu.SemaphoreType.DMA((items * 12 + 12 * layers,)),
        ],
        compiler_params=pltpu.CompilerParams(collective_id=2, has_side_effects=True, vmem_limit_bytes=63 << 20),
        name="backward_all",
    )(cotangent, *weights, *kept, vectors, masks)


def total_kernel(values, out, held, got, sent, arrived):
    a, b, core, z = place()
    to_z = [device(a, b, core, lax.rem(z + s, 4)) for s in (1, 2, 3)]
    steps = [[device(a, b, 1 - core, z)], [device(a, 1 - b, core, z)], [device(1 - a, b, core, z)], to_z]
    greet([target for step in steps for target in step])
    net = Net(sent, arrived)
    held[0] = values[...]
    place_of = 0
    for number, step in enumerate(steps):
        first = place_of
        copies = []
        for target in step:
            copies.append(net.push(held.at[number], got.at[place_of], target))
            place_of += 1
        sum_ = held[number]
        for i, copy in enumerate(copies):
            copy.wait_recv()
            sum_ = sum_ + got[first + i]
        if number < 3:
            held[number + 1] = sum_
        else:
            out[...] = sum_
    net.drain()


def total(values):
    vmem = pl.BlockSpec(memory_space=pltpu.VMEM)
    return pl.pallas_call(
        total_kernel,
        out_shape=jax.ShapeDtypeStruct(values.shape, F32),
        in_specs=[vmem], out_specs=vmem,
        scratch_shapes=[
            pltpu.VMEM((4,) + values.shape, F32), pltpu.VMEM((6,) + values.shape, F32),
            pltpu.SemaphoreType.DMA, pltpu.SemaphoreType.DMA((6,)),
        ],
        compiler_params=pltpu.CompilerParams(collective_id=3, has_side_effects=True),
        name="total",
    )(values)


def plane_shards(
    inputs, lengths, cotangent, attn_gain, attn_shift, query_weight, query_bias, key_weight,
    value_weight, value_bias, out_weight, out_bias, mlp_gain, mlp_shift, up_weight, up_bias,
    down_weight, down_bias,
):
    a, b, core, z = place()
    layers = attn_gain.shape[0]
    block = inputs.shape[1]

    def gather_tokens(values):
        return jnp.concatenate(
            [send(pick(values, (z + step) % 2), "in%d" % step) for step in range(2)], axis=0
        )

    def return_tokens(values):
        got = [send(values[step * block : (step + 1) * block], "out%d" % step) for step in range(2)]
        got = jnp.stack(got)
        return jnp.stack([pick(got, (z + clip) % 2) for clip in range(2)])

    packed = jnp.concatenate(
        [attn_gain, attn_shift, query_bias, value_bias, out_bias, mlp_gain, mlp_shift, down_bias,
         up_bias], axis=1,
    )
    pieces = jnp.stack([packed] + [send(packed, "z%d" % s) for s in (1, 2, 3)])
    pieces = jnp.stack([pick(pieces, (z + 4 - from_z) % 4) for from_z in range(4)]).astype(F32)
    vectors = []
    for layer in range(layers):
        row = [pieces[:, layer, i * 320 : (i + 1) * 320].reshape(1280) for i in range(8)]
        row.append(pieces[:, layer, 2560:].reshape(5120))
        vectors.append(tuple(row))

    state = gather_tokens(inputs).astype(F32)

    far_lengths = send(lengths, "core")
    four = jnp.where(core == 0, jnp.concatenate([lengths, far_lengths]),
                     jnp.concatenate([far_lengths, lengths]))
    length = pick(four, z)

    def positions(which):
        return jnp.concatenate(
            [(2 * which + (z + step) % 2) * block + jnp.arange(block) for step in range(2)]
        )

    def mask_of(which):
        return jnp.where(positions(which) < length, 0.0, NEGATIVE).astype(F32)[:, None]

    masks = (mask_of(core), mask_of(1 - core))

    table = jnp.zeros((layers, 24, 1280), F32)
    for layer in range(layers):
        rows = jnp.stack(vectors[layer][:8])
        wide = jnp.pad(vectors[layer][8].reshape(10, 512), ((0, 0), (0, 768)))
        table = table.at[layer, :18].set(jnp.concatenate([rows, wide]))
    attn = jnp.stack([query_weight, key_weight, value_weight, out_weight], axis=1)
    (attn, up, down, normed_t, qkv, far, lse, context_t, middles, hidden_t, slopes, active_t, states) = forward_all(
        state, attn, up_weight, down_weight, table, jnp.stack(masks)
    )
    state = states[layers]
    output = return_tokens(state.astype(BF16))

    row_mask = (positions(core) < length).astype(F32)
    grad = gather_tokens(cotangent).astype(F32) * row_mask[:, None]
    lse_mask = jnp.stack(masks)
    results = backward_all(
        grad, (attn, up, down),
        (normed_t, qkv, far, lse, context_t, middles, hidden_t, slopes, active_t.reshape(layers, 4, 2, 640, -1), states),
        table, lse_mask,
    )
    grad, down_grad, up_grad, out_grad, qkv_grad, small = results[:6]
    input_grad = return_tokens(grad.astype(BF16)).astype(F32)
    small = jnp.concatenate([small[:, :8].reshape(layers, -1), small[:, 8:18, :512].reshape(layers, -1)], axis=1)
    sums = total(small.reshape(-1, 128)).reshape(layers, -1)
    vec = pick(sums[:, :10240].reshape(layers, 8, 4, 320), z, 2)
    up_bias_grad = pick(sums[:, 10240:].reshape(layers, 4, 1280), z, 1)

    query_grad, key_grad, value_grad = [qkv_grad[:, i].astype(F32) for i in range(3)]
    out_grad, up_grad, down_grad = out_grad.astype(F32), up_grad.astype(F32), down_grad.astype(F32)
    return (
        output, input_grad, vec[:, 0], vec[:, 1], query_grad, vec[:, 2], key_grad, value_grad,
        vec[:, 3], out_grad, vec[:, 4], vec[:, 5], vec[:, 6], up_grad, up_bias_grad, down_grad,
        vec[:, 7],
    )


def pick_body(mesh):
    if mesh.shape["rep"] == 8 and mesh.shape["shard"] == 4:
        return plane_shards
    return general_shards


def solution(mesh):
    body = pick_body(mesh)
    placed = (
        P("rep", "shard", None),
        P("rep"),
        P("rep", "shard", None),
        P(None, "shard"),
        P(None, "shard"),
        P(None, "shard", None),
        P(None, "shard"),
        P(None, "shard", None),
        P(None, "shard", None),
        P(None, "shard"),
        P(None, "shard", None),
        P(None, "shard"),
        P(None, "shard"),
        P(None, "shard"),
        P(None, "shard", None),
        P(None, "shard"),
        P(None, "shard", None),
        P(None, "shard"),
    )
    return jax.shard_map(
        body,
        mesh=mesh,
        in_specs=placed,
        out_specs=(
            P("rep", "shard", None),
            P("rep", "shard", None),
            P(None, "shard"),
            P(None, "shard"),
            P(None, "shard", None),
            P(None, "shard"),
            P(None, "shard", None),
            P(None, "shard", None),
            P(None, "shard"),
            P(None, "shard", None),
            P(None, "shard"),
            P(None, "shard"),
            P(None, "shard"),
            P(None, "shard", None),
            P(None, "shard"),
            P(None, "shard", None),
            P(None, "shard"),
        ),
        check_vma=False,
    )
```

```python
import functools
import itertools
import math

import jax
import jax.numpy as jnp
from jax import lax
from jax.experimental import pallas as pl
from jax.experimental.pallas import tpu as pltpu
from jax.sharding import PartitionSpec as P

H = 16
EPSILON = 1e-05
NEGATIVE = -1e30
BF16 = jnp.bfloat16
F32 = jnp.float32
BOTH = ("rep", "shard")


def norm_affine(values, norm_gain, norm_shift):
    center = values - jnp.mean(values, axis=-1, keepdims=True)
    spread = jnp.mean(center * center, axis=-1, keepdims=True)
    return center * lax.rsqrt(spread + EPSILON) * norm_gain + norm_shift


def gelu_exact(values):
    return jax.nn.gelu(values, approximate=False)


def project(left_operand, right_operand):
    return jnp.einsum(
        "csa,ab->csb", left_operand, right_operand, preferred_element_type=jnp.float32
    )


def project_back(left_operand, right_operand):
    return jnp.einsum(
        "csb,ab->csa", left_operand, right_operand, preferred_element_type=jnp.float32
    )


def weight_grad(left_operand, right_operand):
    return jnp.einsum(
        "csa,csb->ab", left_operand, right_operand, preferred_element_type=jnp.float32
    )


def column_sum(values):
    return jnp.sum(values.astype(jnp.float32), axis=(0, 1))


def layer_slice(params, layer_index):
    return tuple((weight_array[layer_index] for weight_array in params))


def fetch_forward(local_params):
    return (
        lax.all_gather(local_params[0], "shard", axis=0, tiled=True),
        lax.all_gather(local_params[1], "shard", axis=0, tiled=True),
        lax.all_gather(local_params[2], "shard", axis=0, tiled=True),
        lax.all_gather(local_params[3], "shard", axis=0, tiled=True),
        lax.all_gather(local_params[4], "shard", axis=0, tiled=True),
        lax.all_gather(local_params[5], "shard", axis=0, tiled=True),
        lax.all_gather(local_params[6], "shard", axis=0, tiled=True),
        lax.all_gather(local_params[7], "shard", axis=0, tiled=True),
        lax.all_gather(local_params[8], "shard", axis=0, tiled=True),
        lax.all_gather(local_params[9], "shard", axis=0, tiled=True),
        lax.all_gather(local_params[10], "shard", axis=0, tiled=True),
        lax.all_gather(local_params[11], "shard", axis=0, tiled=True),
        lax.all_gather(local_params[12], "shard", axis=0, tiled=True),
        lax.all_gather(local_params[13], "shard", axis=0, tiled=True),
        lax.all_gather(local_params[14], "shard", axis=0, tiled=True),
    )


def fetch_again(local_params):
    return (
        lax.all_gather(local_params[0], "shard", axis=0, tiled=True),
        lax.all_gather(local_params[1], "shard", axis=0, tiled=True),
        lax.all_gather(local_params[2], "shard", axis=0, tiled=True),
        lax.all_gather(local_params[3], "shard", axis=0, tiled=True),
        lax.all_gather(local_params[4], "shard", axis=0, tiled=True),
        lax.all_gather(local_params[5], "shard", axis=0, tiled=True),
        lax.all_gather(local_params[6], "shard", axis=0, tiled=True),
        lax.all_gather(local_params[7], "shard", axis=0, tiled=True),
        lax.all_gather(local_params[8], "shard", axis=0, tiled=True),
        lax.all_gather(local_params[9], "shard", axis=0, tiled=True),
        lax.all_gather(local_params[10], "shard", axis=0, tiled=True),
        lax.all_gather(local_params[11], "shard", axis=0, tiled=True),
        lax.all_gather(local_params[12], "shard", axis=0, tiled=True),
        lax.all_gather(local_params[13], "shard", axis=0, tiled=True),
        lax.all_gather(local_params[14], "shard", axis=0, tiled=True),
    )


def forward_layer(hidden_state, weights, lengths):
    (
        attn_gain,
        attn_shift,
        query_weight,
        query_bias,
        key_weight,
        value_weight,
        value_bias,
        out_weight,
        out_bias,
        mlp_gain,
        mlp_shift,
        up_weight,
        up_bias,
        down_weight,
        down_bias,
    ) = weights
    clip_count, row_count, model_width = hidden_state.shape
    head_size = model_width // H
    query_scale = float(head_size) ** (-0.5)
    normed = norm_affine(
        hidden_state, attn_gain.astype(jnp.float32), attn_shift.astype(jnp.float32)
    ).astype(jnp.bfloat16)
    query_low = (
        (project(normed, query_weight) + query_bias.astype(jnp.float32)) * query_scale
    ).astype(jnp.bfloat16)
    key_low = project(normed, key_weight).astype(jnp.bfloat16)
    value_low = (project(normed, value_weight) + value_bias.astype(jnp.float32)).astype(
        jnp.bfloat16
    )
    key_all, value_all = (
        lax.all_gather(key_low, "shard", axis=1, tiled=True),
        lax.all_gather(value_low, "shard", axis=1, tiled=True),
    )
    length_all = key_all.shape[1]
    valid_keys = jnp.arange(length_all, dtype=jnp.int32)[None, :] < lengths[:, None]
    query_heads = query_low.reshape(clip_count, row_count, H, head_size)
    key_heads = key_all.reshape(clip_count, length_all, H, head_size)
    value_heads = value_all.reshape(clip_count, length_all, H, head_size)
    scores = jnp.einsum(
        "cqhd,ckhd->chqk", query_heads, key_heads, preferred_element_type=jnp.float32
    )
    scores = jnp.where(valid_keys[:, None, None, :], scores, NEGATIVE)
    attention = jax.nn.softmax(scores, axis=-1)
    attention_low = attention.astype(jnp.bfloat16)
    context = jnp.einsum(
        "chqk,ckhd->cqhd", attention_low, value_heads, preferred_element_type=jnp.float32
    )
    context_low = context.reshape(clip_count, row_count, model_width).astype(jnp.bfloat16)
    middle = hidden_state + project(context_low, out_weight) + out_bias.astype(jnp.float32)
    hidden_in = norm_affine(
        middle, mlp_gain.astype(jnp.float32), mlp_shift.astype(jnp.float32)
    ).astype(jnp.bfloat16)
    pre_gelu = project(hidden_in, up_weight) + up_bias.astype(jnp.float32)
    active_low = gelu_exact(pre_gelu).astype(jnp.bfloat16)
    result = middle + project(active_low, down_weight) + down_bias.astype(jnp.float32)
    kept_values = (
        normed,
        query_heads,
        key_heads,
        value_heads,
        attention,
        attention_low,
        context_low,
        middle,
        hidden_in,
        pre_gelu,
        active_low,
    )
    return (result, kept_values)


def backward_layer(hidden_state, grad_after, weights, lengths):
    (
        attn_gain,
        attn_shift,
        query_weight,
        query_bias,
        key_weight,
        value_weight,
        value_bias,
        out_weight,
        out_bias,
        mlp_gain,
        mlp_shift,
        up_weight,
        up_bias,
        down_weight,
        down_bias,
    ) = weights
    unused, kept_values = forward_layer(hidden_state, weights, lengths)
    (
        normed,
        query_heads,
        key_heads,
        value_heads,
        attention,
        attention_low,
        context_low,
        middle,
        hidden_in,
        pre_gelu,
        active_low,
    ) = kept_values
    clip_count, row_count, model_width = hidden_state.shape
    length_all = key_heads.shape[1]
    head_size = model_width // H
    query_scale = float(head_size) ** (-0.5)
    grad_low = grad_after.astype(jnp.bfloat16)
    grad_active = project_back(grad_low, down_weight)
    unused, gelu_pull = jax.vjp(gelu_exact, pre_gelu)
    grad_pre = gelu_pull(grad_active)[0].astype(jnp.bfloat16)
    grad_hidden = project_back(grad_pre, up_weight)
    unused, mlp_pull = jax.vjp(
        norm_affine, middle, mlp_gain.astype(jnp.float32), mlp_shift.astype(jnp.float32)
    )
    grad_middle_norm, grad_mlp_gain, grad_mlp_shift = mlp_pull(grad_hidden)
    grad_middle = grad_after + grad_middle_norm
    middle_low = grad_middle.astype(jnp.bfloat16)
    grad_context = project_back(middle_low, out_weight).astype(jnp.bfloat16)
    grad_context = grad_context.reshape(clip_count, row_count, H, head_size)
    grad_attention = jnp.einsum(
        "cqhd,ckhd->chqk", grad_context, value_heads, preferred_element_type=jnp.float32
    )
    value_part = jnp.einsum(
        "chqk,cqhd->ckhd", attention_low, grad_context, preferred_element_type=jnp.float32
    )
    grad_scores = attention * (
        grad_attention - jnp.sum(attention * grad_attention, axis=-1, keepdims=True)
    )
    scores_low = grad_scores.astype(jnp.bfloat16)
    grad_query = jnp.einsum(
        "chqk,ckhd->cqhd", scores_low, key_heads, preferred_element_type=jnp.float32
    )
    grad_query = grad_query.reshape(clip_count, row_count, model_width).astype(jnp.bfloat16)
    key_part = jnp.einsum(
        "chqk,cqhd->ckhd", scores_low, query_heads, preferred_element_type=jnp.float32
    )
    key_summed, value_summed = (
        lax.psum_scatter(
            key_part.reshape(clip_count, length_all, model_width).astype(jnp.bfloat16),
            "shard",
            scatter_dimension=1,
            tiled=True,
        ).astype(jnp.float32),
        lax.psum_scatter(
            value_part.reshape(clip_count, length_all, model_width).astype(jnp.bfloat16),
            "shard",
            scatter_dimension=1,
            tiled=True,
        ).astype(jnp.float32),
    )
    key_grad_low = key_summed.astype(jnp.bfloat16)
    value_grad_low = value_summed.astype(jnp.bfloat16)
    grad_normed = (
        project_back(grad_query, query_weight) * query_scale
        + project_back(key_grad_low, key_weight)
        + project_back(value_grad_low, value_weight)
    )
    unused, attn_pull = jax.vjp(
        norm_affine, hidden_state, attn_gain.astype(jnp.float32), attn_shift.astype(jnp.float32)
    )
    grad_input_norm, grad_attn_gain, grad_attn_shift = attn_pull(grad_normed)
    grad_before = grad_middle + grad_input_norm
    grad_down = weight_grad(active_low, grad_low)
    grad_down_bias = column_sum(grad_low)
    grad_up = weight_grad(hidden_in, grad_pre)
    grad_up_bias = column_sum(grad_pre)
    grad_out_weight = weight_grad(context_low, middle_low)
    grad_out_bias = column_sum(middle_low)
    grad_query_weight = weight_grad(normed, grad_query) * query_scale
    grad_query_bias = column_sum(grad_query) * query_scale
    grad_key_weight = weight_grad(normed, key_grad_low)
    grad_value_weight = weight_grad(normed, value_grad_low)
    grad_value_bias = column_sum(value_grad_low)
    owned_grads = (
        lax.psum_scatter(
            grad_attn_gain.astype(jnp.bfloat16), "shard", scatter_dimension=0, tiled=True
        ).astype(jnp.float32),
        lax.psum_scatter(
            grad_attn_shift.astype(jnp.bfloat16), "shard", scatter_dimension=0, tiled=True
        ).astype(jnp.float32),
        lax.psum_scatter(
            grad_query_weight.astype(jnp.bfloat16), "shard", scatter_dimension=0, tiled=True
        ).astype(jnp.float32),
        lax.psum_scatter(
            grad_query_bias.astype(jnp.bfloat16), "shard", scatter_dimension=0, tiled=True
        ).astype(jnp.float32),
        lax.psum_scatter(
            grad_key_weight.astype(jnp.bfloat16), "shard", scatter_dimension=0, tiled=True
        ).astype(jnp.float32),
        lax.psum_scatter(
            grad_value_weight.astype(jnp.bfloat16), "shard", scatter_dimension=0, tiled=True
        ).astype(jnp.float32),
        lax.psum_scatter(
            grad_value_bias.astype(jnp.bfloat16), "shard", scatter_dimension=0, tiled=True
        ).astype(jnp.float32),
        lax.psum_scatter(
            grad_out_weight.astype(jnp.bfloat16), "shard", scatter_dimension=0, tiled=True
        ).astype(jnp.float32),
        lax.psum_scatter(
            grad_out_bias.astype(jnp.bfloat16), "shard", scatter_dimension=0, tiled=True
        ).astype(jnp.float32),
        lax.psum_scatter(
            grad_mlp_gain.astype(jnp.bfloat16), "shard", scatter_dimension=0, tiled=True
        ).astype(jnp.float32),
        lax.psum_scatter(
            grad_mlp_shift.astype(jnp.bfloat16), "shard", scatter_dimension=0, tiled=True
        ).astype(jnp.float32),
        lax.psum_scatter(
            grad_up.astype(jnp.bfloat16), "shard", scatter_dimension=0, tiled=True
        ).astype(jnp.float32),
        lax.psum_scatter(
            grad_up_bias.astype(jnp.bfloat16), "shard", scatter_dimension=0, tiled=True
        ).astype(jnp.float32),
        lax.psum_scatter(
            grad_down.astype(jnp.bfloat16), "shard", scatter_dimension=0, tiled=True
        ).astype(jnp.float32),
        lax.psum_scatter(
            grad_down_bias.astype(jnp.bfloat16), "shard", scatter_dimension=0, tiled=True
        ).astype(jnp.float32),
    )
    return (grad_before, owned_grads)


def replica_layer(owned_grads):
    return (
        lax.psum(owned_grads[0].astype(jnp.bfloat16), "rep").astype(jnp.float32),
        lax.psum(owned_grads[1].astype(jnp.bfloat16), "rep").astype(jnp.float32),
        lax.psum(owned_grads[2].astype(jnp.bfloat16), "rep").astype(jnp.float32),
        lax.psum(owned_grads[3].astype(jnp.bfloat16), "rep").astype(jnp.float32),
        lax.psum(owned_grads[4].astype(jnp.bfloat16), "rep").astype(jnp.float32),
        lax.psum(owned_grads[5].astype(jnp.bfloat16), "rep").astype(jnp.float32),
        lax.psum(owned_grads[6].astype(jnp.bfloat16), "rep").astype(jnp.float32),
        lax.psum(owned_grads[7].astype(jnp.bfloat16), "rep").astype(jnp.float32),
        lax.psum(owned_grads[8].astype(jnp.bfloat16), "rep").astype(jnp.float32),
        lax.psum(owned_grads[9].astype(jnp.bfloat16), "rep").astype(jnp.float32),
        lax.psum(owned_grads[10].astype(jnp.bfloat16), "rep").astype(jnp.float32),
        lax.psum(owned_grads[11].astype(jnp.bfloat16), "rep").astype(jnp.float32),
        lax.psum(owned_grads[12].astype(jnp.bfloat16), "rep").astype(jnp.float32),
        lax.psum(owned_grads[13].astype(jnp.bfloat16), "rep").astype(jnp.float32),
        lax.psum(owned_grads[14].astype(jnp.bfloat16), "rep").astype(jnp.float32),
    )


def general_shards(
    inputs,
    lengths,
    cotangent,
    attn_gain,
    attn_shift,
    query_weight,
    query_bias,
    key_weight,
    value_weight,
    value_bias,
    out_weight,
    out_bias,
    mlp_gain,
    mlp_shift,
    up_weight,
    up_bias,
    down_weight,
    down_bias,
):
    params = (
        attn_gain,
        attn_shift,
        query_weight,
        query_bias,
        key_weight,
        value_weight,
        value_bias,
        out_weight,
        out_bias,
        mlp_gain,
        mlp_shift,
        up_weight,
        up_bias,
        down_weight,
        down_bias,
    )
    layers = attn_gain.shape[0]
    hidden_state = inputs.astype(jnp.float32)
    kept_inputs = []
    kept_weights = []
    for layer_index in range(layers):
        gathered = fetch_forward(layer_slice(params, layer_index))
        kept_inputs.append(hidden_state)
        kept_weights.append(gathered)
        hidden_state, unused = forward_layer(hidden_state, gathered, lengths)
    output = hidden_state.astype(jnp.bfloat16)
    row_count = inputs.shape[1]
    first_row = lax.axis_index("shard") * row_count
    positions = first_row + jnp.arange(row_count, dtype=jnp.int32)
    row_mask = (positions[None, :] < lengths[:, None]).astype(jnp.float32)
    grad_state = cotangent.astype(jnp.float32) * row_mask[:, :, None]
    owned_list = [None] * layers
    for layer_index in reversed(range(layers)):
        gathered = fetch_again(layer_slice(params, layer_index))
        grad_state, owned_grads = backward_layer(
            kept_inputs[layer_index], grad_state, gathered, lengths
        )
        owned_grads = replica_layer(owned_grads)
        owned_list[layer_index] = owned_grads
    stacked = tuple(
        (
            jnp.stack([owned_list[layer_index][member] for layer_index in range(layers)])
            for member in range(15)
        )
    )
    return (
        output,
        grad_state,
        stacked[0],
        stacked[1],
        stacked[2],
        stacked[3],
        stacked[4],
        stacked[5],
        stacked[6],
        stacked[7],
        stacked[8],
        stacked[9],
        stacked[10],
        stacked[11],
        stacked[12],
        stacked[13],
        stacked[14],
    )


def pick(values, index, axis=0):
    return lax.dynamic_index_in_dim(values, index, axis, keepdims=False)


def place():
    rep = lax.axis_index("rep")
    return rep // 4, (rep // 2) % 2, rep % 2, lax.axis_index("shard")


MESH = pl.DeviceIdType.MESH

def device(a, b, core, z):
    return ((a * 2 + b) * 2 + core, z)


class Net:
    def __init__(self, sent, arrived):
        self.sent, self.arrived = sent, arrived
        self.copies, self.count = [], 0
    def push(self, source, target_ref, target, sent=None):
        copy = pltpu.make_async_remote_copy(
            src_ref=source, dst_ref=target_ref, send_sem=self.sent if sent is None else sent,
            recv_sem=self.arrived.at[self.count], device_id=target, device_id_type=MESH)
        copy.start()
        self.count += 1
        if sent is None:
            self.copies.append(copy)
        return copy

    def drain(self):
        for copy in self.copies:
            copy.wait_send()

def greet(targets, regroup=None):
    barrier = pltpu.get_barrier_semaphore()

    def signal(target):
        pl.semaphore_signal(barrier, inc=1, device_id=target, device_id_type=MESH)

    for target in targets:
        signal(target)
    if regroup is None:
        pl.semaphore_wait(barrier, len(targets))
        return
    stays, to, source, both = regroup
    for step in range(2):
        for target in (source[step], to[step]) if both else (source[step],):

            @pl.when(True if step else jnp.logical_not(stays))
            def _():
                signal(target)

    extra = 2 if both else 1

    @pl.when(stays)
    def _():
        pl.semaphore_wait(barrier, len(targets) + extra)

    @pl.when(jnp.logical_not(stays))
    def _():
        pl.semaphore_wait(barrier, len(targets) + 2 * extra)


def regrouping():
    a, b, core, z = place()
    to, source = [], []
    for step in range(2):
        to.append(device(a, b, z // 2, 2 * core + lax.rem(z + step, 2)))
        source.append(device(a, b, z // 2, 2 * core + lax.rem(z + step, 2)))
    return core == z // 2, to, source


class Swap:
    def __init__(self, net, source, target_ref, target, stays, sent, local):
        self.stays = stays
        self.far = pltpu.make_async_remote_copy(
            src_ref=source, dst_ref=target_ref, send_sem=sent, recv_sem=net.arrived.at[net.count],
            device_id=target, device_id_type=MESH)
        self.near = pltpu.make_async_copy(source, target_ref, local) if stays is not None else None
        net.count += 1

    def both(self, near, far):
        if self.stays is None:
            far()
            return
        pl.when(self.stays)(near)
        pl.when(jnp.logical_not(self.stays))(far)

    def start(self):
        self.both(lambda: self.near.start(), lambda: self.far.start())
        return self

    def wait(self):
        self.both(lambda: self.near.wait(), lambda: self.far.wait())

def gather_regions(index, zs, chip, core):
    part = chip * 2 + core
    def rows(base, size):
        return pl.ds(pl.multiple_of(base, 8), size)
    if index < 2:
        return 0, (pl.ds(2 * index, 2), rows(zs * 320 + part * 40, 40), slice(None))
    if index < 4:
        return 1, (rows(zs * 320 + part * 40, 40), pl.ds((index - 2) * 2560, 2560))
    return 2, (rows(zs * 1280 + part * 160 + (index - 4) * 80, 80), slice(None))


NN = (((1,), (0,)), ((), ()))
TN = (((0,), (0,)), ((), ()))
NT = (((1,), (1,)), ((), ()))
TOKENS = 512
ROOT_HALF = math.sqrt(0.5)
ROOT_TWO_PI = math.sqrt(2.0 * math.pi)

def dot(left, right, numbers=NN):
    return lax.dot_general(left, right, numbers, preferred_element_type=F32)


def tile(i, size):
    return pl.ds(pl.multiple_of(i * size, size), size)


def stream(count, copy, body):
    copy(0, 0).start()

    @pl.loop(0, count)
    def _(i):
        slot = i % 2

        @pl.when(i + 1 < count)
        def _():
            copy(i + 1, 1 - slot).start()

        copy(i, slot).wait()
        body(i, slot)


def transpose_into(target, source, rows):
    @pl.loop(0, rows // 128)
    def _(i):
        target[tile(i, 128), :] = source[:, tile(i, 128)].T


def gather_program(net, layers, shards, outs, copies, local):
    a, b, core, z = place()
    behind = [lax.rem(z + 4 - s, 4) for s in range(4)]
    to_z = [device(a, b, core, lax.rem(z + s, 4)) for s in range(4)]
    to_a, to_b, to_core = device(1 - a, b, core, z), device(a, 1 - b, core, z), device(a, b, 1 - core, z)
    count = 6 * layers
    twin = [[] for _ in range(count)]

    def refs_at(index, zs, pa, pb, whose):
        which, at = gather_regions(index % 6, zs, pa * 2 + pb, core)
        return whose[which].at[index // 6].at[at]

    def start(index):
        if index % 6 > 1:
            return [[net.push(refs_at(index, 0, a, b, shards), refs_at(index, z, a, b, outs), to_z[s])] for s in (1, 2, 3)]
        here, there = [
            pl.ds(pl.multiple_of(zs * 320 + ((a * 2 + b) * 2 + core) * 40, 8), 40) for zs in (0, z)]
        return [
            [net.push(shards[0][i].at[index // 6, here, :], outs[0].at[index // 6, i, there, :], to_z[s])
             for i in (2 * (index % 6), 2 * (index % 6) + 1)]
            for s in (1, 2, 3)
        ]

    def on(index, s, pa, pb, target):
        ref = refs_at(index, behind[s], pa, pb, outs)
        copy = net.push(ref, ref, target)
        if target is to_core:
            twin[index].append(copy)
        return copy

    def own_copies(step):
        layer, which = step // 3, step % 3
        out = outs[which].at[layer]
        shard = shards[which].at[layer] if which else None
        ins, back = [], []
        for i in range(4):
            if which == 0:
                source, target = shards[0][i].at[layer], out.at[i, pl.ds(pl.multiple_of(z * 320, 8), 320), :]
            elif which == 1:
                source = shard.at[:, pl.ds(i * 1280, 1280)]
                target = out.at[pl.ds(pl.multiple_of(z * 320, 8), 320), pl.ds(i * 1280, 1280)]
            else:
                source = shard.at[pl.ds(i * 320, 320), :]
                target = out.at[pl.ds(pl.multiple_of(z * 1280 + i * 320, 8), 320), :]
            ins.append(pltpu.make_async_copy(source, copies.at[i], local))
            back.append(pltpu.make_async_copy(copies.at[i], target, local))
        for copy in ins:
            copy.start()
        for copy in ins:
            copy.wait()
        for copy in back:
            copy.start()
        for copy in back:
            copy.wait()

    zed, mid, diag = {}, {}, {}
    zed[0] = start(0)
    zed[1] = start(1)
    own_copies(0)
    yield twin
    for t in range(count + 2):
        if t < count:
            mid[t] = {}
            for s in (1, 2, 3):
                for copy in zed[t][s - 1]:
                    copy.wait_recv()
                mid[t][s] = (on(t, s, a, b, to_b), on(t, s, a, b, to_a))
                on(t, s, a, b, to_core)
            if t + 2 < count:
                zed[t + 2] = start(t + 2)
        if 0 <= t - 1 < count:
            k = t - 1
            diag[k] = {}
            for s in (1, 2, 3):
                via_b, via_a = mid[k][s]
                via_b.wait_recv()
                on(k, s, a, 1 - b, to_core)
                if (s + k) % 2 == 0:
                    diag[k][s] = on(k, s, a, 1 - b, to_a)
                via_a.wait_recv()
                on(k, s, 1 - a, b, to_core)
                if (s + k) % 2 == 1:
                    diag[k][s] = on(k, s, 1 - a, b, to_b)
        if 0 <= t - 2 < count:
            k = t - 2
            for s in (1, 2, 3):
                diag[k][s].wait_recv()
                on(k, s, 1 - a, 1 - b, to_core)
        if t + 1 < 3 * layers:
            own_copies(t + 1)
        yield twin


def normalize_rows(source, target, gain, shift, rows=64):
    @pl.loop(0, TOKENS // rows)
    def _(i):
        values = source[tile(i, rows), :]
        center = values - jnp.mean(values, axis=-1, keepdims=True)
        scale = lax.rsqrt(jnp.mean(center * center, axis=-1, keepdims=True) + EPSILON)
        target[tile(i, rows), :] = (center * scale * gain + shift).astype(BF16)


def attend_heads(first, last, query, key, value, far, masks, context, lse):
    @pl.loop(first, last)
    def _(h):
        at = pl.ds(pl.multiple_of(h * 80, 16), 80)
        q = query[at, :]
        s0 = dot(key[at, :], q, TN) + masks[0]
        s1 = dot(far[0, at, :], q, TN) + masks[1]
        top = jnp.maximum(jnp.max(s0, axis=0, keepdims=True), jnp.max(s1, axis=0, keepdims=True))
        e0, e1 = jnp.exp(s0 - top), jnp.exp(s1 - top)
        total = jnp.sum(e0, axis=0, keepdims=True) + jnp.sum(e1, axis=0, keepdims=True)
        out = dot(value[at, :], e0.astype(BF16)) + dot(far[1, at, :], e1.astype(BF16))
        context[at, :] = (out / total).astype(BF16)
        lse[h] = top + jnp.log(total)


def forward_kernel(layers, *refs):
    (tokens, cotangent, query_w, key_w, value_w, out_w, up, down, part, lengths,
     attn_full, up_full, down_full, keep_normed, keep_qkv, keep_far, keep_lse, keep_context, keep_middle,
     keep_hidden, keep_slope, keep_active, states, far_active, far_hidden, far_context, far_normed,
     cotangent_in, final, vectors, masks,
     state, middle, normed, normed_t, hidden_t, qkv, far, context_t, context, active, active_t, slope, lse,
     small_w, up_w, down_w, copies, product, parts_in, lengths_in,
     local, wsem, saved, swapped, handed, early, moved, stayed, sent, arrived) = refs
    a, b, core, z = place()
    to_core = device(a, b, 1 - core, z)
    to_z = [device(a, b, core, lax.rem(z + s, 4)) for s in (1, 2, 3)]
    stays, to, source = regrouping()
    greet(to_z + [device(1 - a, b, core, z), device(a, 1 - b, core, z), to_core], (stays, to, source, False))
    net = Net(sent, arrived)

    def regroup(values, targets, first):
        return [
            Swap(net, values.at[lax.rem(z + step, 2)], targets[step], to[step], None if step else stays,
                 moved.at[first + step], stayed.at[first]).start()
            for step in range(2)
        ]

    shared = [net.push(part, parts_in.at[i], to_z[i], early) for i in range(3)]
    shared.append(net.push(lengths, lengths_in, to_core, early))
    ticks = gather_program(net, layers, ((query_w, key_w, value_w, out_w), up, down), (attn_full, up_full, down_full),
                           copies, local)
    twin = next(ticks)
    clock = [-1]
    block = tokens.shape[1]
    tokens_here = regroup(tokens, [context.at[pl.ds(step * block, block), :] for step in range(2)], 0)
    next(ticks)
    next(ticks)
    clock[0] = 1
    for copy in shared:
        copy.wait()

    @pl.loop(0, layers)
    def _(i):
        total_ = part[i].astype(F32)
        for j in range(3):
            total_ = total_ + parts_in[j, i].astype(F32)
        vectors[i] = total_

    which = lax.rem(z, 2)
    length = jnp.where(z // 2 == core, lengths[which], lengths_in[which])[0:1, 0:1]
    for i in range(2):
        owner = core if i == 0 else 1 - core
        for step in range(2):
            first = (2 * owner + lax.rem(z + step, 2)) * block
            at = (lax.broadcasted_iota(jnp.int32, (block, 1), 0) + first).astype(F32)
            masks[i, step * block : (step + 1) * block, :] = jnp.where(at < length, 0.0, NEGATIVE)
    for copy in tokens_here:
        copy.wait()

    @pl.loop(0, 8)
    def _(i):
        state[tile(i, 64), :] = context[tile(i, 64), :].astype(F32)

    def pump(until):
        while clock[0] < until:
            next(ticks)
            clock[0] += 1

    def ready(*chunks):
        pump(max(chunks) + 2)
        for chunk in chunks:
            for copy in twin[chunk]:
                copy.wait_recv()

    saves = []

    def save(source, target):
        copy = pltpu.make_async_copy(source, target, saved)
        copy.start()
        saves.append(copy)

    given, taken = [], []

    def hand(source, target):
        copy = net.push(source, target, to_core, handed)
        given.append(copy)
        taken.append(copy)

    scale = float(80) ** (-0.5)
    for layer in range(layers):
        base = 6 * layer
        for copy in given:
            copy.wait_send()
        given.clear()
        vec = vectors.at[layer]

        def row(i):
            return vec[i : i + 1, :]

        weights = attn_full.at[layer]
        save(state, states.at[layer])
        normalize_rows(state, normed, row(0), row(1))
        transpose_into(normed_t, normed, 1280)
        save(normed_t, keep_normed.at[layer])
        hand(normed_t, far_normed.at[layer])
        ready(base, base + 1)

        def project(which, bias, factor, target):
            def copy(i, slot):
                return pltpu.make_async_copy(weights.at[which, :, tile(i, 256)], small_w.at[slot], wsem.at[slot])

            def body(i, slot):
                out = dot(normed[...], small_w[slot])
                if bias is not None:
                    out = out + vec[bias : bias + 1, tile(i, 256)]
                if factor != 1.0:
                    out = out * factor
                target[tile(i, 256), :] = out.astype(BF16).T

            stream(5, copy, body)

        project(1, None, 1.0, qkv.at[1])
        project(2, 3, 1.0, qkv.at[2])
        swap = net.push(qkv.at[pl.ds(1, 2)], far.at[layer], to_core, swapped)
        project(0, 2, scale, qkv.at[0])
        pump(base + 4)
        swap.wait()
        for part in range(4):
            if part == 2:
                pump(base + 5)
                if layer == layers - 1:
                    cotangent_at = [copies.at[step, pl.ds(0, block), :] for step in range(2)]
                    cotangent_here = regroup(cotangent, cotangent_at, 2)
            attend_heads(4 * part, 4 * part + 4, qkv.at[0], qkv.at[1], qkv.at[2], far.at[layer], masks, context_t, lse)
        save(qkv, keep_qkv.at[layer])
        save(far.at[layer], keep_far.at[layer])
        save(lse, keep_lse.at[layer])
        save(context_t, keep_context.at[layer])
        hand(context_t, far_context.at[layer])

        @pl.loop(0, 10)
        def _(i):
            context[:, tile(i, 128)] = context_t[tile(i, 128), :].T

        def copy_out(i, slot):
            return pltpu.make_async_copy(weights.at[3, :, tile(i, 256)], small_w.at[slot], wsem.at[slot])

        def body_out(i, slot):
            at = tile(i, 256)
            middle[:, at] = state[:, at] + dot(context[...], small_w[slot]) + vec[4:5, at]

        stream(5, copy_out, body_out)
        save(middle, keep_middle.at[layer])
        normalize_rows(middle, normed, row(5), row(6))
        transpose_into(hidden_t, normed, 1280)
        save(hidden_t, keep_hidden.at[layer])
        hand(hidden_t, far_hidden.at[layer])
        pump(base + 6)
        ready(base + 2, base + 3)

        def copy_up(i, slot):
            return pltpu.make_async_copy(up_full.at[layer, :, tile(i, 512)], up_w.at[slot], wsem.at[slot])

        def body_up(i, slot):
            at = tile(i, 512)
            product[...] = dot(normed[...], up_w[slot])
            bias = vec[pl.ds(8 + i, 1), :512]

            @pl.loop(0, 16)
            def _(j):
                u = product[tile(j, 32), :] + bias
                half = 0.5 * (1.0 + lax.erf(u * ROOT_HALF))
                active[tile(j, 32), at] = (u * half).astype(BF16)
                slope[tile(j, 32), at] = (half + u * jnp.exp(-0.5 * u * u) * (1.0 / ROOT_TWO_PI)).astype(BF16)

            active_t[at, :] = active[:, at].T

        stream(10, copy_up, body_up)
        save(slope, keep_slope.at[layer])
        save(active_t, keep_active.at[layer])
        for i in range(4):
            rows = pl.ds(pl.multiple_of(i * 1280 + (1 - core) * 640, 128), 640)
            hand(active_t.at[rows, :], far_active.at[layer, i])
        ready(base + 4, base + 5)

        def copy_down(i, slot):
            return pltpu.make_async_copy(down_full.at[layer, :, tile(i, 256)], down_w.at[slot], wsem.at[slot])

        for copy in saves:
            copy.wait()
        saves.clear()

        def body_down(i, slot):
            at = tile(i, 256)
            state[:, at] = middle[:, at] + dot(active[...], down_w[slot]) + vec[7:8, at]

        stream(5, copy_down, body_down)

    @pl.loop(0, 8)
    def _(i):
        normed[tile(i, 64), :] = state[tile(i, 64), :].astype(BF16)

    for copy in cotangent_here:
        copy.wait()
    save(normed, final)
    for step in range(2):
        save(cotangent_at[step], cotangent_in.at[step])
    for copy in saves:
        copy.wait()
    for copy in given:
        copy.wait_send()
    for copy in taken:
        copy.wait_recv()
    net.drain()


def forward_all(tokens, cotangent, shards, part, lengths):
    any_ = pl.BlockSpec(memory_space=pl.ANY)
    vmem = pl.BlockSpec(memory_space=pltpu.VMEM)
    layers = part.shape[0]
    t = TOKENS

    def hbm(shape, dtype=BF16):
        return jax.ShapeDtypeStruct((layers,) + shape, dtype)

    out_shape = (
        hbm((4, 1280, 1280)), hbm((1280, 5120)), hbm((5120, 1280)),
        hbm((1280, t)), hbm((3, 1280, t)), hbm((2, 1280, t)), hbm((H, 1, t), F32), hbm((1280, t)), hbm((t, 1280), F32),
        hbm((1280, t)), hbm((t, 5120)), hbm((5120, t)), hbm((t, 1280), F32),
        hbm((4, 640, t)), hbm((1280, t)), hbm((1280, t)), hbm((1280, t)),
        jax.ShapeDtypeStruct(tokens.shape, BF16), jax.ShapeDtypeStruct((t, 1280), BF16), hbm((24, 1280), F32), jax.ShapeDtypeStruct((2, t, 1), F32),
    )
    v = pltpu.VMEM
    return pl.pallas_call(
        functools.partial(forward_kernel, layers),
        out_shape=out_shape,
        in_specs=[any_] * 8 + [vmem] * 2,
        out_specs=(any_,) * (len(out_shape) - 2) + (vmem,) * 2,
        scratch_shapes=[
            v((t, 1280), F32), v((t, 1280), F32), v((t, 1280), BF16), v((1280, t), BF16), v((1280, t), BF16),
            v((3, 1280, t), BF16), v((layers, 2, 1280, t), BF16), v((1280, t), BF16), v((t, 1280), BF16),
            v((t, 5120), BF16), v((5120, t), BF16), v((t, 5120), BF16), v((H, 1, t), F32),
            v((2, 1280, 256), BF16), v((2, 1280, 512), BF16), v((2, 5120, 256), BF16), v((4, 320, 1280), BF16),
            v((t, 512), F32), v((3,) + part.shape, BF16), v(lengths.shape, F32),
            pltpu.SemaphoreType.DMA, pltpu.SemaphoreType.DMA((2,)), pltpu.SemaphoreType.DMA,
            pltpu.SemaphoreType.DMA, pltpu.SemaphoreType.DMA, pltpu.SemaphoreType.DMA,
            pltpu.SemaphoreType.DMA((4,)), pltpu.SemaphoreType.DMA((4,)), pltpu.SemaphoreType.DMA,
            pltpu.SemaphoreType.DMA((6 * layers * 24 + 14 * layers + 8,)),
        ],
        compiler_params=pltpu.CompilerParams(collective_id=1, has_side_effects=True, vmem_limit_bytes=63 << 20),
        name="forward_all",
    )(tokens, cotangent, *shards, part, lengths)


def add(*parts):
    total = parts[0].astype(F32)
    for part in parts[1:]:
        total = total + part.astype(F32)
    return total.astype(BF16)


ITEMS_A_LAYER = 12
RING, XRING = 10, 4
ORDERS = ("azb", "baz", "abz", "bza", "azb", "baz", "abz", "bza", "azb", "baz", "abz", "bza")
PLAN = (
    -1, -1, -1, -1, -1, 0, 1, -1, 2, 3, -1, 0, 1, -1, -1, 4, 5, 2, 3, -1, -1, -1, 6, 7, 4, 5, 0, 1, -1, 2, 6,
    3, -1, 4, -1, 8, 7, 0, 1, 2, -1, 5, 3, 4, 0, 1, 2, -1, -1, 6, 7, 0, 1, 2, -1, -1, 9, 10, 8, 5, 3, 4, -1,
    -2, 3, 4, 9, 5, 11, 5, -1, 6, 7, -1, 10, -1, 12, 11, 8, 9, 13, 14, 10, -1, -2, 11, 15, 12, 13, 6, 7, 8, 6,
    7, 9, -1, -1, 16, 14, 15, 10, -1, -1, -2, -3, 17, -1, 18, 12, 13, 11, 8, 9, -1, -3, 16, 8, 9, -1, -3, 19,
    20, 14, 15, 10, -1, -2, -3, 17, 18, 12, 10, -1, -3, 16, 13, 14, 11, -1, 19, 15, 16, 12, 13, 14, 11, -1,
    12, -1, -2, 13, 14, -1, -4, 20, 17, 21, 22, 15, 16, 15, -4, 16, 18, 19, 21, 23, 20, 17, 21, -4, 17, 17,
    22, 18, 19, 20, 21, 18, -4, 19, 23, 20, 21, 18, 19, 20, 21, 22, 23, 22, 23, 22, 23, 22, -4, 23
)


def streams(count, copies, body):
    for copy in copies(0, 0):
        copy.start()

    @pl.loop(0, count)
    def _(i):
        slot = i % 2

        @pl.when(i + 1 < count)
        def _():
            for copy in copies(i + 1, 1 - slot):
                copy.start()

        for copy in copies(i, slot):
            copy.wait()
        body(i, slot)


def add_blocks(blocks, target, parts):
    @pl.loop(0, blocks * 5)
    def _(i):
        block = i // 5
        at = pl.ds(pl.multiple_of((i % 5) * 16, 16), 16)
        refs = [part(block) for part in parts]
        sums = refs[0][at, :].astype(F32)
        for ref in refs[1:]:
            sums = sums + ref[at, :].astype(F32)
        target(block)[at, :] = sums.astype(BF16)


def backward_kernel(layers, *refs):
    (cotangent, final, attn_full, up_full, down_full, normed_t, qkv, far, lse_all, context_t, middles, hidden_t, slopes,
     active_t, states, active_far, hidden_far, context_far, normed_far, vectors, masks,
     output, grad_out, down_out, up_out, out_out, qkv_out, sums,
     grad_f_far, grad_pre_far, grad_o_far, grad_far, grad_kv_far,
     g, low, gp, gs, gh, rows_in, big, dfar, heads_in, far_in, lse, wide_w, slope_in, left_in,
     xs, got1s, got2s, got3s, finals, sums_held, sums_in,
     local, lsem, swapped, swapped_half, item_sent, item_local, sums_sent, moved, stayed,
     sent, arrived) = refs
    a, b, core, z = place()
    to_z = [device(a, b, core, lax.rem(z + s, 4)) for s in range(4)]
    to_a, to_b, to_core = device(1 - a, b, core, z), device(a, 1 - b, core, z), device(a, b, 1 - core, z)
    stays, to, source = regrouping()
    greet(to_z[1:] + [to_a, to_b, to_core], (stays, to, source, False))
    net = Net(sent, arrived)
    scale = float(80) ** (-0.5)
    side = {"a": (a, to_a), "b": (b, to_b)}

    def program(number, order, spot):
        slot = number % RING
        x, got1, got2, got3, final = (
            xs.at[number % XRING], got1s.at[slot], got2s.at[slot], got3s.at[slot], finals.at[slot])
        target = side[order[0]][1]
        other, other_target = side["b" if order[0] == "a" else "a"]

        def push(source, target_ref, target, stage):
            return net.push(source, target_ref, target, item_sent.at[slot, stage])

        first = push(x.at[1], got1, target, 0)
        yield
        first.wait()
        add_blocks(8, lambda i: got1.at[i // 2, i % 2],
                   [lambda i: got1.at[i // 2, i % 2], lambda i: x.at[0, i // 2, i % 2]])
        if order[1] == "z":
            nexts = [push(got1.at[lax.rem(z + s, 4)], got2.at[pl.ds(2 * s - 2, 2)], to_z[s], 1) for s in (1, 2, 3)]
        else:
            nexts = [push(got1.at[:, 1 - other], got2.at[pl.ds(0, 4)], other_target, 1)]
        yield
        for copy in nexts:
            copy.wait()
        if order[1] == "z":
            add_blocks(2, lambda i: got1.at[z, i],
                       [lambda i: got1.at[z, i]] + [lambda i, s=s: got2.at[2 * s + i] for s in range(3)])
            nexts = [push(got1.at[z, 1 - other], got3.at[0], other_target, 2)]
        else:
            add_blocks(4, lambda i: got2.at[i], [lambda i: got2.at[i], lambda i: got1.at[i, other]])
            nexts = [push(got2.at[lax.rem(z + s, 4)], got3.at[s - 1], to_z[s], 2) for s in (1, 2, 3)]
        yield
        for copy in nexts:
            copy.wait()
        if order[1] == "z":
            add_blocks(1, lambda i: final, [lambda i: got1.at[z, other], lambda i: got3.at[0]])
        else:
            add_blocks(1, lambda i: final, [lambda i: got2.at[z]] + [lambda i, s=s: got3.at[s] for s in range(3)])
        mine = pltpu.make_async_copy(final, spot(core, a, b), item_local.at[slot])
        mine.start()
        via = [push(final, spot(core, a, b), target, 3) for target in (to_a, to_b, to_core)]
        yield
        mine.wait()
        for copy in via:
            copy.wait()

        def on(pa, pb, target):
            return net.push(spot(core, pa, pb), spot(core, pa, pb), target)

        diag = on(1 - a, b, to_b) if number % 2 == 0 else on(a, 1 - b, to_a)
        twin = [on(1 - a, b, to_core), on(a, 1 - b, to_core)]
        yield
        diag.wait_recv()
        twin.append(on(1 - a, 1 - b, to_core))
        yield
        for copy in twin:
            copy.wait_recv()
        yield

    programs, stage = [], []

    def advance(number):
        next(programs[number])
        stage[number] += 1

    def send_item(order, spot):
        number = len(programs)
        assert all(s > 4 for s in stage[: max(0, number + 1 - RING)])
        programs.append(program(number, order, spot))
        stage.append(0)
        advance(number)

    def weight_gradient(height, own, far_, parts):
        base = len(programs)
        count = sum(len(part[3]) for part in parts)
        assert all(s > 1 for s in stage[: max(0, base + count - XRING)])

        def copies(i, slot):
            return [
                pltpu.make_async_copy(own(i), left_in.at[slot, 0, pl.ds(0, height), :], lsem.at[slot]),
                pltpu.make_async_copy(far_(i), left_in.at[slot, 1, pl.ds(0, height), :], lsem.at[slot]),
            ]

        def body(i, slot):
            for right, far_right, factor, targets in parts:
                out = dot(left_in[slot, 0, :height, :], right()) + dot(left_in[slot, 1, :height, :], far_right())
                if factor != 1.0:
                    out = out * factor
                out = out.astype(BF16)
                for item, order, first in targets:
                    x = xs.at[(base + item) % XRING]
                    for pa in range(2):
                        for pb in range(2):
                            row = (pa * 2 + pb) * (height // 4) + first
                            block = out[row : row + 80, :]
                            if order[0] == "a":
                                x[lax.rem(pa + a, 2), i, pb] = block
                            else:
                                x[lax.rem(pb + b, 2), i, pa] = block

        streams(4, copies, body)

    def fetch(*pairs):
        copies = [pltpu.make_async_copy(x, y, local) for x, y in pairs]
        for copy in copies:
            copy.start()
        for copy in copies:
            copy.wait()

    def norm_back(source, gain, gain_at, layer, lowered):
        def copies(i, slot):
            return [pltpu.make_async_copy(source.at[tile(i, 64), :], rows_in.at[slot], lsem.at[slot])]

        def body(i, slot):
            at = tile(i, 64)
            values = rows_in[slot]
            center = values - jnp.mean(values, axis=-1, keepdims=True)
            s = lax.rsqrt(jnp.mean(center * center, axis=-1, keepdims=True) + EPSILON)
            unit = center * s
            grad = gh[at, :]
            e = grad * gain
            out = g[at, :] + s * (
                e - jnp.mean(e, axis=-1, keepdims=True) - unit * jnp.mean(e * unit, axis=-1, keepdims=True))
            g[at, :] = out
            sums[layer, pl.ds(gain_at, 1), :] += jnp.sum(grad * unit, axis=0, keepdims=True)
            sums[layer, pl.ds(gain_at + 1, 1), :] += jnp.sum(grad, axis=0, keepdims=True)
            small = out.astype(BF16)
            if lowered or layer == 0:
                low[0, at, :] = small
            if lowered:
                sums[layer, pl.ds(4, 1), :] += jnp.sum(small.astype(F32), axis=0, keepdims=True)

        streams(8, copies, body)

    block = cotangent.shape[1]

    def give_back(values, target, first):
        return [
            Swap(net, values.at[pl.ds(step * block, block), :], target.at[lax.rem(z, 2)], to[step], None if step else stays,
                 moved.at[first + step], stayed.at[first]).start()
            for step in range(2)
        ]

    held = gs.at[:, pl.ds(0, 1280)]
    fetch((final, held))
    returned = give_back(held, output, 0)
    fetch(*[(cotangent.at[step], low.at[0, pl.ds(step * block, block), :]) for step in range(2)])

    @pl.loop(0, 8)
    def _(i):
        at = tile(i, 64)
        g[at, :] = jnp.where(masks[0, at, :] == 0.0, low[0, at, :].astype(F32), 0.0)

    sums[...] = jnp.zeros_like(sums)

    def sum_program(which, layer, first, size):
        rows = pl.ds(first, size)
        steps = [[to_core], [to_b], [to_a], to_z[1:]]
        sums_held[layer, 0, rows, :] = sums[layer, rows, :]
        place_in = 0
        for number, targets in enumerate(steps):
            copies = [
                net.push(sums_held.at[layer, number, rows], sums_in.at[layer, place_in + i, rows], target,
                         sums_sent.at[which, number])
                for i, target in enumerate(targets)
            ]
            yield
            for copy in copies:
                copy.wait()
            all_ = sums_held[layer, number, rows, :]
            for i in range(len(targets)):
                all_ = all_ + sums_in[layer, place_in + i, rows, :]
            place_in += len(targets)
            if number < 3:
                sums_held[layer, number + 1, rows, :] = all_
            else:
                sums[layer, rows, :] = all_
        yield

    def work(layer):
        vec = vectors.at[layer]
        first_item = ITEMS_A_LAYER * (layers - 1 - layer)

        def order_of(item):
            return ORDERS[item]

        @pl.loop(0, 8)
        def _(i):
            at = tile(i, 64)
            small = g[at, :].astype(BF16)
            low[0, at, :] = small
            sums[layer, pl.ds(7, 1), :] += jnp.sum(small.astype(F32), axis=0, keepdims=True)

        swap = net.push(low.at[0], grad_f_far.at[layer], to_core, swapped)
        yield
        swap.wait()
        fetch((grad_f_far.at[layer], low.at[1]))

        def down_spot(half, column):
            def spot(pc, pa, pb):
                row = pc * 640 + (pa * 2 + pb) * 160 + half * 80
                return down_out.at[layer, pl.ds(pl.multiple_of(row, 16), 80), pl.ds(column * 640, 640)]
            return spot

        for column in range(2):
            orders = [order_of(2 * column), order_of(2 * column + 1)]
            weight_gradient(
                640, lambda i: active_t.at[layer, i, core], lambda i: active_far.at[layer, i],
                [(lambda column=column: low[0, :, column * 640 : column * 640 + 640],
                  lambda column=column: low[1, :, column * 640 : column * 640 + 640], 1.0,
                  [(0, orders[0], 0), (1, orders[1], 80)])],
            )
            send_item(orders[0], down_spot(0, column))
            send_item(orders[1], down_spot(1, column))
            yield

        def unit_of(i):
            return lax.rem(i + 5 * (1 - core), 10)

        def copies_down(i, slot):
            at = tile(unit_of(i), 512)
            return [
                pltpu.make_async_copy(down_full.at[layer, at, :], wide_w.at[slot], lsem.at[slot]),
                pltpu.make_async_copy(slopes.at[layer, :, at], slope_in.at[slot], lsem.at[slot]),
            ]

        def body_down(i, slot):
            unit = unit_of(i)
            at = tile(unit, 512)
            gh[:, :512] = dot(low[0], wide_w[slot], NT)

            @pl.loop(0, 8)
            def _(j):
                rows = tile(j, 64)
                small = (gh[rows, :512] * slope_in[slot, rows, :].astype(F32)).astype(BF16)
                gp[rows, at] = small
                sums[layer, pl.ds(8 + unit, 1), :512] += jnp.sum(small.astype(F32), axis=0, keepdims=True)

        streams(5, copies_down, body_down)
        swap = net.push(gp.at[:, pl.ds(pl.multiple_of((1 - core) * 2560, 128), 2560)], grad_pre_far.at[layer], to_core,
                        swapped)
        yield
        streams(5, lambda i, slot: copies_down(i + 5, slot), lambda i, slot: body_down(i + 5, slot))
        yield
        swap.wait()
        while layer == layers - 1 and returned:
            returned.pop().wait()
        fetch((grad_pre_far.at[layer], gs))

        def up_spot(unit):
            def spot(pc, pa, pb):
                return up_out.at[layer, pl.ds(pl.multiple_of((pa * 2 + pb) * 80, 16), 80),
                                 pl.ds(pl.multiple_of(pc * 2560 + unit * 640, 128), 640)]
            return spot

        def rows_of(values, i):
            return values.at[layer, pl.ds(pl.multiple_of(i * 320, 16), 320), :]

        for pair in range(2):
            orders = [order_of(4 + 2 * pair), order_of(5 + 2 * pair)]
            weight_gradient(
                320, lambda i: rows_of(hidden_t, i), lambda i: rows_of(hidden_far, i),
                [(lambda unit=unit: gp[:, pl.ds(pl.multiple_of(core * 2560 + unit * 640, 128), 640)],
                  lambda unit=unit: gs[:, unit * 640 : unit * 640 + 640], 1.0,
                  [(unit % 2, orders[unit % 2], 0)]) for unit in (2 * pair, 2 * pair + 1)],
            )
            send_item(orders[0], up_spot(2 * pair))
            send_item(orders[1], up_spot(2 * pair + 1))
            yield

        def copies_up(i, slot):
            return [
                pltpu.make_async_copy(up_full.at[layer, tile(i, 256), pl.ds(k * 512, 512)],
                                      big.at[pl.ds(pl.multiple_of(slot * 2560 + k * 256, 256), 256), :], lsem.at[slot])
                for k in range(10)
            ]

        def body_up(i, slot):
            total_ = None
            for k in range(10):
                part = dot(gp[:, k * 512 : k * 512 + 512],
                           big[pl.ds(pl.multiple_of(slot * 2560 + k * 256, 256), 256), :], NT)
                total_ = part if total_ is None else total_ + part
            gh[:, tile(i, 256)] = total_

        streams(5, copies_up, body_up)
        yield
        norm_back(middles.at[layer], vec[5:6, :], 5, layer, True)
        swap = net.push(low.at[0, :, pl.ds(pl.multiple_of((1 - core) * 640, 128), 640)], grad_o_far.at[layer], to_core,
                        swapped)
        yield

        def copies_out(i, slot):
            return [pltpu.make_async_copy(attn_full.at[layer, 3, tile(i, 256), :], wide_w.at[slot, pl.ds(0, 256), :],
                                          lsem.at[slot])]

        def body_out(i, slot):
            big[pl.ds(pl.multiple_of(3840 + i * 256, 256), 256), :] = dot(
                wide_w[slot, :256, :], low[0], NT).astype(BF16)

        streams(5, copies_out, body_out)
        swap.wait()
        fetch((grad_o_far.at[layer], low.at[1, :, pl.ds(0, 640)]), (lse_all.at[layer], lse))

        def small_spot(whole):
            def spot(pc, pa, pb):
                return whole.at[pl.ds(pl.multiple_of((pa * 2 + pb) * 80, 16), 80),
                                pl.ds(pl.multiple_of(pc * 640, 128), 640)]
            return spot

        weight_gradient(
            320, lambda i: rows_of(context_t, i), lambda i: rows_of(context_far, i),
            [(lambda: low[0, :, pl.ds(pl.multiple_of(core * 640, 128), 640)], lambda: low[1, :, :640], 1.0,
              [(0, order_of(8), 0)])],
        )
        send_item(order_of(8), small_spot(out_out.at[layer]))
        yield

        def copies_head(h, slot):
            at = pl.ds(pl.multiple_of(h * 80, 16), 80)
            return [
                pltpu.make_async_copy(qkv.at[layer, :, at, :], heads_in.at[slot, pl.ds(0, 3)], lsem.at[slot]),
                pltpu.make_async_copy(far.at[layer, :, at, :], heads_in.at[slot, pl.ds(3, 2)], lsem.at[slot]),
            ]

        def body_head(h, slot):
            at = pl.ds(pl.multiple_of(h * 80, 16), 80)
            at_k = pl.ds(pl.multiple_of(1280 + h * 80, 16), 80)
            at_v = pl.ds(pl.multiple_of(2560 + h * 80, 16), 80)
            query, norm = heads_in[slot, 0], lse[h]
            grad = big[pl.ds(pl.multiple_of(3840 + h * 80, 16), 80), :]
            halves, delta = [], None
            for k, v, mask, target in ((1, 2, 0, big.at[at_v, :]), (3, 4, 1, dfar.at[1, at, :])):
                p = jnp.exp(dot(heads_in[slot, k], query, TN) + masks[mask] - norm)
                dp = dot(heads_in[slot, v], grad, TN)
                part = jnp.sum(p * dp, axis=0, keepdims=True)
                delta = part if delta is None else delta + part
                target[...] = dot(grad, p.astype(BF16), NT).astype(BF16)
                halves.append((p, dp))
            total_ = None
            for (p, dp), k, target in zip(halves, (1, 3), (big.at[at_k, :], dfar.at[0, at, :])):
                ds = (p * (dp - delta)).astype(BF16)
                part = dot(heads_in[slot, k], ds)
                total_ = part if total_ is None else total_ + part
                target[...] = dot(query, ds, NT).astype(BF16)
            big[at, :] = total_.astype(BF16)

        swap = []
        for part in range(4):
            streams(4, lambda i, slot: copies_head(i + 4 * part, slot), lambda i, slot: body_head(i + 4 * part, slot))
            if part % 2 == 1:
                rows = pl.ds(320 * (2 * (part // 2)), 640)
                swap.append(net.push(dfar.at[:, rows, :], grad_kv_far.at[layer, :, rows, :], to_core,
                                     swapped_half.at[part // 2]))
            yield
        for copy in swap:
            copy.wait()

        def copies_far(i, slot):
            return [pltpu.make_async_copy(grad_kv_far.at[layer, :, tile(i, 128), :], far_in.at[slot], lsem.at[slot])]

        def body_far(i, slot):
            at = tile(i, 128)
            query = big[at, :].T
            gp[:, at] = query
            sums[layer, 20:21, at] = jnp.sum(query.astype(F32), axis=0, keepdims=True) * scale
            for which in range(2):
                rows = pl.ds(pl.multiple_of(1280 + which * 1280 + i * 128, 128), 128)
                both = (big[rows, :].astype(F32) + far_in[slot, which].astype(F32)).astype(BF16).T
                gp[:, pl.ds(pl.multiple_of(1280 + which * 1280 + i * 128, 128), 128)] = both
                if which == 1:
                    sums[layer, 21:22, at] = jnp.sum(both.astype(F32), axis=0, keepdims=True)

        streams(10, copies_far, body_far)
        swap = [
            net.push(gp.at[:, pl.ds(pl.multiple_of(t * 1280 + (1 - core) * 640, 128), 640)], grad_far.at[layer, t],
                     to_core, swapped)
            for t in range(3)
        ]
        yield

        def copies_back(i, slot):
            return [pltpu.make_async_copy(attn_full.at[layer, i // 5, tile(i % 5, 256), :],
                                          wide_w.at[slot, pl.ds(0, 256), :], lsem.at[slot])]

        def body_back(i, slot):
            at = tile(i % 5, 256)
            out = dot(gp[:, pl.ds(pl.multiple_of((i // 5) * 1280, 128), 1280)], wide_w[slot, :256, :], NT)

            @pl.when(i < 5)
            def _():
                gh[:, at] = out * scale

            @pl.when(i >= 5)
            def _():
                gh[:, at] += out

        streams(5, copies_back, body_back)
        for copy in swap:
            copy.wait()
        fetch(*[(grad_far.at[layer, t], gs.at[:, pl.ds(t * 640, 640)]) for t in range(3)])
        for group in ((0, 1), (2,)):
            weight_gradient(
                320, lambda i: rows_of(normed_t, i), lambda i: rows_of(normed_far, i),
                [(lambda t=t: gp[:, pl.ds(pl.multiple_of(t * 1280 + core * 640, 128), 640)],
                  lambda t=t: gs[:, t * 640 : t * 640 + 640], scale if t == 0 else 1.0,
                  [(t % 2, order_of(9 + t), 0)]) for t in group],
            )
            for t in group:
                send_item(order_of(9 + t), small_spot(qkv_out.at[layer, t]))
            yield
        streams(10, lambda i, slot: copies_back(i + 5, slot), lambda i, slot: body_back(i + 5, slot))
        yield
        norm_back(states.at[layer], vec[0:1, :], 18, layer, False)
        if layer == 0:
            returned.extend(give_back(low.at[0], grad_out, 2))
        yield

    sum_programs = [sum_program(0, 1, 0, 24), sum_program(1, 0, 0, 16), sum_program(2, 0, 16, 8)]
    segments = itertools.chain.from_iterable(work(layer) for layer in reversed(range(layers)))
    for action in PLAN:
        if action == -1:
            next(segments)
        elif action < 0:
            next(sum_programs[-2 - action])
        else:
            advance(action)
    for copy in returned:
        copy.wait()
    assert next(segments, None) is None and all(s == 7 for s in stage)
    net.drain()


def backward_all(cotangent, final, weights, kept, vectors, masks):
    any_ = pl.BlockSpec(memory_space=pl.ANY)
    vmem = pl.BlockSpec(memory_space=pltpu.VMEM)
    layers = vectors.shape[0]
    t = TOKENS

    def hbm(shape, dtype=BF16):
        return jax.ShapeDtypeStruct((layers,) + shape, dtype)

    out_shape = (
        jax.ShapeDtypeStruct(cotangent.shape, BF16), jax.ShapeDtypeStruct(cotangent.shape, BF16),
        hbm((1280, 1280)), hbm((320, 5120)), hbm((320, 1280)), hbm((3, 320, 1280)),
        hbm((24, 1280), F32),
        hbm((t, 1280)), hbm((t, 2560)), hbm((t, 640)), hbm((3, t, 640)), hbm((2, 1280, t)),
    )
    v = pltpu.VMEM
    items = ITEMS_A_LAYER * layers
    return pl.pallas_call(
        functools.partial(backward_kernel, layers),
        out_shape=out_shape,
        in_specs=[any_] * 19 + [vmem] * 2,
        out_specs=(any_,) * 6 + (vmem,) + (any_,) * 5,
        scratch_shapes=[
            v((t, 1280), F32), v((2, t, 1280), BF16), v((t, 5120), BF16), v((t, 2560), BF16), v((t, 1280), F32),
            v((2, 64, 1280), F32), v((5120, t), BF16), v((2, 1280, t), BF16), v((2, 5, 80, t), BF16), v((2, 2, 128, t), BF16),
            v((H, 1, t), F32), v((2, 512, 1280), BF16), v((2, t, 512), BF16), v((2, 2, 640, t), BF16),
            v((XRING, 2, 4, 2, 80, 640), BF16), v((RING, 4, 2, 80, 640), BF16), v((RING, 6, 80, 640), BF16),
            v((RING, 3, 80, 640), BF16), v((RING, 80, 640), BF16),
            v((layers, 4, 24, 1280), F32), v((layers, 6, 24, 1280), F32),
            pltpu.SemaphoreType.DMA, pltpu.SemaphoreType.DMA((2,)), pltpu.SemaphoreType.DMA,
            pltpu.SemaphoreType.DMA((2,)),
            pltpu.SemaphoreType.DMA((RING, 4)), pltpu.SemaphoreType.DMA((RING,)), pltpu.SemaphoreType.DMA((3, 4)),
            pltpu.SemaphoreType.DMA((4,)), pltpu.SemaphoreType.DMA((4,)), pltpu.SemaphoreType.DMA,
            pltpu.SemaphoreType.DMA((items * 12 + 16 * layers + 8,)),
        ],
        compiler_params=pltpu.CompilerParams(collective_id=2, has_side_effects=True, vmem_limit_bytes=63 << 20),
        name="backward_all",
    )(cotangent, final, *weights, *kept, vectors, masks)


def plane_shards(
    inputs, lengths, cotangent, attn_gain, attn_shift, query_weight, query_bias, key_weight,
    value_weight, value_bias, out_weight, out_bias, mlp_gain, mlp_shift, up_weight, up_bias,
    down_weight, down_bias,
):
    z = lax.axis_index("shard")
    layers = attn_gain.shape[0]
    rows = jnp.stack([attn_gain, attn_shift, query_bias, value_bias, out_bias, mlp_gain, mlp_shift, down_bias], axis=1)
    part = jnp.zeros((layers, 24, 1280), BF16)
    part = lax.dynamic_update_slice(part, rows, (0, 0, z * 320))
    wide = lax.dynamic_update_slice(jnp.zeros((layers, 5120), BF16), up_bias, (0, z * 1280)).reshape(layers, 10, 512)
    part = lax.dynamic_update_slice(part, wide, (0, 8, 0))
    spread = jnp.broadcast_to(lengths.astype(F32)[:, None, None], (2, 8, 128))
    results = forward_all(
        inputs, cotangent, (query_weight, key_weight, value_weight, out_weight, up_weight, down_weight), part, spread
    )
    weights, kept = results[:3], list(results[3:17])
    cotangent, final, table, masks = results[17:]
    kept[8] = kept[8].reshape(layers, 4, 2, 640, -1)
    output, grad, down_grad, up_grad, out_grad, qkv_grad, small = backward_all(
        cotangent, final, weights, kept, table, masks
    )[:7]
    input_grad = grad.astype(F32)
    small_rows = jnp.concatenate([small[:, 18:22], small[:, 4:8]], axis=1)
    sums = jnp.concatenate([small_rows.reshape(layers, -1), small[:, 8:18, :512].reshape(layers, -1)], axis=1)
    vec = pick(sums[:, :10240].reshape(layers, 8, 4, 320), z, 2)
    up_bias_grad = pick(sums[:, 10240:].reshape(layers, 4, 1280), z, 1)

    query_grad, key_grad, value_grad = [qkv_grad[:, i].astype(F32) for i in range(3)]
    out_grad, up_grad, down_grad = out_grad.astype(F32), up_grad.astype(F32), down_grad.astype(F32)
    return (
        output, input_grad, vec[:, 0], vec[:, 1], query_grad, vec[:, 2], key_grad, value_grad,
        vec[:, 3], out_grad, vec[:, 4], vec[:, 5], vec[:, 6], up_grad, up_bias_grad, down_grad,
        vec[:, 7],
    )


def pick_body(mesh):
    if mesh.shape["rep"] == 8 and mesh.shape["shard"] == 4:
        return plane_shards
    return general_shards


def solution(mesh):
    body = pick_body(mesh)
    placed = (
        P("rep", "shard", None),
        P("rep"),
        P("rep", "shard", None),
        P(None, "shard"),
        P(None, "shard"),
        P(None, "shard", None),
        P(None, "shard"),
        P(None, "shard", None),
        P(None, "shard", None),
        P(None, "shard"),
        P(None, "shard", None),
        P(None, "shard"),
        P(None, "shard"),
        P(None, "shard"),
        P(None, "shard", None),
        P(None, "shard"),
        P(None, "shard", None),
        P(None, "shard"),
    )
    return jax.shard_map(
        body,
        mesh=mesh,
        in_specs=placed,
        out_specs=(
            P("rep", "shard", None),
            P("rep", "shard", None),
            P(None, "shard"),
            P(None, "shard"),
            P(None, "shard", None),
            P(None, "shard"),
            P(None, "shard", None),
            P(None, "shard", None),
            P(None, "shard"),
            P(None, "shard", None),
            P(None, "shard"),
            P(None, "shard"),
            P(None, "shard"),
            P(None, "shard", None),
            P(None, "shard"),
            P(None, "shard", None),
            P(None, "shard"),
        ),
        check_vma=False,
    )
```

```python
import functools
import itertools
import math

import jax
import jax.numpy as jnp
from jax import lax
from jax.experimental import pallas as pl
from jax.experimental.pallas import tpu as pltpu
from jax.sharding import PartitionSpec as P

H = 16
EPSILON = 1e-05
NEGATIVE = -1e30
BF16 = jnp.bfloat16
F32 = jnp.float32
BOTH = ("rep", "shard")


def norm_affine(values, norm_gain, norm_shift):
    center = values - jnp.mean(values, axis=-1, keepdims=True)
    spread = jnp.mean(center * center, axis=-1, keepdims=True)
    return center * lax.rsqrt(spread + EPSILON) * norm_gain + norm_shift


def gelu_exact(values):
    return jax.nn.gelu(values, approximate=False)


def project(left_operand, right_operand):
    return jnp.einsum(
        "csa,ab->csb", left_operand, right_operand, preferred_element_type=jnp.float32
    )


def project_back(left_operand, right_operand):
    return jnp.einsum(
        "csb,ab->csa", left_operand, right_operand, preferred_element_type=jnp.float32
    )


def weight_grad(left_operand, right_operand):
    return jnp.einsum(
        "csa,csb->ab", left_operand, right_operand, preferred_element_type=jnp.float32
    )


def column_sum(values):
    return jnp.sum(values.astype(jnp.float32), axis=(0, 1))


def layer_slice(params, layer_index):
    return tuple((weight_array[layer_index] for weight_array in params))


def fetch_forward(local_params):
    return (
        lax.all_gather(local_params[0], "shard", axis=0, tiled=True),
        lax.all_gather(local_params[1], "shard", axis=0, tiled=True),
        lax.all_gather(local_params[2], "shard", axis=0, tiled=True),
        lax.all_gather(local_params[3], "shard", axis=0, tiled=True),
        lax.all_gather(local_params[4], "shard", axis=0, tiled=True),
        lax.all_gather(local_params[5], "shard", axis=0, tiled=True),
        lax.all_gather(local_params[6], "shard", axis=0, tiled=True),
        lax.all_gather(local_params[7], "shard", axis=0, tiled=True),
        lax.all_gather(local_params[8], "shard", axis=0, tiled=True),
        lax.all_gather(local_params[9], "shard", axis=0, tiled=True),
        lax.all_gather(local_params[10], "shard", axis=0, tiled=True),
        lax.all_gather(local_params[11], "shard", axis=0, tiled=True),
        lax.all_gather(local_params[12], "shard", axis=0, tiled=True),
        lax.all_gather(local_params[13], "shard", axis=0, tiled=True),
        lax.all_gather(local_params[14], "shard", axis=0, tiled=True),
    )


def fetch_again(local_params):
    return (
        lax.all_gather(local_params[0], "shard", axis=0, tiled=True),
        lax.all_gather(local_params[1], "shard", axis=0, tiled=True),
        lax.all_gather(local_params[2], "shard", axis=0, tiled=True),
        lax.all_gather(local_params[3], "shard", axis=0, tiled=True),
        lax.all_gather(local_params[4], "shard", axis=0, tiled=True),
        lax.all_gather(local_params[5], "shard", axis=0, tiled=True),
        lax.all_gather(local_params[6], "shard", axis=0, tiled=True),
        lax.all_gather(local_params[7], "shard", axis=0, tiled=True),
        lax.all_gather(local_params[8], "shard", axis=0, tiled=True),
        lax.all_gather(local_params[9], "shard", axis=0, tiled=True),
        lax.all_gather(local_params[10], "shard", axis=0, tiled=True),
        lax.all_gather(local_params[11], "shard", axis=0, tiled=True),
        lax.all_gather(local_params[12], "shard", axis=0, tiled=True),
        lax.all_gather(local_params[13], "shard", axis=0, tiled=True),
        lax.all_gather(local_params[14], "shard", axis=0, tiled=True),
    )


def forward_layer(hidden_state, weights, lengths):
    (
        attn_gain,
        attn_shift,
        query_weight,
        query_bias,
        key_weight,
        value_weight,
        value_bias,
        out_weight,
        out_bias,
        mlp_gain,
        mlp_shift,
        up_weight,
        up_bias,
        down_weight,
        down_bias,
    ) = weights
    clip_count, row_count, model_width = hidden_state.shape
    head_size = model_width // H
    query_scale = float(head_size) ** (-0.5)
    normed = norm_affine(
        hidden_state, attn_gain.astype(jnp.float32), attn_shift.astype(jnp.float32)
    ).astype(jnp.bfloat16)
    query_low = (
        (project(normed, query_weight) + query_bias.astype(jnp.float32)) * query_scale
    ).astype(jnp.bfloat16)
    key_low = project(normed, key_weight).astype(jnp.bfloat16)
    value_low = (project(normed, value_weight) + value_bias.astype(jnp.float32)).astype(
        jnp.bfloat16
    )
    key_all, value_all = (
        lax.all_gather(key_low, "shard", axis=1, tiled=True),
        lax.all_gather(value_low, "shard", axis=1, tiled=True),
    )
    length_all = key_all.shape[1]
    valid_keys = jnp.arange(length_all, dtype=jnp.int32)[None, :] < lengths[:, None]
    query_heads = query_low.reshape(clip_count, row_count, H, head_size)
    key_heads = key_all.reshape(clip_count, length_all, H, head_size)
    value_heads = value_all.reshape(clip_count, length_all, H, head_size)
    scores = jnp.einsum(
        "cqhd,ckhd->chqk", query_heads, key_heads, preferred_element_type=jnp.float32
    )
    scores = jnp.where(valid_keys[:, None, None, :], scores, NEGATIVE)
    attention = jax.nn.softmax(scores, axis=-1)
    attention_low = attention.astype(jnp.bfloat16)
    context = jnp.einsum(
        "chqk,ckhd->cqhd", attention_low, value_heads, preferred_element_type=jnp.float32
    )
    context_low = context.reshape(clip_count, row_count, model_width).astype(jnp.bfloat16)
    middle = hidden_state + project(context_low, out_weight) + out_bias.astype(jnp.float32)
    hidden_in = norm_affine(
        middle, mlp_gain.astype(jnp.float32), mlp_shift.astype(jnp.float32)
    ).astype(jnp.bfloat16)
    pre_gelu = project(hidden_in, up_weight) + up_bias.astype(jnp.float32)
    active_low = gelu_exact(pre_gelu).astype(jnp.bfloat16)
    result = middle + project(active_low, down_weight) + down_bias.astype(jnp.float32)
    kept_values = (
        normed,
        query_heads,
        key_heads,
        value_heads,
        attention,
        attention_low,
        context_low,
        middle,
        hidden_in,
        pre_gelu,
        active_low,
    )
    return (result, kept_values)


def backward_layer(hidden_state, grad_after, weights, lengths):
    (
        attn_gain,
        attn_shift,
        query_weight,
        query_bias,
        key_weight,
        value_weight,
        value_bias,
        out_weight,
        out_bias,
        mlp_gain,
        mlp_shift,
        up_weight,
        up_bias,
        down_weight,
        down_bias,
    ) = weights
    unused, kept_values = forward_layer(hidden_state, weights, lengths)
    (
        normed,
        query_heads,
        key_heads,
        value_heads,
        attention,
        attention_low,
        context_low,
        middle,
        hidden_in,
        pre_gelu,
        active_low,
    ) = kept_values
    clip_count, row_count, model_width = hidden_state.shape
    length_all = key_heads.shape[1]
    head_size = model_width // H
    query_scale = float(head_size) ** (-0.5)
    grad_low = grad_after.astype(jnp.bfloat16)
    grad_active = project_back(grad_low, down_weight)
    unused, gelu_pull = jax.vjp(gelu_exact, pre_gelu)
    grad_pre = gelu_pull(grad_active)[0].astype(jnp.bfloat16)
    grad_hidden = project_back(grad_pre, up_weight)
    unused, mlp_pull = jax.vjp(
        norm_affine, middle, mlp_gain.astype(jnp.float32), mlp_shift.astype(jnp.float32)
    )
    grad_middle_norm, grad_mlp_gain, grad_mlp_shift = mlp_pull(grad_hidden)
    grad_middle = grad_after + grad_middle_norm
    middle_low = grad_middle.astype(jnp.bfloat16)
    grad_context = project_back(middle_low, out_weight).astype(jnp.bfloat16)
    grad_context = grad_context.reshape(clip_count, row_count, H, head_size)
    grad_attention = jnp.einsum(
        "cqhd,ckhd->chqk", grad_context, value_heads, preferred_element_type=jnp.float32
    )
    value_part = jnp.einsum(
        "chqk,cqhd->ckhd", attention_low, grad_context, preferred_element_type=jnp.float32
    )
    grad_scores = attention * (
        grad_attention - jnp.sum(attention * grad_attention, axis=-1, keepdims=True)
    )
    scores_low = grad_scores.astype(jnp.bfloat16)
    grad_query = jnp.einsum(
        "chqk,ckhd->cqhd", scores_low, key_heads, preferred_element_type=jnp.float32
    )
    grad_query = grad_query.reshape(clip_count, row_count, model_width).astype(jnp.bfloat16)
    key_part = jnp.einsum(
        "chqk,cqhd->ckhd", scores_low, query_heads, preferred_element_type=jnp.float32
    )
    key_summed, value_summed = (
        lax.psum_scatter(
            key_part.reshape(clip_count, length_all, model_width).astype(jnp.bfloat16),
            "shard",
            scatter_dimension=1,
            tiled=True,
        ).astype(jnp.float32),
        lax.psum_scatter(
            value_part.reshape(clip_count, length_all, model_width).astype(jnp.bfloat16),
            "shard",
            scatter_dimension=1,
            tiled=True,
        ).astype(jnp.float32),
    )
    key_grad_low = key_summed.astype(jnp.bfloat16)
    value_grad_low = value_summed.astype(jnp.bfloat16)
    grad_normed = (
        project_back(grad_query, query_weight) * query_scale
        + project_back(key_grad_low, key_weight)
        + project_back(value_grad_low, value_weight)
    )
    unused, attn_pull = jax.vjp(
        norm_affine, hidden_state, attn_gain.astype(jnp.float32), attn_shift.astype(jnp.float32)
    )
    grad_input_norm, grad_attn_gain, grad_attn_shift = attn_pull(grad_normed)
    grad_before = grad_middle + grad_input_norm
    grad_down = weight_grad(active_low, grad_low)
    grad_down_bias = column_sum(grad_low)
    grad_up = weight_grad(hidden_in, grad_pre)
    grad_up_bias = column_sum(grad_pre)
    grad_out_weight = weight_grad(context_low, middle_low)
    grad_out_bias = column_sum(middle_low)
    grad_query_weight = weight_grad(normed, grad_query) * query_scale
    grad_query_bias = column_sum(grad_query) * query_scale
    grad_key_weight = weight_grad(normed, key_grad_low)
    grad_value_weight = weight_grad(normed, value_grad_low)
    grad_value_bias = column_sum(value_grad_low)
    owned_grads = (
        lax.psum_scatter(
            grad_attn_gain.astype(jnp.bfloat16), "shard", scatter_dimension=0, tiled=True
        ).astype(jnp.float32),
        lax.psum_scatter(
            grad_attn_shift.astype(jnp.bfloat16), "shard", scatter_dimension=0, tiled=True
        ).astype(jnp.float32),
        lax.psum_scatter(
            grad_query_weight.astype(jnp.bfloat16), "shard", scatter_dimension=0, tiled=True
        ).astype(jnp.float32),
        lax.psum_scatter(
            grad_query_bias.astype(jnp.bfloat16), "shard", scatter_dimension=0, tiled=True
        ).astype(jnp.float32),
        lax.psum_scatter(
            grad_key_weight.astype(jnp.bfloat16), "shard", scatter_dimension=0, tiled=True
        ).astype(jnp.float32),
        lax.psum_scatter(
            grad_value_weight.astype(jnp.bfloat16), "shard", scatter_dimension=0, tiled=True
        ).astype(jnp.float32),
        lax.psum_scatter(
            grad_value_bias.astype(jnp.bfloat16), "shard", scatter_dimension=0, tiled=True
        ).astype(jnp.float32),
        lax.psum_scatter(
            grad_out_weight.astype(jnp.bfloat16), "shard", scatter_dimension=0, tiled=True
        ).astype(jnp.float32),
        lax.psum_scatter(
            grad_out_bias.astype(jnp.bfloat16), "shard", scatter_dimension=0, tiled=True
        ).astype(jnp.float32),
        lax.psum_scatter(
            grad_mlp_gain.astype(jnp.bfloat16), "shard", scatter_dimension=0, tiled=True
        ).astype(jnp.float32),
        lax.psum_scatter(
            grad_mlp_shift.astype(jnp.bfloat16), "shard", scatter_dimension=0, tiled=True
        ).astype(jnp.float32),
        lax.psum_scatter(
            grad_up.astype(jnp.bfloat16), "shard", scatter_dimension=0, tiled=True
        ).astype(jnp.float32),
        lax.psum_scatter(
            grad_up_bias.astype(jnp.bfloat16), "shard", scatter_dimension=0, tiled=True
        ).astype(jnp.float32),
        lax.psum_scatter(
            grad_down.astype(jnp.bfloat16), "shard", scatter_dimension=0, tiled=True
        ).astype(jnp.float32),
        lax.psum_scatter(
            grad_down_bias.astype(jnp.bfloat16), "shard", scatter_dimension=0, tiled=True
        ).astype(jnp.float32),
    )
    return (grad_before, owned_grads)


def replica_layer(owned_grads):
    return (
        lax.psum(owned_grads[0].astype(jnp.bfloat16), "rep").astype(jnp.float32),
        lax.psum(owned_grads[1].astype(jnp.bfloat16), "rep").astype(jnp.float32),
        lax.psum(owned_grads[2].astype(jnp.bfloat16), "rep").astype(jnp.float32),
        lax.psum(owned_grads[3].astype(jnp.bfloat16), "rep").astype(jnp.float32),
        lax.psum(owned_grads[4].astype(jnp.bfloat16), "rep").astype(jnp.float32),
        lax.psum(owned_grads[5].astype(jnp.bfloat16), "rep").astype(jnp.float32),
        lax.psum(owned_grads[6].astype(jnp.bfloat16), "rep").astype(jnp.float32),
        lax.psum(owned_grads[7].astype(jnp.bfloat16), "rep").astype(jnp.float32),
        lax.psum(owned_grads[8].astype(jnp.bfloat16), "rep").astype(jnp.float32),
        lax.psum(owned_grads[9].astype(jnp.bfloat16), "rep").astype(jnp.float32),
        lax.psum(owned_grads[10].astype(jnp.bfloat16), "rep").astype(jnp.float32),
        lax.psum(owned_grads[11].astype(jnp.bfloat16), "rep").astype(jnp.float32),
        lax.psum(owned_grads[12].astype(jnp.bfloat16), "rep").astype(jnp.float32),
        lax.psum(owned_grads[13].astype(jnp.bfloat16), "rep").astype(jnp.float32),
        lax.psum(owned_grads[14].astype(jnp.bfloat16), "rep").astype(jnp.float32),
    )


def general_shards(
    inputs,
    lengths,
    cotangent,
    attn_gain,
    attn_shift,
    query_weight,
    query_bias,
    key_weight,
    value_weight,
    value_bias,
    out_weight,
    out_bias,
    mlp_gain,
    mlp_shift,
    up_weight,
    up_bias,
    down_weight,
    down_bias,
):
    params = (
        attn_gain,
        attn_shift,
        query_weight,
        query_bias,
        key_weight,
        value_weight,
        value_bias,
        out_weight,
        out_bias,
        mlp_gain,
        mlp_shift,
        up_weight,
        up_bias,
        down_weight,
        down_bias,
    )
    layers = attn_gain.shape[0]
    hidden_state = inputs.astype(jnp.float32)
    kept_inputs = []
    kept_weights = []
    for layer_index in range(layers):
        gathered = fetch_forward(layer_slice(params, layer_index))
        kept_inputs.append(hidden_state)
        kept_weights.append(gathered)
        hidden_state, unused = forward_layer(hidden_state, gathered, lengths)
    output = hidden_state.astype(jnp.bfloat16)
    row_count = inputs.shape[1]
    first_row = lax.axis_index("shard") * row_count
    positions = first_row + jnp.arange(row_count, dtype=jnp.int32)
    row_mask = (positions[None, :] < lengths[:, None]).astype(jnp.float32)
    grad_state = cotangent.astype(jnp.float32) * row_mask[:, :, None]
    owned_list = [None] * layers
    for layer_index in reversed(range(layers)):
        gathered = fetch_again(layer_slice(params, layer_index))
        grad_state, owned_grads = backward_layer(
            kept_inputs[layer_index], grad_state, gathered, lengths
        )
        owned_grads = replica_layer(owned_grads)
        owned_list[layer_index] = owned_grads
    stacked = tuple(
        (
            jnp.stack([owned_list[layer_index][member] for layer_index in range(layers)])
            for member in range(15)
        )
    )
    return (
        output,
        grad_state,
        stacked[0],
        stacked[1],
        stacked[2],
        stacked[3],
        stacked[4],
        stacked[5],
        stacked[6],
        stacked[7],
        stacked[8],
        stacked[9],
        stacked[10],
        stacked[11],
        stacked[12],
        stacked[13],
        stacked[14],
    )


def pick(values, index, axis=0):
    return lax.dynamic_index_in_dim(values, index, axis, keepdims=False)


def place():
    rep = lax.axis_index("rep")
    return rep // 4, (rep // 2) % 2, rep % 2, lax.axis_index("shard")


MESH = pl.DeviceIdType.MESH

def device(a, b, core, z):
    return ((a * 2 + b) * 2 + core, z)


class Net:
    def __init__(self, sent, arrived):
        self.sent, self.arrived = sent, arrived
        self.copies, self.count = [], 0
    def push(self, source, target_ref, target, sent=None):
        copy = pltpu.make_async_remote_copy(
            src_ref=source, dst_ref=target_ref, send_sem=self.sent if sent is None else sent,
            recv_sem=self.arrived.at[self.count], device_id=target, device_id_type=MESH)
        copy.start()
        self.count += 1
        if sent is None:
            self.copies.append(copy)
        return copy

    def drain(self):
        for copy in self.copies:
            copy.wait_send()

def greet(targets, regroup=None):
    barrier = pltpu.get_barrier_semaphore()

    def signal(target):
        pl.semaphore_signal(barrier, inc=1, device_id=target, device_id_type=MESH)

    for target in targets:
        signal(target)
    if regroup is None:
        pl.semaphore_wait(barrier, len(targets))
        return
    stays, to, source, both = regroup
    for step in range(2):
        for target in (source[step], to[step]) if both else (source[step],):

            @pl.when(True if step else jnp.logical_not(stays))
            def _():
                signal(target)

    extra = 2 if both else 1

    @pl.when(stays)
    def _():
        pl.semaphore_wait(barrier, len(targets) + extra)

    @pl.when(jnp.logical_not(stays))
    def _():
        pl.semaphore_wait(barrier, len(targets) + 2 * extra)


def regrouping():
    a, b, core, z = place()
    to, source = [], []
    for step in range(2):
        to.append(device(a, b, z // 2, 2 * core + lax.rem(z + step, 2)))
        source.append(device(a, b, z // 2, 2 * core + lax.rem(z + step, 2)))
    return core == z // 2, to, source


class Swap:
    def __init__(self, net, source, target_ref, target, stays, sent, local):
        self.stays = stays
        self.far = pltpu.make_async_remote_copy(
            src_ref=source, dst_ref=target_ref, send_sem=sent, recv_sem=net.arrived.at[net.count],
            device_id=target, device_id_type=MESH)
        self.near = pltpu.make_async_copy(source, target_ref, local) if stays is not None else None
        net.count += 1

    def both(self, near, far):
        if self.stays is None:
            far()
            return
        pl.when(self.stays)(near)
        pl.when(jnp.logical_not(self.stays))(far)

    def start(self):
        self.both(lambda: self.near.start(), lambda: self.far.start())
        return self

    def wait(self):
        self.both(lambda: self.near.wait(), lambda: self.far.wait())

def gather_regions(index, zs, chip, core):
    part = chip * 2 + core
    def rows(base, size):
        return pl.ds(pl.multiple_of(base, 8), size)
    if index < 2:
        return 0, (pl.ds(2 * index, 2), rows(zs * 320 + part * 40, 40), slice(None))
    if index < 4:
        return 1, (rows(zs * 320 + part * 40, 40), pl.ds((index - 2) * 2560, 2560))
    return 2, (rows(zs * 1280 + part * 160 + (index - 4) * 80, 80), slice(None))


NN = (((1,), (0,)), ((), ()))
TN = (((0,), (0,)), ((), ()))
NT = (((1,), (1,)), ((), ()))
TOKENS = 512
ROOT_HALF = math.sqrt(0.5)
ROOT_TWO_PI = math.sqrt(2.0 * math.pi)

def dot(left, right, numbers=NN):
    return lax.dot_general(left, right, numbers, preferred_element_type=F32)


def tile(i, size):
    return pl.ds(pl.multiple_of(i * size, size), size)


def stream(count, copy, body):
    copy(0, 0).start()

    @pl.loop(0, count)
    def _(i):
        slot = i % 2

        @pl.when(i + 1 < count)
        def _():
            copy(i + 1, 1 - slot).start()

        copy(i, slot).wait()
        body(i, slot)


def transpose_into(target, source, rows):
    @pl.loop(0, rows // 128)
    def _(i):
        target[tile(i, 128), :] = source[:, tile(i, 128)].T


def gather_program(net, layers, shards, outs, copies, local):
    a, b, core, z = place()
    behind = [lax.rem(z + 4 - s, 4) for s in range(4)]
    to_z = [device(a, b, core, lax.rem(z + s, 4)) for s in range(4)]
    to_a, to_b, to_core = device(1 - a, b, core, z), device(a, 1 - b, core, z), device(a, b, 1 - core, z)
    count = 6 * layers
    twin = [[] for _ in range(count)]

    def refs_at(index, zs, pa, pb, whose):
        which, at = gather_regions(index % 6, zs, pa * 2 + pb, core)
        return whose[which].at[index // 6].at[at]

    def start(index):
        if index % 6 > 1:
            return [[net.push(refs_at(index, 0, a, b, shards), refs_at(index, z, a, b, outs), to_z[s])] for s in (1, 2, 3)]
        here, there = [
            pl.ds(pl.multiple_of(zs * 320 + ((a * 2 + b) * 2 + core) * 40, 8), 40) for zs in (0, z)]
        return [
            [net.push(shards[0][i].at[index // 6, here, :], outs[0].at[index // 6, i, there, :], to_z[s])
             for i in (2 * (index % 6), 2 * (index % 6) + 1)]
            for s in (1, 2, 3)
        ]

    def on(index, s, pa, pb, target):
        ref = refs_at(index, behind[s], pa, pb, outs)
        copy = net.push(ref, ref, target)
        if target is to_core:
            twin[index].append(copy)
        return copy

    def own_copies(step):
        layer, which = step // 3, step % 3
        out = outs[which].at[layer]
        shard = shards[which].at[layer] if which else None
        ins, back = [], []
        for i in range(4):
            if which == 0:
                source, target = shards[0][i].at[layer], out.at[i, pl.ds(pl.multiple_of(z * 320, 8), 320), :]
            elif which == 1:
                source = shard.at[:, pl.ds(i * 1280, 1280)]
                target = out.at[pl.ds(pl.multiple_of(z * 320, 8), 320), pl.ds(i * 1280, 1280)]
            else:
                source = shard.at[pl.ds(i * 320, 320), :]
                target = out.at[pl.ds(pl.multiple_of(z * 1280 + i * 320, 8), 320), :]
            ins.append(pltpu.make_async_copy(source, copies.at[i], local))
            back.append(pltpu.make_async_copy(copies.at[i], target, local))
        for copy in ins:
            copy.start()
        for copy in ins:
            copy.wait()
        for copy in back:
            copy.start()
        for copy in back:
            copy.wait()

    zed, mid, diag = {}, {}, {}
    zed[0] = start(0)
    zed[1] = start(1)
    own_copies(0)
    yield twin
    for t in range(count + 2):
        if t < count:
            mid[t] = {}
            for s in (1, 2, 3):
                for copy in zed[t][s - 1]:
                    copy.wait_recv()
                mid[t][s] = (on(t, s, a, b, to_b), on(t, s, a, b, to_a))
                on(t, s, a, b, to_core)
            if t + 2 < count:
                zed[t + 2] = start(t + 2)
        if 0 <= t - 1 < count:
            k = t - 1
            diag[k] = {}
            for s in (1, 2, 3):
                via_b, via_a = mid[k][s]
                via_b.wait_recv()
                on(k, s, a, 1 - b, to_core)
                if (s + k) % 2 == 0:
                    diag[k][s] = on(k, s, a, 1 - b, to_a)
                via_a.wait_recv()
                on(k, s, 1 - a, b, to_core)
                if (s + k) % 2 == 1:
                    diag[k][s] = on(k, s, 1 - a, b, to_b)
        if 0 <= t - 2 < count:
            k = t - 2
            for s in (1, 2, 3):
                diag[k][s].wait_recv()
                on(k, s, 1 - a, 1 - b, to_core)
        if t + 1 < 3 * layers:
            own_copies(t + 1)
        yield twin


def normalize_rows(source, target, gain, shift, rows=64):
    @pl.loop(0, TOKENS // rows)
    def _(i):
        values = source[tile(i, rows), :]
        center = values - jnp.mean(values, axis=-1, keepdims=True)
        scale = lax.rsqrt(jnp.mean(center * center, axis=-1, keepdims=True) + EPSILON)
        target[tile(i, rows), :] = (center * scale * gain + shift).astype(BF16)


def attend_heads(first, last, query, key, value, far, masks, context, lse):
    @pl.loop(first, last)
    def _(h):
        at = pl.ds(pl.multiple_of(h * 80, 16), 80)
        q = query[at, :]
        s0 = dot(key[at, :], q, TN) + masks[0]
        s1 = dot(far[0, at, :], q, TN) + masks[1]
        top = jnp.maximum(jnp.max(s0, axis=0, keepdims=True), jnp.max(s1, axis=0, keepdims=True))
        e0, e1 = jnp.exp(s0 - top), jnp.exp(s1 - top)
        total = jnp.sum(e0, axis=0, keepdims=True) + jnp.sum(e1, axis=0, keepdims=True)
        out = dot(value[at, :], e0.astype(BF16)) + dot(far[1, at, :], e1.astype(BF16))
        context[at, :] = (out / total).astype(BF16)
        lse[h] = top + jnp.log(total)


def forward_kernel(layers, *refs):
    (tokens, cotangent, query_w, key_w, value_w, out_w, up, down, part, lengths,
     attn_full, up_full, down_full, keep_normed, keep_qkv, keep_far, keep_lse, keep_context, keep_middle,
     keep_hidden, keep_slope, keep_active, states, far_active, far_hidden, far_context, far_normed,
     cotangent_in, final, vectors, masks,
     state, middle, normed, normed_t, hidden_t, qkv, far, context_t, context, active, active_t, slope, lse,
     small_w, up_w, down_w, copies, product, parts_in, lengths_in,
     local, wsem, saved, swapped, handed, early, moved, stayed, sent, arrived) = refs
    a, b, core, z = place()
    to_core = device(a, b, 1 - core, z)
    to_z = [device(a, b, core, lax.rem(z + s, 4)) for s in (1, 2, 3)]
    stays, to, source = regrouping()
    greet(to_z + [device(1 - a, b, core, z), device(a, 1 - b, core, z), to_core], (stays, to, source, False))
    net = Net(sent, arrived)

    def regroup(values, targets, first):
        return [
            Swap(net, values.at[lax.rem(z + step, 2)], targets[step], to[step], None if step else stays,
                 moved.at[first + step], stayed.at[first]).start()
            for step in range(2)
        ]

    shared = [net.push(part, parts_in.at[i], to_z[i], early) for i in range(3)]
    shared.append(net.push(lengths, lengths_in, to_core, early))
    ticks = gather_program(net, layers, ((query_w, key_w, value_w, out_w), up, down), (attn_full, up_full, down_full),
                           copies, local)
    twin = next(ticks)
    clock = [-1]
    block = tokens.shape[1]
    tokens_here = regroup(tokens, [context.at[pl.ds(step * block, block), :] for step in range(2)], 0)
    next(ticks)
    next(ticks)
    clock[0] = 1
    for copy in shared:
        copy.wait()

    @pl.loop(0, layers)
    def _(i):
        total_ = part[i].astype(F32)
        for j in range(3):
            total_ = total_ + parts_in[j, i].astype(F32)
        vectors[i] = total_

    which = lax.rem(z, 2)
    length = jnp.where(z // 2 == core, lengths[which], lengths_in[which])[0:1, 0:1]
    for i in range(2):
        owner = core if i == 0 else 1 - core
        for step in range(2):
            first = (2 * owner + lax.rem(z + step, 2)) * block
            at = (lax.broadcasted_iota(jnp.int32, (block, 1), 0) + first).astype(F32)
            masks[i, step * block : (step + 1) * block, :] = jnp.where(at < length, 0.0, NEGATIVE)
    for copy in tokens_here:
        copy.wait()

    @pl.loop(0, 8)
    def _(i):
        state[tile(i, 64), :] = context[tile(i, 64), :].astype(F32)

    def pump(until):
        while clock[0] < until:
            next(ticks)
            clock[0] += 1

    def ready(*chunks):
        pump(max(chunks) + 2)
        for chunk in chunks:
            for copy in twin[chunk]:
                copy.wait_recv()

    saves = []

    def save(source, target):
        copy = pltpu.make_async_copy(source, target, saved)
        copy.start()
        saves.append(copy)

    given, taken = [], []

    def hand(source, target):
        copy = net.push(source, target, to_core, handed)
        given.append(copy)
        taken.append(copy)

    scale = float(80) ** (-0.5)
    for layer in range(layers):
        base = 6 * layer
        for copy in given:
            copy.wait_send()
        given.clear()
        vec = vectors.at[layer]

        def row(i):
            return vec[i : i + 1, :]

        weights = attn_full.at[layer]
        save(state, states.at[layer])
        normalize_rows(state, normed, row(0), row(1))
        transpose_into(normed_t, normed, 1280)
        save(normed_t, keep_normed.at[layer])
        hand(normed_t, far_normed.at[layer])
        ready(base, base + 1)

        def project(which, bias, factor, target):
            def copy(i, slot):
                return pltpu.make_async_copy(weights.at[which, :, tile(i, 256)], small_w.at[slot], wsem.at[slot])

            def body(i, slot):
                out = dot(normed[...], small_w[slot])
                if bias is not None:
                    out = out + vec[bias : bias + 1, tile(i, 256)]
                if factor != 1.0:
                    out = out * factor
                target[tile(i, 256), :] = out.astype(BF16).T

            stream(5, copy, body)

        project(1, None, 1.0, qkv.at[1])
        project(2, 3, 1.0, qkv.at[2])
        swap = net.push(qkv.at[pl.ds(1, 2)], far.at[layer], to_core, swapped)
        project(0, 2, scale, qkv.at[0])
        pump(base + 4)
        swap.wait()
        for part in range(4):
            if part == 2:
                pump(base + 5)
                if layer == layers - 1:
                    cotangent_at = [copies.at[step, pl.ds(0, block), :] for step in range(2)]
                    cotangent_here = regroup(cotangent, cotangent_at, 2)
            attend_heads(4 * part, 4 * part + 4, qkv.at[0], qkv.at[1], qkv.at[2], far.at[layer], masks, context_t, lse)
        save(qkv, keep_qkv.at[layer])
        save(far.at[layer], keep_far.at[layer])
        save(lse, keep_lse.at[layer])
        save(context_t, keep_context.at[layer])
        hand(context_t, far_context.at[layer])

        @pl.loop(0, 10)
        def _(i):
            context[:, tile(i, 128)] = context_t[tile(i, 128), :].T

        def copy_out(i, slot):
            return pltpu.make_async_copy(weights.at[3, :, tile(i, 256)], small_w.at[slot], wsem.at[slot])

        def body_out(i, slot):
            at = tile(i, 256)
            middle[:, at] = state[:, at] + dot(context[...], small_w[slot]) + vec[4:5, at]

        stream(5, copy_out, body_out)
        save(middle, keep_middle.at[layer])
        normalize_rows(middle, normed, row(5), row(6))
        transpose_into(hidden_t, normed, 1280)
        save(hidden_t, keep_hidden.at[layer])
        hand(hidden_t, far_hidden.at[layer])
        pump(base + 6)
        ready(base + 2, base + 3)

        def copy_up(i, slot):
            return pltpu.make_async_copy(up_full.at[layer, :, tile(i, 512)], up_w.at[slot], wsem.at[slot])

        def body_up(i, slot):
            at = tile(i, 512)
            product[...] = dot(normed[...], up_w[slot])
            bias = vec[pl.ds(8 + i, 1), :512]

            @pl.loop(0, 16)
            def _(j):
                u = product[tile(j, 32), :] + bias
                half = 0.5 * (1.0 + lax.erf(u * ROOT_HALF))
                active[tile(j, 32), at] = (u * half).astype(BF16)
                slope[tile(j, 32), at] = (half + u * jnp.exp(-0.5 * u * u) * (1.0 / ROOT_TWO_PI)).astype(BF16)

            active_t[at, :] = active[:, at].T

        stream(10, copy_up, body_up)
        save(slope, keep_slope.at[layer])
        save(active_t, keep_active.at[layer])
        for i in range(4):
            rows = pl.ds(pl.multiple_of(i * 1280 + (1 - core) * 640, 128), 640)
            hand(active_t.at[rows, :], far_active.at[layer, i])
        ready(base + 4, base + 5)

        def copy_down(i, slot):
            return pltpu.make_async_copy(down_full.at[layer, :, tile(i, 256)], down_w.at[slot], wsem.at[slot])

        for copy in saves:
            copy.wait()
        saves.clear()

        def body_down(i, slot):
            at = tile(i, 256)
            state[:, at] = middle[:, at] + dot(active[...], down_w[slot]) + vec[7:8, at]

        stream(5, copy_down, body_down)

    @pl.loop(0, 8)
    def _(i):
        normed[tile(i, 64), :] = state[tile(i, 64), :].astype(BF16)

    for copy in cotangent_here:
        copy.wait()
    save(normed, final)
    for step in range(2):
        save(cotangent_at[step], cotangent_in.at[step])
    for copy in saves:
        copy.wait()
    for copy in given:
        copy.wait_send()
    for copy in taken:
        copy.wait_recv()
    net.drain()


def forward_all(tokens, cotangent, shards, part, lengths):
    any_ = pl.BlockSpec(memory_space=pl.ANY)
    vmem = pl.BlockSpec(memory_space=pltpu.VMEM)
    layers = part.shape[0]
    t = TOKENS

    def hbm(shape, dtype=BF16):
        return jax.ShapeDtypeStruct((layers,) + shape, dtype)

    out_shape = (
        hbm((4, 1280, 1280)), hbm((1280, 5120)), hbm((5120, 1280)),
        hbm((1280, t)), hbm((3, 1280, t)), hbm((2, 1280, t)), hbm((H, 1, t), F32), hbm((1280, t)), hbm((t, 1280), F32),
        hbm((1280, t)), hbm((t, 5120)), hbm((5120, t)), hbm((t, 1280), F32),
        hbm((4, 640, t)), hbm((1280, t)), hbm((1280, t)), hbm((1280, t)),
        jax.ShapeDtypeStruct(tokens.shape, BF16), jax.ShapeDtypeStruct((t, 1280), BF16), hbm((24, 1280), F32), jax.ShapeDtypeStruct((2, t, 1), F32),
    )
    v = pltpu.VMEM
    return pl.pallas_call(
        functools.partial(forward_kernel, layers),
        out_shape=out_shape,
        in_specs=[any_] * 8 + [vmem] * 2,
        out_specs=(any_,) * (len(out_shape) - 2) + (vmem,) * 2,
        scratch_shapes=[
            v((t, 1280), F32), v((t, 1280), F32), v((t, 1280), BF16), v((1280, t), BF16), v((1280, t), BF16),
            v((3, 1280, t), BF16), v((layers, 2, 1280, t), BF16), v((1280, t), BF16), v((t, 1280), BF16),
            v((t, 5120), BF16), v((5120, t), BF16), v((t, 5120), BF16), v((H, 1, t), F32),
            v((2, 1280, 256), BF16), v((2, 1280, 512), BF16), v((2, 5120, 256), BF16), v((4, 320, 1280), BF16),
            v((t, 512), F32), v((3,) + part.shape, BF16), v(lengths.shape, F32),
            pltpu.SemaphoreType.DMA, pltpu.SemaphoreType.DMA((2,)), pltpu.SemaphoreType.DMA,
            pltpu.SemaphoreType.DMA, pltpu.SemaphoreType.DMA, pltpu.SemaphoreType.DMA,
            pltpu.SemaphoreType.DMA((4,)), pltpu.SemaphoreType.DMA((4,)), pltpu.SemaphoreType.DMA,
            pltpu.SemaphoreType.DMA((6 * layers * 24 + 14 * layers + 8,)),
        ],
        compiler_params=pltpu.CompilerParams(collective_id=1, has_side_effects=True, vmem_limit_bytes=63 << 20),
        name="forward_all",
    )(tokens, cotangent, *shards, part, lengths)


def add(*parts):
    total = parts[0].astype(F32)
    for part in parts[1:]:
        total = total + part.astype(F32)
    return total.astype(BF16)


ITEMS_A_LAYER = 12
RING, XRING = 10, 4
ORDERS = ("azb", "baz", "abz", "bza", "azb", "baz", "abz", "bza", "azb", "baz", "abz", "bza")
PLAN = (
    -1, -1, -1, -1, -1, 0, 1, -1, 2, 3, -1, 0, 1, -1, -1, 4, 5, 2, 3, -1, -1, -1, 6, 7, 4, 5, 0, 1, -1, 2, 6,
    3, -1, 4, -1, 8, 7, 0, 1, 2, -1, 5, 3, 4, 0, 1, 2, -1, -1, 6, 7, 0, 1, 2, -1, -1, 9, 10, 8, 5, 3, 4, -1,
    3, 4, 9, 5, 11, 5, -1, 6, 7, -1, 10, -1, 12, 11, 8, 9, 13, 14, 10, -1, 11, 15, 12, 13, 6, 7, 8, 6, 7, 9,
    -1, -1, 16, 14, 15, 10, -1, -1, 17, -1, 18, 12, 13, 11, 8, 9, -1, 16, 8, 9, -1, 19, 20, 14, 15, 10, -1,
    17, 18, 12, 10, -1, 16, 13, 14, 11, -1, 19, 15, 16, 12, 13, 14, 11, -1, 12, -1, 13, 14, -1, -4, -3, -2,
    20, 17, 21, 22, 15, 16, 15, -4, -3, -2, 16, 18, 19, 21, 23, 20, 17, 21, -4, -3, -2, 17, 17, 22, 18, 19,
    20, 21, 18, -4, -3, -2, 19, 23, 20, 21, 18, 19, 20, 21, 22, 23, 22, 23, 22, 23, 22, -4, -3, -2, 23
)


def streams(count, copies, body):
    for copy in copies(0, 0):
        copy.start()

    @pl.loop(0, count)
    def _(i):
        slot = i % 2

        @pl.when(i + 1 < count)
        def _():
            for copy in copies(i + 1, 1 - slot):
                copy.start()

        for copy in copies(i, slot):
            copy.wait()
        body(i, slot)


def add_blocks(blocks, target, parts):
    @pl.loop(0, blocks * 5)
    def _(i):
        block = i // 5
        at = pl.ds(pl.multiple_of((i % 5) * 16, 16), 16)
        refs = [part(block) for part in parts]
        sums = refs[0][at, :].astype(F32)
        for ref in refs[1:]:
            sums = sums + ref[at, :].astype(F32)
        target(block)[at, :] = sums.astype(BF16)


def backward_kernel(layers, *refs):
    (cotangent, final, attn_full, up_full, down_full, normed_t, qkv, far, lse_all, context_t, middles, hidden_t, slopes,
     active_t, states, active_far, hidden_far, context_far, normed_far, vectors, masks,
     output, grad_out, down_out, up_out, out_out, qkv_out, sums,
     grad_f_far, grad_pre_far, grad_o_far, grad_far, grad_kv_far,
     g, low, gp, gs, gh, rows_in, big, dfar, heads_in, far_in, lse, wide_w, slope_in, left_in,
     xs, got1s, got2s, got3s, finals, sums_held, sums_in,
     local, lsem, swapped, swapped_half, item_sent, item_local, sums_sent, moved, stayed,
     sent, arrived) = refs
    a, b, core, z = place()
    to_z = [device(a, b, core, lax.rem(z + s, 4)) for s in range(4)]
    to_a, to_b, to_core = device(1 - a, b, core, z), device(a, 1 - b, core, z), device(a, b, 1 - core, z)
    stays, to, source = regrouping()
    greet(to_z[1:] + [to_a, to_b, to_core], (stays, to, source, False))
    net = Net(sent, arrived)
    scale = float(80) ** (-0.5)
    side = {"a": (a, to_a), "b": (b, to_b)}

    def program(number, order, spot):
        slot = number % RING
        x, got1, got2, got3, final = (
            xs.at[number % XRING], got1s.at[slot], got2s.at[slot], got3s.at[slot], finals.at[slot])
        target = side[order[0]][1]
        other, other_target = side["b" if order[0] == "a" else "a"]

        def push(source, target_ref, target, stage):
            return net.push(source, target_ref, target, item_sent.at[slot, stage])

        first = push(x.at[1], got1, target, 0)
        yield
        first.wait()
        add_blocks(8, lambda i: got1.at[i // 2, i % 2],
                   [lambda i: got1.at[i // 2, i % 2], lambda i: x.at[0, i // 2, i % 2]])
        if order[1] == "z":
            nexts = [push(got1.at[lax.rem(z + s, 4)], got2.at[pl.ds(2 * s - 2, 2)], to_z[s], 1) for s in (1, 2, 3)]
        else:
            nexts = [push(got1.at[:, 1 - other], got2.at[pl.ds(0, 4)], other_target, 1)]
        yield
        for copy in nexts:
            copy.wait()
        if order[1] == "z":
            add_blocks(2, lambda i: got1.at[z, i],
                       [lambda i: got1.at[z, i]] + [lambda i, s=s: got2.at[2 * s + i] for s in range(3)])
            nexts = [push(got1.at[z, 1 - other], got3.at[0], other_target, 2)]
        else:
            add_blocks(4, lambda i: got2.at[i], [lambda i: got2.at[i], lambda i: got1.at[i, other]])
            nexts = [push(got2.at[lax.rem(z + s, 4)], got3.at[s - 1], to_z[s], 2) for s in (1, 2, 3)]
        yield
        for copy in nexts:
            copy.wait()
        if order[1] == "z":
            add_blocks(1, lambda i: final, [lambda i: got1.at[z, other], lambda i: got3.at[0]])
        else:
            add_blocks(1, lambda i: final, [lambda i: got2.at[z]] + [lambda i, s=s: got3.at[s] for s in range(3)])
        mine = pltpu.make_async_copy(final, spot(core, a, b), item_local.at[slot])
        mine.start()
        via = [push(final, spot(core, a, b), target, 3) for target in (to_a, to_b, to_core)]
        yield
        mine.wait()
        for copy in via:
            copy.wait()

        def on(pa, pb, target):
            return net.push(spot(core, pa, pb), spot(core, pa, pb), target)

        diag = on(1 - a, b, to_b) if number % 2 == 0 else on(a, 1 - b, to_a)
        twin = [on(1 - a, b, to_core), on(a, 1 - b, to_core)]
        yield
        diag.wait_recv()
        twin.append(on(1 - a, 1 - b, to_core))
        yield
        for copy in twin:
            copy.wait_recv()
        yield

    programs, stage = [], []

    def advance(number):
        next(programs[number])
        stage[number] += 1

    def send_item(order, spot):
        number = len(programs)
        assert all(s > 4 for s in stage[: max(0, number + 1 - RING)])
        programs.append(program(number, order, spot))
        stage.append(0)
        advance(number)

    def weight_gradient(height, own, far_, parts):
        base = len(programs)
        count = sum(len(part[3]) for part in parts)
        assert all(s > 1 for s in stage[: max(0, base + count - XRING)])

        def copies(i, slot):
            return [
                pltpu.make_async_copy(own(i), left_in.at[slot, 0, pl.ds(0, height), :], lsem.at[slot]),
                pltpu.make_async_copy(far_(i), left_in.at[slot, 1, pl.ds(0, height), :], lsem.at[slot]),
            ]

        def body(i, slot):
            for right, far_right, factor, targets in parts:
                out = dot(left_in[slot, 0, :height, :], right()) + dot(left_in[slot, 1, :height, :], far_right())
                if factor != 1.0:
                    out = out * factor
                out = out.astype(BF16)
                for item, order, first in targets:
                    x = xs.at[(base + item) % XRING]
                    for pa in range(2):
                        for pb in range(2):
                            row = (pa * 2 + pb) * (height // 4) + first
                            block = out[row : row + 80, :]
                            if order[0] == "a":
                                x[lax.rem(pa + a, 2), i, pb] = block
                            else:
                                x[lax.rem(pb + b, 2), i, pa] = block

        streams(4, copies, body)

    def fetch(*pairs):
        copies = [pltpu.make_async_copy(x, y, local) for x, y in pairs]
        for copy in copies:
            copy.start()
        for copy in copies:
            copy.wait()

    def norm_back(source, gain, gain_at, layer, lowered):
        def copies(i, slot):
            return [pltpu.make_async_copy(source.at[tile(i, 64), :], rows_in.at[slot], lsem.at[slot])]

        def body(i, slot):
            at = tile(i, 64)
            values = rows_in[slot]
            center = values - jnp.mean(values, axis=-1, keepdims=True)
            s = lax.rsqrt(jnp.mean(center * center, axis=-1, keepdims=True) + EPSILON)
            unit = center * s
            grad = gh[at, :]
            e = grad * gain
            out = g[at, :] + s * (
                e - jnp.mean(e, axis=-1, keepdims=True) - unit * jnp.mean(e * unit, axis=-1, keepdims=True))
            g[at, :] = out
            sums[layer, pl.ds(gain_at, 1), :] += jnp.sum(grad * unit, axis=0, keepdims=True)
            sums[layer, pl.ds(gain_at + 1, 1), :] += jnp.sum(grad, axis=0, keepdims=True)
            small = out.astype(BF16)
            if lowered or layer == 0:
                low[0, at, :] = small
            if lowered:
                sums[layer, pl.ds(4, 1), :] += jnp.sum(small.astype(F32), axis=0, keepdims=True)

        streams(8, copies, body)

    block = cotangent.shape[1]

    def give_back(values, target, first):
        return [
            Swap(net, values.at[pl.ds(step * block, block), :], target.at[lax.rem(z, 2)], to[step], None if step else stays,
                 moved.at[first + step], stayed.at[first]).start()
            for step in range(2)
        ]

    held = gs.at[:, pl.ds(0, 1280)]
    fetch((final, held))
    returned = give_back(held, output, 0)
    fetch(*[(cotangent.at[step], low.at[0, pl.ds(step * block, block), :]) for step in range(2)])

    @pl.loop(0, 8)
    def _(i):
        at = tile(i, 64)
        g[at, :] = jnp.where(masks[0, at, :] == 0.0, low[0, at, :].astype(F32), 0.0)

    sums[...] = jnp.zeros_like(sums)

    def sum_program(which, layer, first, size):
        rows = pl.ds(first, size)
        steps = [[to_core], [to_b], [to_a], to_z[1:]]
        sums_held[layer, 0, rows, :] = sums[layer, rows, :]
        place_in = 0
        for number, targets in enumerate(steps):
            copies = [
                net.push(sums_held.at[layer, number, rows], sums_in.at[layer, place_in + i, rows], target,
                         sums_sent.at[which, number])
                for i, target in enumerate(targets)
            ]
            yield
            for copy in copies:
                copy.wait()
            all_ = sums_held[layer, number, rows, :]
            for i in range(len(targets)):
                all_ = all_ + sums_in[layer, place_in + i, rows, :]
            place_in += len(targets)
            if number < 3:
                sums_held[layer, number + 1, rows, :] = all_
            else:
                sums[layer, rows, :] = all_
        yield

    def work(layer):
        vec = vectors.at[layer]
        first_item = ITEMS_A_LAYER * (layers - 1 - layer)

        def order_of(item):
            return ORDERS[item]

        @pl.loop(0, 8)
        def _(i):
            at = tile(i, 64)
            small = g[at, :].astype(BF16)
            low[0, at, :] = small
            sums[layer, pl.ds(7, 1), :] += jnp.sum(small.astype(F32), axis=0, keepdims=True)

        swap = net.push(low.at[0], grad_f_far.at[layer], to_core, swapped)
        yield
        swap.wait()
        fetch((grad_f_far.at[layer], low.at[1]))

        def down_spot(half, column):
            def spot(pc, pa, pb):
                row = pc * 640 + (pa * 2 + pb) * 160 + half * 80
                return down_out.at[layer, pl.ds(pl.multiple_of(row, 16), 80), pl.ds(column * 640, 640)]
            return spot

        for column in range(2):
            orders = [order_of(2 * column), order_of(2 * column + 1)]
            weight_gradient(
                640, lambda i: active_t.at[layer, i, core], lambda i: active_far.at[layer, i],
                [(lambda column=column: low[0, :, column * 640 : column * 640 + 640],
                  lambda column=column: low[1, :, column * 640 : column * 640 + 640], 1.0,
                  [(0, orders[0], 0), (1, orders[1], 80)])],
            )
            send_item(orders[0], down_spot(0, column))
            send_item(orders[1], down_spot(1, column))
            yield

        def unit_of(i):
            return lax.rem(i + 5 * (1 - core), 10)

        def copies_down(i, slot):
            at = tile(unit_of(i), 512)
            return [
                pltpu.make_async_copy(down_full.at[layer, at, :], wide_w.at[slot], lsem.at[slot]),
                pltpu.make_async_copy(slopes.at[layer, :, at], slope_in.at[slot], lsem.at[slot]),
            ]

        def body_down(i, slot):
            unit = unit_of(i)
            at = tile(unit, 512)
            gh[:, :512] = dot(low[0], wide_w[slot], NT)

            @pl.loop(0, 8)
            def _(j):
                rows = tile(j, 64)
                small = (gh[rows, :512] * slope_in[slot, rows, :].astype(F32)).astype(BF16)
                gp[rows, at] = small
                sums[layer, pl.ds(8 + unit, 1), :512] += jnp.sum(small.astype(F32), axis=0, keepdims=True)

        streams(5, copies_down, body_down)
        swap = net.push(gp.at[:, pl.ds(pl.multiple_of((1 - core) * 2560, 128), 2560)], grad_pre_far.at[layer], to_core,
                        swapped)
        yield
        streams(5, lambda i, slot: copies_down(i + 5, slot), lambda i, slot: body_down(i + 5, slot))
        yield
        swap.wait()
        while layer == layers - 1 and returned:
            returned.pop().wait()
        fetch((grad_pre_far.at[layer], gs))

        def up_spot(unit):
            def spot(pc, pa, pb):
                return up_out.at[layer, pl.ds(pl.multiple_of((pa * 2 + pb) * 80, 16), 80),
                                 pl.ds(pl.multiple_of(pc * 2560 + unit * 640, 128), 640)]
            return spot

        def rows_of(values, i):
            return values.at[layer, pl.ds(pl.multiple_of(i * 320, 16), 320), :]

        for pair in range(2):
            orders = [order_of(4 + 2 * pair), order_of(5 + 2 * pair)]
            weight_gradient(
                320, lambda i: rows_of(hidden_t, i), lambda i: rows_of(hidden_far, i),
                [(lambda unit=unit: gp[:, pl.ds(pl.multiple_of(core * 2560 + unit * 640, 128), 640)],
                  lambda unit=unit: gs[:, unit * 640 : unit * 640 + 640], 1.0,
                  [(unit % 2, orders[unit % 2], 0)]) for unit in (2 * pair, 2 * pair + 1)],
            )
            send_item(orders[0], up_spot(2 * pair))
            send_item(orders[1], up_spot(2 * pair + 1))
            yield

        def copies_up(i, slot):
            return [
                pltpu.make_async_copy(up_full.at[layer, tile(i, 256), pl.ds(k * 512, 512)],
                                      big.at[pl.ds(pl.multiple_of(slot * 2560 + k * 256, 256), 256), :], lsem.at[slot])
                for k in range(10)
            ]

        def body_up(i, slot):
            total_ = None
            for k in range(10):
                part = dot(gp[:, k * 512 : k * 512 + 512],
                           big[pl.ds(pl.multiple_of(slot * 2560 + k * 256, 256), 256), :], NT)
                total_ = part if total_ is None else total_ + part
            gh[:, tile(i, 256)] = total_

        streams(5, copies_up, body_up)
        yield
        norm_back(middles.at[layer], vec[5:6, :], 5, layer, True)
        swap = net.push(low.at[0, :, pl.ds(pl.multiple_of((1 - core) * 640, 128), 640)], grad_o_far.at[layer], to_core,
                        swapped)
        yield

        def copies_out(i, slot):
            return [pltpu.make_async_copy(attn_full.at[layer, 3, tile(i, 256), :], wide_w.at[slot, pl.ds(0, 256), :],
                                          lsem.at[slot])]

        def body_out(i, slot):
            big[pl.ds(pl.multiple_of(3840 + i * 256, 256), 256), :] = dot(
                wide_w[slot, :256, :], low[0], NT).astype(BF16)

        streams(5, copies_out, body_out)
        swap.wait()
        fetch((grad_o_far.at[layer], low.at[1, :, pl.ds(0, 640)]), (lse_all.at[layer], lse))

        def small_spot(whole):
            def spot(pc, pa, pb):
                return whole.at[pl.ds(pl.multiple_of((pa * 2 + pb) * 80, 16), 80),
                                pl.ds(pl.multiple_of(pc * 640, 128), 640)]
            return spot

        weight_gradient(
            320, lambda i: rows_of(context_t, i), lambda i: rows_of(context_far, i),
            [(lambda: low[0, :, pl.ds(pl.multiple_of(core * 640, 128), 640)], lambda: low[1, :, :640], 1.0,
              [(0, order_of(8), 0)])],
        )
        send_item(order_of(8), small_spot(out_out.at[layer]))
        yield

        def copies_head(h, slot):
            at = pl.ds(pl.multiple_of(h * 80, 16), 80)
            return [
                pltpu.make_async_copy(qkv.at[layer, :, at, :], heads_in.at[slot, pl.ds(0, 3)], lsem.at[slot]),
                pltpu.make_async_copy(far.at[layer, :, at, :], heads_in.at[slot, pl.ds(3, 2)], lsem.at[slot]),
            ]

        def body_head(h, slot):
            at = pl.ds(pl.multiple_of(h * 80, 16), 80)
            at_k = pl.ds(pl.multiple_of(1280 + h * 80, 16), 80)
            at_v = pl.ds(pl.multiple_of(2560 + h * 80, 16), 80)
            query, norm = heads_in[slot, 0], lse[h]
            grad = big[pl.ds(pl.multiple_of(3840 + h * 80, 16), 80), :]
            halves, delta = [], None
            for k, v, mask, target in ((1, 2, 0, big.at[at_v, :]), (3, 4, 1, dfar.at[1, at, :])):
                p = jnp.exp(dot(heads_in[slot, k], query, TN) + masks[mask] - norm)
                dp = dot(heads_in[slot, v], grad, TN)
                part = jnp.sum(p * dp, axis=0, keepdims=True)
                delta = part if delta is None else delta + part
                target[...] = dot(grad, p.astype(BF16), NT).astype(BF16)
                halves.append((p, dp))
            total_ = None
            for (p, dp), k, target in zip(halves, (1, 3), (big.at[at_k, :], dfar.at[0, at, :])):
                ds = (p * (dp - delta)).astype(BF16)
                part = dot(heads_in[slot, k], ds)
                total_ = part if total_ is None else total_ + part
                target[...] = dot(query, ds, NT).astype(BF16)
            big[at, :] = total_.astype(BF16)

        swap = []
        for part in range(4):
            streams(4, lambda i, slot: copies_head(i + 4 * part, slot), lambda i, slot: body_head(i + 4 * part, slot))
            if part % 2 == 1:
                rows = pl.ds(320 * (2 * (part // 2)), 640)
                swap.append(net.push(dfar.at[:, rows, :], grad_kv_far.at[layer, :, rows, :], to_core,
                                     swapped_half.at[part // 2]))
            yield
        for copy in swap:
            copy.wait()

        def copies_far(i, slot):
            return [pltpu.make_async_copy(grad_kv_far.at[layer, :, tile(i, 128), :], far_in.at[slot], lsem.at[slot])]

        def body_far(i, slot):
            at = tile(i, 128)
            query = big[at, :].T
            gp[:, at] = query
            sums[layer, 20:21, at] = jnp.sum(query.astype(F32), axis=0, keepdims=True) * scale
            for which in range(2):
                rows = pl.ds(pl.multiple_of(1280 + which * 1280 + i * 128, 128), 128)
                both = (big[rows, :].astype(F32) + far_in[slot, which].astype(F32)).astype(BF16).T
                gp[:, pl.ds(pl.multiple_of(1280 + which * 1280 + i * 128, 128), 128)] = both
                if which == 1:
                    sums[layer, 21:22, at] = jnp.sum(both.astype(F32), axis=0, keepdims=True)

        streams(10, copies_far, body_far)
        swap = [
            net.push(gp.at[:, pl.ds(pl.multiple_of(t * 1280 + (1 - core) * 640, 128), 640)], grad_far.at[layer, t],
                     to_core, swapped)
            for t in range(3)
        ]
        yield

        def copies_back(i, slot):
            return [pltpu.make_async_copy(attn_full.at[layer, i // 5, tile(i % 5, 256), :],
                                          wide_w.at[slot, pl.ds(0, 256), :], lsem.at[slot])]

        def body_back(i, slot):
            at = tile(i % 5, 256)
            out = dot(gp[:, pl.ds(pl.multiple_of((i // 5) * 1280, 128), 1280)], wide_w[slot, :256, :], NT)

            @pl.when(i < 5)
            def _():
                gh[:, at] = out * scale

            @pl.when(i >= 5)
            def _():
                gh[:, at] += out

        streams(5, copies_back, body_back)
        for copy in swap:
            copy.wait()
        fetch(*[(grad_far.at[layer, t], gs.at[:, pl.ds(t * 640, 640)]) for t in range(3)])
        for group in ((0, 1), (2,)):
            weight_gradient(
                320, lambda i: rows_of(normed_t, i), lambda i: rows_of(normed_far, i),
                [(lambda t=t: gp[:, pl.ds(pl.multiple_of(t * 1280 + core * 640, 128), 640)],
                  lambda t=t: gs[:, t * 640 : t * 640 + 640], scale if t == 0 else 1.0,
                  [(t % 2, order_of(9 + t), 0)]) for t in group],
            )
            for t in group:
                send_item(order_of(9 + t), small_spot(qkv_out.at[layer, t]))
            yield
        streams(10, lambda i, slot: copies_back(i + 5, slot), lambda i, slot: body_back(i + 5, slot))
        yield
        norm_back(states.at[layer], vec[0:1, :], 18, layer, False)
        if layer == 0:
            returned.extend(give_back(low.at[0], grad_out, 2))
        yield

    sum_programs = [sum_program(0, 1, 0, 24), sum_program(1, 0, 0, 16), sum_program(2, 0, 16, 8)]
    segments = itertools.chain.from_iterable(work(layer) for layer in reversed(range(layers)))
    for action in PLAN:
        if action == -1:
            next(segments)
        elif action < 0:
            next(sum_programs[-2 - action])
        else:
            advance(action)
    for copy in returned:
        copy.wait()
    assert next(segments, None) is None and all(s == 7 for s in stage)
    net.drain()


def backward_all(cotangent, final, weights, kept, vectors, masks):
    any_ = pl.BlockSpec(memory_space=pl.ANY)
    vmem = pl.BlockSpec(memory_space=pltpu.VMEM)
    layers = vectors.shape[0]
    t = TOKENS

    def hbm(shape, dtype=BF16):
        return jax.ShapeDtypeStruct((layers,) + shape, dtype)

    out_shape = (
        jax.ShapeDtypeStruct(cotangent.shape, BF16), jax.ShapeDtypeStruct(cotangent.shape, BF16),
        hbm((1280, 1280)), hbm((320, 5120)), hbm((320, 1280)), hbm((3, 320, 1280)),
        hbm((24, 1280), F32),
        hbm((t, 1280)), hbm((t, 2560)), hbm((t, 640)), hbm((3, t, 640)), hbm((2, 1280, t)),
    )
    v = pltpu.VMEM
    items = ITEMS_A_LAYER * layers
    return pl.pallas_call(
        functools.partial(backward_kernel, layers),
        out_shape=out_shape,
        in_specs=[any_] * 19 + [vmem] * 2,
        out_specs=(any_,) * 6 + (vmem,) + (any_,) * 5,
        scratch_shapes=[
            v((t, 1280), F32), v((2, t, 1280), BF16), v((t, 5120), BF16), v((t, 2560), BF16), v((t, 1280), F32),
            v((2, 64, 1280), F32), v((5120, t), BF16), v((2, 1280, t), BF16), v((2, 5, 80, t), BF16), v((2, 2, 128, t), BF16),
            v((H, 1, t), F32), v((2, 512, 1280), BF16), v((2, t, 512), BF16), v((2, 2, 640, t), BF16),
            v((XRING, 2, 4, 2, 80, 640), BF16), v((RING, 4, 2, 80, 640), BF16), v((RING, 6, 80, 640), BF16),
            v((RING, 3, 80, 640), BF16), v((RING, 80, 640), BF16),
            v((layers, 4, 24, 1280), F32), v((layers, 6, 24, 1280), F32),
            pltpu.SemaphoreType.DMA, pltpu.SemaphoreType.DMA((2,)), pltpu.SemaphoreType.DMA,
            pltpu.SemaphoreType.DMA((2,)),
            pltpu.SemaphoreType.DMA((RING, 4)), pltpu.SemaphoreType.DMA((RING,)), pltpu.SemaphoreType.DMA((3, 4)),
            pltpu.SemaphoreType.DMA((4,)), pltpu.SemaphoreType.DMA((4,)), pltpu.SemaphoreType.DMA,
            pltpu.SemaphoreType.DMA((items * 12 + 16 * layers + 8,)),
        ],
        compiler_params=pltpu.CompilerParams(collective_id=2, has_side_effects=True, vmem_limit_bytes=63 << 20),
        name="backward_all",
    )(cotangent, final, *weights, *kept, vectors, masks)


def plane_shards(
    inputs, lengths, cotangent, attn_gain, attn_shift, query_weight, query_bias, key_weight,
    value_weight, value_bias, out_weight, out_bias, mlp_gain, mlp_shift, up_weight, up_bias,
    down_weight, down_bias,
):
    z = lax.axis_index("shard")
    layers = attn_gain.shape[0]
    rows = jnp.stack([attn_gain, attn_shift, query_bias, value_bias, out_bias, mlp_gain, mlp_shift, down_bias], axis=1)
    part = jnp.zeros((layers, 24, 1280), BF16)
    part = lax.dynamic_update_slice(part, rows, (0, 0, z * 320))
    wide = lax.dynamic_update_slice(jnp.zeros((layers, 5120), BF16), up_bias, (0, z * 1280)).reshape(layers, 10, 512)
    part = lax.dynamic_update_slice(part, wide, (0, 8, 0))
    spread = jnp.broadcast_to(lengths.astype(F32)[:, None, None], (2, 8, 128))
    results = forward_all(
        inputs, cotangent, (query_weight, key_weight, value_weight, out_weight, up_weight, down_weight), part, spread
    )
    weights, kept = results[:3], list(results[3:17])
    cotangent, final, table, masks = results[17:]
    kept[8] = kept[8].reshape(layers, 4, 2, 640, -1)
    output, grad, down_grad, up_grad, out_grad, qkv_grad, small = backward_all(
        cotangent, final, weights, kept, table, masks
    )[:7]
    input_grad = grad.astype(F32)
    small_rows = jnp.concatenate([small[:, 18:22], small[:, 4:8]], axis=1)
    sums = jnp.concatenate([small_rows.reshape(layers, -1), small[:, 8:18, :512].reshape(layers, -1)], axis=1)
    vec = pick(sums[:, :10240].reshape(layers, 8, 4, 320), z, 2)
    up_bias_grad = pick(sums[:, 10240:].reshape(layers, 4, 1280), z, 1)

    query_grad, key_grad, value_grad = [qkv_grad[:, i].astype(F32) for i in range(3)]
    out_grad, up_grad, down_grad = out_grad.astype(F32), up_grad.astype(F32), down_grad.astype(F32)
    return (
        output, input_grad, vec[:, 0], vec[:, 1], query_grad, vec[:, 2], key_grad, value_grad,
        vec[:, 3], out_grad, vec[:, 4], vec[:, 5], vec[:, 6], up_grad, up_bias_grad, down_grad,
        vec[:, 7],
    )


def pick_body(mesh):
    if mesh.shape["rep"] == 8 and mesh.shape["shard"] == 4:
        return plane_shards
    return general_shards


def solution(mesh):
    body = pick_body(mesh)
    placed = (
        P("rep", "shard", None),
        P("rep"),
        P("rep", "shard", None),
        P(None, "shard"),
        P(None, "shard"),
        P(None, "shard", None),
        P(None, "shard"),
        P(None, "shard", None),
        P(None, "shard", None),
        P(None, "shard"),
        P(None, "shard", None),
        P(None, "shard"),
        P(None, "shard"),
        P(None, "shard"),
        P(None, "shard", None),
        P(None, "shard"),
        P(None, "shard", None),
        P(None, "shard"),
    )
    return jax.shard_map(
        body,
        mesh=mesh,
        in_specs=placed,
        out_specs=(
            P("rep", "shard", None),
            P("rep", "shard", None),
            P(None, "shard"),
            P(None, "shard"),
            P(None, "shard", None),
            P(None, "shard"),
            P(None, "shard", None),
            P(None, "shard", None),
            P(None, "shard"),
            P(None, "shard", None),
            P(None, "shard"),
            P(None, "shard"),
            P(None, "shard"),
            P(None, "shard", None),
            P(None, "shard"),
            P(None, "shard", None),
            P(None, "shard"),
        ),
        check_vma=False,
    )
```

```python
import functools
import itertools
import math

import jax
import jax.numpy as jnp
from jax import lax
from jax.experimental import pallas as pl
from jax.experimental.pallas import tpu as pltpu
from jax.sharding import PartitionSpec as P

H = 16
EPSILON = 1e-05
NEGATIVE = -1e30
BF16 = jnp.bfloat16
F32 = jnp.float32
BOTH = ("rep", "shard")


def norm_affine(values, norm_gain, norm_shift):
    center = values - jnp.mean(values, axis=-1, keepdims=True)
    spread = jnp.mean(center * center, axis=-1, keepdims=True)
    return center * lax.rsqrt(spread + EPSILON) * norm_gain + norm_shift


def gelu_exact(values):
    return jax.nn.gelu(values, approximate=False)


def project(left_operand, right_operand):
    return jnp.einsum(
        "csa,ab->csb", left_operand, right_operand, preferred_element_type=jnp.float32
    )


def project_back(left_operand, right_operand):
    return jnp.einsum(
        "csb,ab->csa", left_operand, right_operand, preferred_element_type=jnp.float32
    )


def weight_grad(left_operand, right_operand):
    return jnp.einsum(
        "csa,csb->ab", left_operand, right_operand, preferred_element_type=jnp.float32
    )


def column_sum(values):
    return jnp.sum(values.astype(jnp.float32), axis=(0, 1))


def layer_slice(params, layer_index):
    return tuple((weight_array[layer_index] for weight_array in params))


def fetch_forward(local_params):
    return (
        lax.all_gather(local_params[0], "shard", axis=0, tiled=True),
        lax.all_gather(local_params[1], "shard", axis=0, tiled=True),
        lax.all_gather(local_params[2], "shard", axis=0, tiled=True),
        lax.all_gather(local_params[3], "shard", axis=0, tiled=True),
        lax.all_gather(local_params[4], "shard", axis=0, tiled=True),
        lax.all_gather(local_params[5], "shard", axis=0, tiled=True),
        lax.all_gather(local_params[6], "shard", axis=0, tiled=True),
        lax.all_gather(local_params[7], "shard", axis=0, tiled=True),
        lax.all_gather(local_params[8], "shard", axis=0, tiled=True),
        lax.all_gather(local_params[9], "shard", axis=0, tiled=True),
        lax.all_gather(local_params[10], "shard", axis=0, tiled=True),
        lax.all_gather(local_params[11], "shard", axis=0, tiled=True),
        lax.all_gather(local_params[12], "shard", axis=0, tiled=True),
        lax.all_gather(local_params[13], "shard", axis=0, tiled=True),
        lax.all_gather(local_params[14], "shard", axis=0, tiled=True),
    )


def fetch_again(local_params):
    return (
        lax.all_gather(local_params[0], "shard", axis=0, tiled=True),
        lax.all_gather(local_params[1], "shard", axis=0, tiled=True),
        lax.all_gather(local_params[2], "shard", axis=0, tiled=True),
        lax.all_gather(local_params[3], "shard", axis=0, tiled=True),
        lax.all_gather(local_params[4], "shard", axis=0, tiled=True),
        lax.all_gather(local_params[5], "shard", axis=0, tiled=True),
        lax.all_gather(local_params[6], "shard", axis=0, tiled=True),
        lax.all_gather(local_params[7], "shard", axis=0, tiled=True),
        lax.all_gather(local_params[8], "shard", axis=0, tiled=True),
        lax.all_gather(local_params[9], "shard", axis=0, tiled=True),
        lax.all_gather(local_params[10], "shard", axis=0, tiled=True),
        lax.all_gather(local_params[11], "shard", axis=0, tiled=True),
        lax.all_gather(local_params[12], "shard", axis=0, tiled=True),
        lax.all_gather(local_params[13], "shard", axis=0, tiled=True),
        lax.all_gather(local_params[14], "shard", axis=0, tiled=True),
    )


def forward_layer(hidden_state, weights, lengths):
    (
        attn_gain,
        attn_shift,
        query_weight,
        query_bias,
        key_weight,
        value_weight,
        value_bias,
        out_weight,
        out_bias,
        mlp_gain,
        mlp_shift,
        up_weight,
        up_bias,
        down_weight,
        down_bias,
    ) = weights
    clip_count, row_count, model_width = hidden_state.shape
    head_size = model_width // H
    query_scale = float(head_size) ** (-0.5)
    normed = norm_affine(
        hidden_state, attn_gain.astype(jnp.float32), attn_shift.astype(jnp.float32)
    ).astype(jnp.bfloat16)
    query_low = (
        (project(normed, query_weight) + query_bias.astype(jnp.float32)) * query_scale
    ).astype(jnp.bfloat16)
    key_low = project(normed, key_weight).astype(jnp.bfloat16)
    value_low = (project(normed, value_weight) + value_bias.astype(jnp.float32)).astype(
        jnp.bfloat16
    )
    key_all, value_all = (
        lax.all_gather(key_low, "shard", axis=1, tiled=True),
        lax.all_gather(value_low, "shard", axis=1, tiled=True),
    )
    length_all = key_all.shape[1]
    valid_keys = jnp.arange(length_all, dtype=jnp.int32)[None, :] < lengths[:, None]
    query_heads = query_low.reshape(clip_count, row_count, H, head_size)
    key_heads = key_all.reshape(clip_count, length_all, H, head_size)
    value_heads = value_all.reshape(clip_count, length_all, H, head_size)
    scores = jnp.einsum(
        "cqhd,ckhd->chqk", query_heads, key_heads, preferred_element_type=jnp.float32
    )
    scores = jnp.where(valid_keys[:, None, None, :], scores, NEGATIVE)
    attention = jax.nn.softmax(scores, axis=-1)
    attention_low = attention.astype(jnp.bfloat16)
    context = jnp.einsum(
        "chqk,ckhd->cqhd", attention_low, value_heads, preferred_element_type=jnp.float32
    )
    context_low = context.reshape(clip_count, row_count, model_width).astype(jnp.bfloat16)
    middle = hidden_state + project(context_low, out_weight) + out_bias.astype(jnp.float32)
    hidden_in = norm_affine(
        middle, mlp_gain.astype(jnp.float32), mlp_shift.astype(jnp.float32)
    ).astype(jnp.bfloat16)
    pre_gelu = project(hidden_in, up_weight) + up_bias.astype(jnp.float32)
    active_low = gelu_exact(pre_gelu).astype(jnp.bfloat16)
    result = middle + project(active_low, down_weight) + down_bias.astype(jnp.float32)
    kept_values = (
        normed,
        query_heads,
        key_heads,
        value_heads,
        attention,
        attention_low,
        context_low,
        middle,
        hidden_in,
        pre_gelu,
        active_low,
    )
    return (result, kept_values)


def backward_layer(hidden_state, grad_after, weights, lengths):
    (
        attn_gain,
        attn_shift,
        query_weight,
        query_bias,
        key_weight,
        value_weight,
        value_bias,
        out_weight,
        out_bias,
        mlp_gain,
        mlp_shift,
        up_weight,
        up_bias,
        down_weight,
        down_bias,
    ) = weights
    unused, kept_values = forward_layer(hidden_state, weights, lengths)
    (
        normed,
        query_heads,
        key_heads,
        value_heads,
        attention,
        attention_low,
        context_low,
        middle,
        hidden_in,
        pre_gelu,
        active_low,
    ) = kept_values
    clip_count, row_count, model_width = hidden_state.shape
    length_all = key_heads.shape[1]
    head_size = model_width // H
    query_scale = float(head_size) ** (-0.5)
    grad_low = grad_after.astype(jnp.bfloat16)
    grad_active = project_back(grad_low, down_weight)
    unused, gelu_pull = jax.vjp(gelu_exact, pre_gelu)
    grad_pre = gelu_pull(grad_active)[0].astype(jnp.bfloat16)
    grad_hidden = project_back(grad_pre, up_weight)
    unused, mlp_pull = jax.vjp(
        norm_affine, middle, mlp_gain.astype(jnp.float32), mlp_shift.astype(jnp.float32)
    )
    grad_middle_norm, grad_mlp_gain, grad_mlp_shift = mlp_pull(grad_hidden)
    grad_middle = grad_after + grad_middle_norm
    middle_low = grad_middle.astype(jnp.bfloat16)
    grad_context = project_back(middle_low, out_weight).astype(jnp.bfloat16)
    grad_context = grad_context.reshape(clip_count, row_count, H, head_size)
    grad_attention = jnp.einsum(
        "cqhd,ckhd->chqk", grad_context, value_heads, preferred_element_type=jnp.float32
    )
    value_part = jnp.einsum(
        "chqk,cqhd->ckhd", attention_low, grad_context, preferred_element_type=jnp.float32
    )
    grad_scores = attention * (
        grad_attention - jnp.sum(attention * grad_attention, axis=-1, keepdims=True)
    )
    scores_low = grad_scores.astype(jnp.bfloat16)
    grad_query = jnp.einsum(
        "chqk,ckhd->cqhd", scores_low, key_heads, preferred_element_type=jnp.float32
    )
    grad_query = grad_query.reshape(clip_count, row_count, model_width).astype(jnp.bfloat16)
    key_part = jnp.einsum(
        "chqk,cqhd->ckhd", scores_low, query_heads, preferred_element_type=jnp.float32
    )
    key_summed, value_summed = (
        lax.psum_scatter(
            key_part.reshape(clip_count, length_all, model_width).astype(jnp.bfloat16),
            "shard",
            scatter_dimension=1,
            tiled=True,
        ).astype(jnp.float32),
        lax.psum_scatter(
            value_part.reshape(clip_count, length_all, model_width).astype(jnp.bfloat16),
            "shard",
            scatter_dimension=1,
            tiled=True,
        ).astype(jnp.float32),
    )
    key_grad_low = key_summed.astype(jnp.bfloat16)
    value_grad_low = value_summed.astype(jnp.bfloat16)
    grad_normed = (
        project_back(grad_query, query_weight) * query_scale
        + project_back(key_grad_low, key_weight)
        + project_back(value_grad_low, value_weight)
    )
    unused, attn_pull = jax.vjp(
        norm_affine, hidden_state, attn_gain.astype(jnp.float32), attn_shift.astype(jnp.float32)
    )
    grad_input_norm, grad_attn_gain, grad_attn_shift = attn_pull(grad_normed)
    grad_before = grad_middle + grad_input_norm
    grad_down = weight_grad(active_low, grad_low)
    grad_down_bias = column_sum(grad_low)
    grad_up = weight_grad(hidden_in, grad_pre)
    grad_up_bias = column_sum(grad_pre)
    grad_out_weight = weight_grad(context_low, middle_low)
    grad_out_bias = column_sum(middle_low)
    grad_query_weight = weight_grad(normed, grad_query) * query_scale
    grad_query_bias = column_sum(grad_query) * query_scale
    grad_key_weight = weight_grad(normed, key_grad_low)
    grad_value_weight = weight_grad(normed, value_grad_low)
    grad_value_bias = column_sum(value_grad_low)
    owned_grads = (
        lax.psum_scatter(
            grad_attn_gain.astype(jnp.bfloat16), "shard", scatter_dimension=0, tiled=True
        ).astype(jnp.float32),
        lax.psum_scatter(
            grad_attn_shift.astype(jnp.bfloat16), "shard", scatter_dimension=0, tiled=True
        ).astype(jnp.float32),
        lax.psum_scatter(
            grad_query_weight.astype(jnp.bfloat16), "shard", scatter_dimension=0, tiled=True
        ).astype(jnp.float32),
        lax.psum_scatter(
            grad_query_bias.astype(jnp.bfloat16), "shard", scatter_dimension=0, tiled=True
        ).astype(jnp.float32),
        lax.psum_scatter(
            grad_key_weight.astype(jnp.bfloat16), "shard", scatter_dimension=0, tiled=True
        ).astype(jnp.float32),
        lax.psum_scatter(
            grad_value_weight.astype(jnp.bfloat16), "shard", scatter_dimension=0, tiled=True
        ).astype(jnp.float32),
        lax.psum_scatter(
            grad_value_bias.astype(jnp.bfloat16), "shard", scatter_dimension=0, tiled=True
        ).astype(jnp.float32),
        lax.psum_scatter(
            grad_out_weight.astype(jnp.bfloat16), "shard", scatter_dimension=0, tiled=True
        ).astype(jnp.float32),
        lax.psum_scatter(
            grad_out_bias.astype(jnp.bfloat16), "shard", scatter_dimension=0, tiled=True
        ).astype(jnp.float32),
        lax.psum_scatter(
            grad_mlp_gain.astype(jnp.bfloat16), "shard", scatter_dimension=0, tiled=True
        ).astype(jnp.float32),
        lax.psum_scatter(
            grad_mlp_shift.astype(jnp.bfloat16), "shard", scatter_dimension=0, tiled=True
        ).astype(jnp.float32),
        lax.psum_scatter(
            grad_up.astype(jnp.bfloat16), "shard", scatter_dimension=0, tiled=True
        ).astype(jnp.float32),
        lax.psum_scatter(
            grad_up_bias.astype(jnp.bfloat16), "shard", scatter_dimension=0, tiled=True
        ).astype(jnp.float32),
        lax.psum_scatter(
            grad_down.astype(jnp.bfloat16), "shard", scatter_dimension=0, tiled=True
        ).astype(jnp.float32),
        lax.psum_scatter(
            grad_down_bias.astype(jnp.bfloat16), "shard", scatter_dimension=0, tiled=True
        ).astype(jnp.float32),
    )
    return (grad_before, owned_grads)


def replica_layer(owned_grads):
    return (
        lax.psum(owned_grads[0].astype(jnp.bfloat16), "rep").astype(jnp.float32),
        lax.psum(owned_grads[1].astype(jnp.bfloat16), "rep").astype(jnp.float32),
        lax.psum(owned_grads[2].astype(jnp.bfloat16), "rep").astype(jnp.float32),
        lax.psum(owned_grads[3].astype(jnp.bfloat16), "rep").astype(jnp.float32),
        lax.psum(owned_grads[4].astype(jnp.bfloat16), "rep").astype(jnp.float32),
        lax.psum(owned_grads[5].astype(jnp.bfloat16), "rep").astype(jnp.float32),
        lax.psum(owned_grads[6].astype(jnp.bfloat16), "rep").astype(jnp.float32),
        lax.psum(owned_grads[7].astype(jnp.bfloat16), "rep").astype(jnp.float32),
        lax.psum(owned_grads[8].astype(jnp.bfloat16), "rep").astype(jnp.float32),
        lax.psum(owned_grads[9].astype(jnp.bfloat16), "rep").astype(jnp.float32),
        lax.psum(owned_grads[10].astype(jnp.bfloat16), "rep").astype(jnp.float32),
        lax.psum(owned_grads[11].astype(jnp.bfloat16), "rep").astype(jnp.float32),
        lax.psum(owned_grads[12].astype(jnp.bfloat16), "rep").astype(jnp.float32),
        lax.psum(owned_grads[13].astype(jnp.bfloat16), "rep").astype(jnp.float32),
        lax.psum(owned_grads[14].astype(jnp.bfloat16), "rep").astype(jnp.float32),
    )


def general_shards(
    inputs,
    lengths,
    cotangent,
    attn_gain,
    attn_shift,
    query_weight,
    query_bias,
    key_weight,
    value_weight,
    value_bias,
    out_weight,
    out_bias,
    mlp_gain,
    mlp_shift,
    up_weight,
    up_bias,
    down_weight,
    down_bias,
):
    params = (
        attn_gain,
        attn_shift,
        query_weight,
        query_bias,
        key_weight,
        value_weight,
        value_bias,
        out_weight,
        out_bias,
        mlp_gain,
        mlp_shift,
        up_weight,
        up_bias,
        down_weight,
        down_bias,
    )
    layers = attn_gain.shape[0]
    hidden_state = inputs.astype(jnp.float32)
    kept_inputs = []
    kept_weights = []
    for layer_index in range(layers):
        gathered = fetch_forward(layer_slice(params, layer_index))
        kept_inputs.append(hidden_state)
        kept_weights.append(gathered)
        hidden_state, unused = forward_layer(hidden_state, gathered, lengths)
    output = hidden_state.astype(jnp.bfloat16)
    row_count = inputs.shape[1]
    first_row = lax.axis_index("shard") * row_count
    positions = first_row + jnp.arange(row_count, dtype=jnp.int32)
    row_mask = (positions[None, :] < lengths[:, None]).astype(jnp.float32)
    grad_state = cotangent.astype(jnp.float32) * row_mask[:, :, None]
    owned_list = [None] * layers
    for layer_index in reversed(range(layers)):
        gathered = fetch_again(layer_slice(params, layer_index))
        grad_state, owned_grads = backward_layer(
            kept_inputs[layer_index], grad_state, gathered, lengths
        )
        owned_grads = replica_layer(owned_grads)
        owned_list[layer_index] = owned_grads
    stacked = tuple(
        (
            jnp.stack([owned_list[layer_index][member] for layer_index in range(layers)])
            for member in range(15)
        )
    )
    return (
        output,
        grad_state,
        stacked[0],
        stacked[1],
        stacked[2],
        stacked[3],
        stacked[4],
        stacked[5],
        stacked[6],
        stacked[7],
        stacked[8],
        stacked[9],
        stacked[10],
        stacked[11],
        stacked[12],
        stacked[13],
        stacked[14],
    )


def pick(values, index, axis=0):
    return lax.dynamic_index_in_dim(values, index, axis, keepdims=False)


def place():
    rep = lax.axis_index("rep")
    return rep // 4, (rep // 2) % 2, rep % 2, lax.axis_index("shard")


MESH = pl.DeviceIdType.MESH

def device(a, b, core, z):
    return ((a * 2 + b) * 2 + core, z)


class Net:
    def __init__(self, sent, arrived):
        self.sent, self.arrived = sent, arrived
        self.copies, self.some, self.count = [], [], 0
    def push(self, source, target_ref, target, sent=None):
        copy = pltpu.make_async_remote_copy(
            src_ref=source, dst_ref=target_ref, send_sem=self.sent if sent is None else sent,
            recv_sem=self.arrived.at[self.count], device_id=target, device_id_type=MESH)
        copy.start()
        self.count += 1
        if sent is None:
            self.copies.append(copy)
        return copy

    def push_if(self, wanted, source, target_ref, target, at=None):
        copy = pltpu.make_async_remote_copy(
            src_ref=source, dst_ref=target_ref, send_sem=self.sent,
            recv_sem=self.arrived.at[self.count if at is None else at], device_id=target, device_id_type=MESH)
        pl.when(wanted)(lambda: copy.start())
        if at is None:
            self.count += 1
        self.some.append((wanted, copy))
        return copy

    def drain(self):
        for copy in self.copies:
            copy.wait_send()
        for wanted, copy in self.some:
            pl.when(wanted)(lambda copy=copy: copy.wait_send())

def greet(targets, regroup=None):
    barrier = pltpu.get_barrier_semaphore()

    def signal(target):
        pl.semaphore_signal(barrier, inc=1, device_id=target, device_id_type=MESH)

    for target in targets:
        signal(target)
    if regroup is None:
        pl.semaphore_wait(barrier, len(targets))
        return
    stays, to, source, both = regroup
    for step in range(2):
        for target in (source[step], to[step]) if both else (source[step],):

            @pl.when(True if step else jnp.logical_not(stays))
            def _():
                signal(target)

    extra = 2 if both else 1

    @pl.when(stays)
    def _():
        pl.semaphore_wait(barrier, len(targets) + extra)

    @pl.when(jnp.logical_not(stays))
    def _():
        pl.semaphore_wait(barrier, len(targets) + 2 * extra)


def regrouping():
    a, b, core, z = place()
    to, source = [], []
    for step in range(2):
        to.append(device(a, b, z // 2, 2 * core + lax.rem(z + step, 2)))
        source.append(device(a, b, z // 2, 2 * core + lax.rem(z + step, 2)))
    return core == z // 2, to, source


class Swap:
    def __init__(self, net, source, target_ref, target, stays, sent, local):
        self.stays = stays
        self.far = pltpu.make_async_remote_copy(
            src_ref=source, dst_ref=target_ref, send_sem=sent, recv_sem=net.arrived.at[net.count],
            device_id=target, device_id_type=MESH)
        self.near = pltpu.make_async_copy(source, target_ref, local) if stays is not None else None
        net.count += 1

    def both(self, near, far):
        if self.stays is None:
            far()
            return
        pl.when(self.stays)(near)
        pl.when(jnp.logical_not(self.stays))(far)

    def start(self):
        self.both(lambda: self.near.start(), lambda: self.far.start())
        return self

    def wait(self):
        self.both(lambda: self.near.wait(), lambda: self.far.wait())

def gather_regions(index, zs, chip, core):
    part = chip * 2 + core
    def rows(base, size):
        return pl.ds(pl.multiple_of(base, 8), size)
    if index < 2:
        return 0, (pl.ds(2 * index, 2), rows(zs * 320 + part * 40, 40), slice(None))
    if index < 4:
        return 1, (rows(zs * 320 + part * 40, 40), pl.ds((index - 2) * 2560, 2560))
    return 2, (rows(zs * 1280 + part * 160 + (index - 4) * 80, 80), slice(None))


NN = (((1,), (0,)), ((), ()))
TN = (((0,), (0,)), ((), ()))
NT = (((1,), (1,)), ((), ()))
TOKENS = 512
ROOT_HALF = math.sqrt(0.5)
ROOT_TWO_PI = math.sqrt(2.0 * math.pi)

def dot(left, right, numbers=NN):
    return lax.dot_general(left, right, numbers, preferred_element_type=F32)


def tile(i, size):
    return pl.ds(pl.multiple_of(i * size, size), size)


def stream(count, copy, body):
    copy(0, 0).start()

    @pl.loop(0, count)
    def _(i):
        slot = i % 2

        @pl.when(i + 1 < count)
        def _():
            copy(i + 1, 1 - slot).start()

        copy(i, slot).wait()
        body(i, slot)


def transpose_into(target, source, rows):
    @pl.loop(0, rows // 128)
    def _(i):
        target[tile(i, 128), :] = source[:, tile(i, 128)].T


def gather_program(net, layers, shards, outs, copies, local):
    a, b, core, z = place()
    behind = [lax.rem(z + 4 - s, 4) for s in range(4)]
    to_z = [device(a, b, core, lax.rem(z + s, 4)) for s in range(4)]
    to_a, to_b, to_core = device(1 - a, b, core, z), device(a, 1 - b, core, z), device(a, b, 1 - core, z)
    count = 6 * layers
    twin = [[] for _ in range(count)]

    def refs_at(index, zs, pa, pb, whose):
        which, at = gather_regions(index % 6, zs, pa * 2 + pb, core)
        return whose[which].at[index // 6].at[at]

    starts = [None, z != 3, None, z != 0]
    inner = jnp.logical_and(z > 0, z < 3)
    to_end = device(a, b, core, jnp.where(z == 2, 3, 0))
    first_slot = {}

    def start(index):
        first_slot[index] = net.count
        layer, within = index // 6, index % 6
        pieces = [(refs_at(index, 0, a, b, shards), refs_at(index, z, a, b, outs))] if within > 1 else []
        if within < 2:
            here, there = [
                pl.ds(pl.multiple_of(zs * 320 + ((a * 2 + b) * 2 + core) * 40, 8), 40) for zs in (0, z)]
            pieces = [(shards[0][i].at[layer, here, :], outs[0].at[layer, i, there, :])
                      for i in (2 * within, 2 * within + 1)]
        return [
            [net.push(x, y, to_z[s]) if starts[s] is None else net.push_if(starts[s], x, y, to_z[s]) for x, y in pieces]
            for s in (1, 2, 3)
        ]

    def pass_on(index):
        within = index % 6
        if within > 1:
            refs = [refs_at(index, behind[2], a, b, outs)]
        else:
            rows = pl.ds(pl.multiple_of(behind[2] * 320 + ((a * 2 + b) * 2 + core) * 40, 8), 40)
            refs = [outs[0].at[index // 6, i, rows, :] for i in (2 * within, 2 * within + 1)]
        for i, ref in enumerate(refs):
            slot = first_slot[index] + i
            net.push_if(inner, ref, ref, to_end, jnp.where(z == 2, slot + 2 * len(refs), slot))

    def on(index, s, pa, pb, target):
        ref = refs_at(index, behind[s], pa, pb, outs)
        copy = net.push(ref, ref, target)
        if target is to_core:
            twin[index].append(copy)
        return copy

    storing = []

    def stored():
        for copy in storing:
            copy.wait()
        storing.clear()

    def own_copies(step):
        layer, which = step // 3, step % 3
        out = outs[which].at[layer]
        shard = shards[which].at[layer] if which else None
        ins, back = [], []
        for i in range(4):
            if which == 0:
                source, target = shards[0][i].at[layer], out.at[i, pl.ds(pl.multiple_of(z * 320, 8), 320), :]
            elif which == 1:
                source = shard.at[:, pl.ds(i * 1280, 1280)]
                target = out.at[pl.ds(pl.multiple_of(z * 320, 8), 320), pl.ds(i * 1280, 1280)]
            else:
                source = shard.at[pl.ds(i * 320, 320), :]
                target = out.at[pl.ds(pl.multiple_of(z * 1280 + i * 320, 8), 320), :]
            ins.append(pltpu.make_async_copy(source, copies.at[i], local))
            back.append(pltpu.make_async_copy(copies.at[i], target, local))
        stored()
        for copy in ins:
            copy.start()
        for copy in ins:
            copy.wait()
        for copy in back:
            copy.start()
        storing.extend(back)

    zed, mid, diag = {}, {}, {}
    zed[0] = start(0)
    zed[1] = start(1)
    own_copies(0)
    yield twin
    for t in range(count + 2):
        if t < count:
            mid[t] = {}
            for s in (2, 3, 1):
                for copy in zed[t][s - 1]:
                    copy.wait_recv()
                if s == 2:
                    pass_on(t)
                mid[t][s] = (on(t, s, a, b, to_b), on(t, s, a, b, to_a))
                on(t, s, a, b, to_core)
            if t + 2 < count:
                zed[t + 2] = start(t + 2)
        if 0 <= t - 1 < count:
            k = t - 1
            diag[k] = {}
            for s in (1, 2, 3):
                via_b, via_a = mid[k][s]
                via_b.wait_recv()
                on(k, s, a, 1 - b, to_core)
                if (s + k) % 2 == 0:
                    diag[k][s] = on(k, s, a, 1 - b, to_a)
                via_a.wait_recv()
                on(k, s, 1 - a, b, to_core)
                if (s + k) % 2 == 1:
                    diag[k][s] = on(k, s, 1 - a, b, to_b)
        if 0 <= t - 2 < count:
            k = t - 2
            for s in (1, 2, 3):
                diag[k][s].wait_recv()
                on(k, s, 1 - a, 1 - b, to_core)
        if t + 1 < 3 * layers:
            own_copies(t + 1)
        else:
            stored()
        yield twin


def normalize_rows(source, target, gain, shift, rows=64):
    @pl.loop(0, TOKENS // rows)
    def _(i):
        values = source[tile(i, rows), :]
        center = values - jnp.mean(values, axis=-1, keepdims=True)
        scale = lax.rsqrt(jnp.mean(center * center, axis=-1, keepdims=True) + EPSILON)
        target[tile(i, rows), :] = (center * scale * gain + shift).astype(BF16)


def attend_heads(first, last, query, key, value, far, masks, context, lse):
    @pl.loop(first, last)
    def _(h):
        at = pl.ds(pl.multiple_of(h * 80, 16), 80)
        q = query[at, :]
        s0 = dot(key[at, :], q, TN) + masks[0]
        s1 = dot(far[0, at, :], q, TN) + masks[1]
        top = jnp.maximum(jnp.max(s0, axis=0, keepdims=True), jnp.max(s1, axis=0, keepdims=True))
        e0, e1 = jnp.exp(s0 - top), jnp.exp(s1 - top)
        total = jnp.sum(e0, axis=0, keepdims=True) + jnp.sum(e1, axis=0, keepdims=True)
        out = dot(value[at, :], e0.astype(BF16)) + dot(far[1, at, :], e1.astype(BF16))
        context[at, :] = (out / total).astype(BF16)
        lse[h] = top + jnp.log(total)


def forward_kernel(layers, *refs):
    (tokens, cotangent, query_w, key_w, value_w, out_w, up, down, part, lengths,
     attn_full, up_full, down_full, keep_normed, keep_qkv, keep_far, keep_lse, keep_context, keep_middle,
     keep_hidden, keep_slope, keep_active, states, far_active, far_hidden, far_context, far_normed,
     cotangent_in, final, vectors, masks,
     state, middle, normed, normed_t, hidden_t, qkv, far, context_t, context, active, active_t, slope, lse,
     small_w, up_w, down_w, copies, product, parts_in, lengths_in,
     local, wsem, saved, swapped, handed, early, moved, stayed, sent, arrived) = refs
    a, b, core, z = place()
    to_core = device(a, b, 1 - core, z)
    to_z = [device(a, b, core, lax.rem(z + s, 4)) for s in (1, 2, 3)]
    stays, to, source = regrouping()
    greet(to_z + [device(1 - a, b, core, z), device(a, 1 - b, core, z), to_core], (stays, to, source, False))
    net = Net(sent, arrived)

    def regroup(values, targets, first):
        return [
            Swap(net, values.at[lax.rem(z + step, 2)], targets[step], to[step], None if step else stays,
                 moved.at[first + step], stayed.at[first]).start()
            for step in range(2)
        ]

    shared = [net.push(part, parts_in.at[i], to_z[i], early) for i in range(3)]
    shared.append(net.push(lengths, lengths_in, to_core, early))
    ticks = gather_program(net, layers, ((query_w, key_w, value_w, out_w), up, down), (attn_full, up_full, down_full),
                           copies, local)
    twin = next(ticks)
    clock = [-1]
    block = tokens.shape[1]
    next(ticks)
    tokens_here = regroup(tokens, [context.at[pl.ds(step * block, block), :] for step in range(2)], 0)
    next(ticks)
    next(ticks)
    clock[0] = 2
    for copy in shared:
        copy.wait()

    @pl.loop(0, layers)
    def _(i):
        total_ = part[i].astype(F32)
        for j in range(3):
            total_ = total_ + parts_in[j, i].astype(F32)
        vectors[i] = total_

    which = lax.rem(z, 2)
    length = jnp.where(z // 2 == core, lengths[which], lengths_in[which])[0:1, 0:1]
    for i in range(2):
        owner = core if i == 0 else 1 - core
        for step in range(2):
            first = (2 * owner + lax.rem(z + step, 2)) * block
            at = (lax.broadcasted_iota(jnp.int32, (block, 1), 0) + first).astype(F32)
            masks[i, step * block : (step + 1) * block, :] = jnp.where(at < length, 0.0, NEGATIVE)
    for copy in tokens_here:
        copy.wait()

    @pl.loop(0, 8)
    def _(i):
        state[tile(i, 64), :] = context[tile(i, 64), :].astype(F32)

    def pump(until):
        while clock[0] < until:
            next(ticks)
            clock[0] += 1

    def ready(*chunks):
        pump(max(chunks) + 2)
        for chunk in chunks:
            for copy in twin[chunk]:
                copy.wait_recv()

    saves = []

    def save(source, target):
        copy = pltpu.make_async_copy(source, target, saved)
        copy.start()
        saves.append(copy)

    given, taken = [], []

    def hand(source, target):
        copy = net.push(source, target, to_core, handed)
        given.append(copy)
        taken.append(copy)

    scale = float(80) ** (-0.5)
    for layer in range(layers):
        base = 6 * layer
        for copy in given:
            copy.wait_send()
        given.clear()
        vec = vectors.at[layer]

        def row(i):
            return vec[i : i + 1, :]

        weights = attn_full.at[layer]
        save(state, states.at[layer])
        normalize_rows(state, normed, row(0), row(1))
        transpose_into(normed_t, normed, 1280)
        save(normed_t, keep_normed.at[layer])
        hand(normed_t, far_normed.at[layer])
        ready(base, base + 1)

        def project(which, bias, factor, target):
            def copy(i, slot):
                return pltpu.make_async_copy(weights.at[which, :, tile(i, 256)], small_w.at[slot], wsem.at[slot])

            def body(i, slot):
                out = dot(normed[...], small_w[slot])
                if bias is not None:
                    out = out + vec[bias : bias + 1, tile(i, 256)]
                if factor != 1.0:
                    out = out * factor
                target[tile(i, 256), :] = out.astype(BF16).T

            stream(5, copy, body)

        project(1, None, 1.0, qkv.at[1])
        project(2, 3, 1.0, qkv.at[2])
        swap = net.push(qkv.at[pl.ds(1, 2)], far.at[layer], to_core, swapped)
        project(0, 2, scale, qkv.at[0])
        pump(base + 4)
        swap.wait()
        for part in range(4):
            if part == 2:
                pump(base + 5)
                if layer == layers - 1:
                    cotangent_at = [copies.at[step, pl.ds(0, block), :] for step in range(2)]
                    cotangent_here = regroup(cotangent, cotangent_at, 2)
            attend_heads(4 * part, 4 * part + 4, qkv.at[0], qkv.at[1], qkv.at[2], far.at[layer], masks, context_t, lse)
        save(qkv, keep_qkv.at[layer])
        save(far.at[layer], keep_far.at[layer])
        save(lse, keep_lse.at[layer])
        save(context_t, keep_context.at[layer])
        hand(context_t, far_context.at[layer])

        @pl.loop(0, 10)
        def _(i):
            context[:, tile(i, 128)] = context_t[tile(i, 128), :].T

        def copy_out(i, slot):
            return pltpu.make_async_copy(weights.at[3, :, tile(i, 256)], small_w.at[slot], wsem.at[slot])

        def body_out(i, slot):
            at = tile(i, 256)
            middle[:, at] = state[:, at] + dot(context[...], small_w[slot]) + vec[4:5, at]

        stream(5, copy_out, body_out)
        save(middle, keep_middle.at[layer])
        normalize_rows(middle, normed, row(5), row(6))
        transpose_into(hidden_t, normed, 1280)
        save(hidden_t, keep_hidden.at[layer])
        hand(hidden_t, far_hidden.at[layer])
        pump(base + 6)
        ready(base + 2, base + 3)

        def copy_up(i, slot):
            return pltpu.make_async_copy(up_full.at[layer, :, tile(i, 512)], up_w.at[slot], wsem.at[slot])

        def body_up(i, slot):
            at = tile(i, 512)
            product[...] = dot(normed[...], up_w[slot])
            bias = vec[pl.ds(8 + i, 1), :512]

            @pl.loop(0, 16)
            def _(j):
                u = product[tile(j, 32), :] + bias
                half = 0.5 * (1.0 + lax.erf(u * ROOT_HALF))
                active[tile(j, 32), at] = (u * half).astype(BF16)
                slope[tile(j, 32), at] = (half + u * jnp.exp(-0.5 * u * u) * (1.0 / ROOT_TWO_PI)).astype(BF16)

            active_t[at, :] = active[:, at].T

        stream(10, copy_up, body_up)
        save(slope, keep_slope.at[layer])
        save(active_t, keep_active.at[layer])
        for i in range(4):
            rows = pl.ds(pl.multiple_of(i * 1280 + (1 - core) * 640, 128), 640)
            hand(active_t.at[rows, :], far_active.at[layer, i])
        ready(base + 4, base + 5)

        def copy_down(i, slot):
            return pltpu.make_async_copy(down_full.at[layer, :, tile(i, 256)], down_w.at[slot], wsem.at[slot])

        for copy in saves:
            copy.wait()
        saves.clear()

        def body_down(i, slot):
            at = tile(i, 256)
            state[:, at] = middle[:, at] + dot(active[...], down_w[slot]) + vec[7:8, at]

        stream(5, copy_down, body_down)

    @pl.loop(0, 8)
    def _(i):
        normed[tile(i, 64), :] = state[tile(i, 64), :].astype(BF16)

    for copy in cotangent_here:
        copy.wait()
    save(normed, final)
    for step in range(2):
        save(cotangent_at[step], cotangent_in.at[step])
    for copy in saves:
        copy.wait()
    for copy in given:
        copy.wait_send()
    for copy in taken:
        copy.wait_recv()
    net.drain()


def forward_all(tokens, cotangent, shards, part, lengths):
    any_ = pl.BlockSpec(memory_space=pl.ANY)
    vmem = pl.BlockSpec(memory_space=pltpu.VMEM)
    layers = part.shape[0]
    t = TOKENS

    def hbm(shape, dtype=BF16):
        return jax.ShapeDtypeStruct((layers,) + shape, dtype)

    out_shape = (
        hbm((4, 1280, 1280)), hbm((1280, 5120)), hbm((5120, 1280)),
        hbm((1280, t)), hbm((3, 1280, t)), hbm((2, 1280, t)), hbm((H, 1, t), F32), hbm((1280, t)), hbm((t, 1280), F32),
        hbm((1280, t)), hbm((t, 5120)), hbm((5120, t)), hbm((t, 1280), F32),
        hbm((4, 640, t)), hbm((1280, t)), hbm((1280, t)), hbm((1280, t)),
        jax.ShapeDtypeStruct(tokens.shape, BF16), jax.ShapeDtypeStruct((t, 1280), BF16), hbm((24, 1280), F32), jax.ShapeDtypeStruct((2, t, 1), F32),
    )
    v = pltpu.VMEM
    return pl.pallas_call(
        functools.partial(forward_kernel, layers),
        out_shape=out_shape,
        in_specs=[any_] * 8 + [vmem] * 2,
        out_specs=(any_,) * (len(out_shape) - 2) + (vmem,) * 2,
        scratch_shapes=[
            v((t, 1280), F32), v((t, 1280), F32), v((t, 1280), BF16), v((1280, t), BF16), v((1280, t), BF16),
            v((3, 1280, t), BF16), v((layers, 2, 1280, t), BF16), v((1280, t), BF16), v((t, 1280), BF16),
            v((t, 5120), BF16), v((5120, t), BF16), v((t, 5120), BF16), v((H, 1, t), F32),
            v((2, 1280, 256), BF16), v((2, 1280, 512), BF16), v((2, 5120, 256), BF16), v((4, 320, 1280), BF16),
            v((t, 512), F32), v((3,) + part.shape, BF16), v(lengths.shape, F32),
            pltpu.SemaphoreType.DMA, pltpu.SemaphoreType.DMA((2,)), pltpu.SemaphoreType.DMA,
            pltpu.SemaphoreType.DMA, pltpu.SemaphoreType.DMA, pltpu.SemaphoreType.DMA,
            pltpu.SemaphoreType.DMA((4,)), pltpu.SemaphoreType.DMA((4,)), pltpu.SemaphoreType.DMA,
            pltpu.SemaphoreType.DMA((6 * layers * 24 + 14 * layers + 8,)),
        ],
        compiler_params=pltpu.CompilerParams(collective_id=1, has_side_effects=True, vmem_limit_bytes=63 << 20),
        name="forward_all",
    )(tokens, cotangent, *shards, part, lengths)


def add(*parts):
    total = parts[0].astype(F32)
    for part in parts[1:]:
        total = total + part.astype(F32)
    return total.astype(BF16)


ITEMS_A_LAYER = 12
RING, XRING = 10, 4
ORDERS = ("azb", "baz", "abz", "bza", "azb", "baz", "abz", "bza", "azb", "baz", "abz", "bza")
PLAN = (
    -1, -1, -1, -1, -1, 0, 1, -1, 2, 3, -1, 0, 1, -1, -1, 4, 5, 2, 3, -1, -1, -1, 6, 7, 4, 5, 0, 1, -1, 2, 6,
    3, -1, 4, -1, 8, 7, 0, 1, 2, -1, 5, 3, 4, 0, 1, 2, -1, -1, 6, 7, 0, 1, 2, -1, -1, 9, 10, 8, 5, 3, 4, -1,
    3, 4, 9, 5, 11, 5, -1, 6, 7, -1, 10, -1, 12, 11, 8, 9, 13, 14, 10, -1, 11, 15, 12, 13, 6, 7, 8, 6, 7, 9,
    -1, -1, 16, 14, 15, 10, -1, -1, 17, -1, 18, 12, 13, 11, 8, 9, -1, 16, 8, 9, -1, 19, 20, 14, 15, 10, -1,
    17, 18, 12, 10, -1, 16, 13, 14, 11, -1, 19, 15, 16, 12, 13, 14, 11, -1, 12, -1, 13, 14, -1, -4, -3, -2,
    20, 17, 21, 22, 15, 16, 15, -4, -3, -2, 16, 18, 19, 21, 23, 20, 17, 21, -4, -3, -2, 17, 17, 22, 18, 19,
    20, 21, 18, -4, -3, -2, 19, 23, 20, 21, 18, 19, 20, 21, 22, 23, 22, 23, 22, 23, 22, -4, -3, -2, 23
)


def streams(count, copies, body):
    for copy in copies(0, 0):
        copy.start()

    @pl.loop(0, count)
    def _(i):
        slot = i % 2

        @pl.when(i + 1 < count)
        def _():
            for copy in copies(i + 1, 1 - slot):
                copy.start()

        for copy in copies(i, slot):
            copy.wait()
        body(i, slot)


def add_blocks(blocks, target, parts):
    @pl.loop(0, blocks * 5)
    def _(i):
        block = i // 5
        at = pl.ds(pl.multiple_of((i % 5) * 16, 16), 16)
        refs = [part(block) for part in parts]
        sums = refs[0][at, :].astype(F32)
        for ref in refs[1:]:
            sums = sums + ref[at, :].astype(F32)
        target(block)[at, :] = sums.astype(BF16)


def backward_kernel(layers, *refs):
    (cotangent, final, attn_full, up_full, down_full, normed_t, qkv, far, lse_all, context_t, middles, hidden_t, slopes,
     active_t, states, active_far, hidden_far, context_far, normed_far, vectors, masks,
     output, grad_out, down_out, up_out, out_out, qkv_out, sums,
     grad_f_far, grad_pre_far, grad_o_far, grad_far, grad_kv_far,
     g, low, gp, gs, gh, rows_in, big, dfar, heads_in, far_in, lse, wide_w, slope_in, left_in,
     xs, got1s, got2s, got3s, finals, sums_held, sums_in,
     local, lsem, swapped, swapped_half, item_sent, item_local, sums_sent, moved, stayed,
     sent, arrived) = refs
    a, b, core, z = place()
    to_z = [device(a, b, core, lax.rem(z + s, 4)) for s in range(4)]
    to_a, to_b, to_core = device(1 - a, b, core, z), device(a, 1 - b, core, z), device(a, b, 1 - core, z)
    stays, to, source = regrouping()
    greet(to_z[1:] + [to_a, to_b, to_core], (stays, to, source, False))
    net = Net(sent, arrived)
    scale = float(80) ** (-0.5)
    side = {"a": (a, to_a), "b": (b, to_b)}

    def program(number, order, spot):
        slot = number % RING
        x, got1, got2, got3, final = (
            xs.at[number % XRING], got1s.at[slot], got2s.at[slot], got3s.at[slot], finals.at[slot])
        target = side[order[0]][1]
        other, other_target = side["b" if order[0] == "a" else "a"]

        def push(source, target_ref, target, stage):
            return net.push(source, target_ref, target, item_sent.at[slot, stage])

        first = push(x.at[1], got1, target, 0)
        yield
        first.wait()
        add_blocks(8, lambda i: got1.at[i // 2, i % 2],
                   [lambda i: got1.at[i // 2, i % 2], lambda i: x.at[0, i // 2, i % 2]])
        if order[1] == "z":
            nexts = [push(got1.at[lax.rem(z + s, 4)], got2.at[pl.ds(2 * s - 2, 2)], to_z[s], 1) for s in (1, 2, 3)]
        else:
            nexts = [push(got1.at[:, 1 - other], got2.at[pl.ds(0, 4)], other_target, 1)]
        yield
        for copy in nexts:
            copy.wait()
        if order[1] == "z":
            add_blocks(2, lambda i: got1.at[z, i],
                       [lambda i: got1.at[z, i]] + [lambda i, s=s: got2.at[2 * s + i] for s in range(3)])
            nexts = [push(got1.at[z, 1 - other], got3.at[0], other_target, 2)]
        else:
            add_blocks(4, lambda i: got2.at[i], [lambda i: got2.at[i], lambda i: got1.at[i, other]])
            nexts = [push(got2.at[lax.rem(z + s, 4)], got3.at[s - 1], to_z[s], 2) for s in (1, 2, 3)]
        yield
        for copy in nexts:
            copy.wait()
        if order[1] == "z":
            add_blocks(1, lambda i: final, [lambda i: got1.at[z, other], lambda i: got3.at[0]])
        else:
            add_blocks(1, lambda i: final, [lambda i: got2.at[z]] + [lambda i, s=s: got3.at[s] for s in range(3)])
        mine = pltpu.make_async_copy(final, spot(core, a, b), item_local.at[slot])
        mine.start()
        via = [push(final, spot(core, a, b), target, 3) for target in (to_a, to_b, to_core)]
        yield
        mine.wait()
        for copy in via:
            copy.wait()

        def on(pa, pb, target):
            return net.push(spot(core, pa, pb), spot(core, pa, pb), target)

        diag = on(1 - a, b, to_b) if number % 2 == 0 else on(a, 1 - b, to_a)
        twin = [on(1 - a, b, to_core), on(a, 1 - b, to_core)]
        yield
        diag.wait_recv()
        twin.append(on(1 - a, 1 - b, to_core))
        yield
        for copy in twin:
            copy.wait_recv()
        yield

    programs, stage = [], []

    def advance(number):
        next(programs[number])
        stage[number] += 1

    def send_item(order, spot):
        number = len(programs)
        assert all(s > 4 for s in stage[: max(0, number + 1 - RING)])
        programs.append(program(number, order, spot))
        stage.append(0)
        advance(number)

    def weight_gradient(height, own, far_, parts):
        base = len(programs)
        count = sum(len(part[3]) for part in parts)
        assert all(s > 1 for s in stage[: max(0, base + count - XRING)])

        def copies(i, slot):
            return [
                pltpu.make_async_copy(own(i), left_in.at[slot, 0, pl.ds(0, height), :], lsem.at[slot]),
                pltpu.make_async_copy(far_(i), left_in.at[slot, 1, pl.ds(0, height), :], lsem.at[slot]),
            ]

        def body(i, slot):
            for right, far_right, factor, targets in parts:
                out = dot(left_in[slot, 0, :height, :], right()) + dot(left_in[slot, 1, :height, :], far_right())
                if factor != 1.0:
                    out = out * factor
                out = out.astype(BF16)
                for item, order, first in targets:
                    x = xs.at[(base + item) % XRING]
                    for pa in range(2):
                        for pb in range(2):
                            row = (pa * 2 + pb) * (height // 4) + first
                            block = out[row : row + 80, :]
                            if order[0] == "a":
                                x[lax.rem(pa + a, 2), i, pb] = block
                            else:
                                x[lax.rem(pb + b, 2), i, pa] = block

        streams(4, copies, body)

    def fetch(*pairs):
        copies = [pltpu.make_async_copy(x, y, local) for x, y in pairs]
        for copy in copies:
            copy.start()
        for copy in copies:
            copy.wait()

    def norm_back(source, gain, gain_at, layer, lowered):
        def copies(i, slot):
            return [pltpu.make_async_copy(source.at[tile(i, 64), :], rows_in.at[slot], lsem.at[slot])]

        def body(i, slot):
            at = tile(i, 64)
            values = rows_in[slot]
            center = values - jnp.mean(values, axis=-1, keepdims=True)
            s = lax.rsqrt(jnp.mean(center * center, axis=-1, keepdims=True) + EPSILON)
            unit = center * s
            grad = gh[at, :]
            e = grad * gain
            out = g[at, :] + s * (
                e - jnp.mean(e, axis=-1, keepdims=True) - unit * jnp.mean(e * unit, axis=-1, keepdims=True))
            g[at, :] = out
            sums[layer, pl.ds(gain_at, 1), :] += jnp.sum(grad * unit, axis=0, keepdims=True)
            sums[layer, pl.ds(gain_at + 1, 1), :] += jnp.sum(grad, axis=0, keepdims=True)
            small = out.astype(BF16)
            if lowered or layer == 0:
                low[0, at, :] = small
            if lowered:
                sums[layer, pl.ds(4, 1), :] += jnp.sum(small.astype(F32), axis=0, keepdims=True)

        streams(8, copies, body)

    block = cotangent.shape[1]

    def give_back(values, target, first):
        return [
            Swap(net, values.at[pl.ds(step * block, block), :], target.at[lax.rem(z, 2)], to[step], None if step else stays,
                 moved.at[first + step], stayed.at[first]).start()
            for step in range(2)
        ]

    held = gs.at[:, pl.ds(0, 1280)]
    fetch((final, held))
    returned = give_back(held, output, 0)
    fetch(*[(cotangent.at[step], low.at[0, pl.ds(step * block, block), :]) for step in range(2)])

    @pl.loop(0, 8)
    def _(i):
        at = tile(i, 64)
        g[at, :] = jnp.where(masks[0, at, :] == 0.0, low[0, at, :].astype(F32), 0.0)

    sums[...] = jnp.zeros_like(sums)

    def sum_program(which, layer, first, size):
        rows = pl.ds(first, size)
        steps = [[to_core], [to_b], [to_a], to_z[1:]]
        sums_held[layer, 0, rows, :] = sums[layer, rows, :]
        place_in = 0
        for number, targets in enumerate(steps):
            copies = [
                net.push(sums_held.at[layer, number, rows], sums_in.at[layer, place_in + i, rows], target,
                         sums_sent.at[which, number])
                for i, target in enumerate(targets)
            ]
            yield
            for copy in copies:
                copy.wait()
            all_ = sums_held[layer, number, rows, :]
            for i in range(len(targets)):
                all_ = all_ + sums_in[layer, place_in + i, rows, :]
            place_in += len(targets)
            if number < 3:
                sums_held[layer, number + 1, rows, :] = all_
            else:
                sums[layer, rows, :] = all_
        yield

    def work(layer):
        vec = vectors.at[layer]
        first_item = ITEMS_A_LAYER * (layers - 1 - layer)

        def order_of(item):
            return ORDERS[item]

        @pl.loop(0, 8)
        def _(i):
            at = tile(i, 64)
            small = g[at, :].astype(BF16)
            low[0, at, :] = small
            sums[layer, pl.ds(7, 1), :] += jnp.sum(small.astype(F32), axis=0, keepdims=True)

        swap = net.push(low.at[0], grad_f_far.at[layer], to_core, swapped)
        yield
        swap.wait()
        fetch((grad_f_far.at[layer], low.at[1]))

        def down_spot(half, column):
            def spot(pc, pa, pb):
                row = pc * 640 + (pa * 2 + pb) * 160 + half * 80
                return down_out.at[layer, pl.ds(pl.multiple_of(row, 16), 80), pl.ds(column * 640, 640)]
            return spot

        for column in range(2):
            orders = [order_of(2 * column), order_of(2 * column + 1)]
            weight_gradient(
                640, lambda i: active_t.at[layer, i, core], lambda i: active_far.at[layer, i],
                [(lambda column=column: low[0, :, column * 640 : column * 640 + 640],
                  lambda column=column: low[1, :, column * 640 : column * 640 + 640], 1.0,
                  [(0, orders[0], 0), (1, orders[1], 80)])],
            )
            send_item(orders[0], down_spot(0, column))
            send_item(orders[1], down_spot(1, column))
            yield

        def unit_of(i):
            return lax.rem(i + 5 * (1 - core), 10)

        def copies_down(i, slot):
            at = tile(unit_of(i), 512)
            return [
                pltpu.make_async_copy(down_full.at[layer, at, :], wide_w.at[slot], lsem.at[slot]),
                pltpu.make_async_copy(slopes.at[layer, :, at], slope_in.at[slot], lsem.at[slot]),
            ]

        def body_down(i, slot):
            unit = unit_of(i)
            at = tile(unit, 512)
            gh[:, :512] = dot(low[0], wide_w[slot], NT)

            @pl.loop(0, 8)
            def _(j):
                rows = tile(j, 64)
                small = (gh[rows, :512] * slope_in[slot, rows, :].astype(F32)).astype(BF16)
                gp[rows, at] = small
                sums[layer, pl.ds(8 + unit, 1), :512] += jnp.sum(small.astype(F32), axis=0, keepdims=True)

        streams(5, copies_down, body_down)
        swap = net.push(gp.at[:, pl.ds(pl.multiple_of((1 - core) * 2560, 128), 2560)], grad_pre_far.at[layer], to_core,
                        swapped)
        yield
        streams(5, lambda i, slot: copies_down(i + 5, slot), lambda i, slot: body_down(i + 5, slot))
        yield
        swap.wait()
        while layer == layers - 1 and returned:
            returned.pop().wait()
        fetch((grad_pre_far.at[layer], gs))

        def up_spot(unit):
            def spot(pc, pa, pb):
                return up_out.at[layer, pl.ds(pl.multiple_of((pa * 2 + pb) * 80, 16), 80),
                                 pl.ds(pl.multiple_of(pc * 2560 + unit * 640, 128), 640)]
            return spot

        def rows_of(values, i):
            return values.at[layer, pl.ds(pl.multiple_of(i * 320, 16), 320), :]

        for pair in range(2):
            orders = [order_of(4 + 2 * pair), order_of(5 + 2 * pair)]
            weight_gradient(
                320, lambda i: rows_of(hidden_t, i), lambda i: rows_of(hidden_far, i),
                [(lambda unit=unit: gp[:, pl.ds(pl.multiple_of(core * 2560 + unit * 640, 128), 640)],
                  lambda unit=unit: gs[:, unit * 640 : unit * 640 + 640], 1.0,
                  [(unit % 2, orders[unit % 2], 0)]) for unit in (2 * pair, 2 * pair + 1)],
            )
            send_item(orders[0], up_spot(2 * pair))
            send_item(orders[1], up_spot(2 * pair + 1))
            yield

        def copies_up(i, slot):
            return [
                pltpu.make_async_copy(up_full.at[layer, tile(i, 256), pl.ds(k * 512, 512)],
                                      big.at[pl.ds(pl.multiple_of(slot * 2560 + k * 256, 256), 256), :], lsem.at[slot])
                for k in range(10)
            ]

        def body_up(i, slot):
            total_ = None
            for k in range(10):
                part = dot(gp[:, k * 512 : k * 512 + 512],
                           big[pl.ds(pl.multiple_of(slot * 2560 + k * 256, 256), 256), :], NT)
                total_ = part if total_ is None else total_ + part
            gh[:, tile(i, 256)] = total_

        streams(5, copies_up, body_up)
        yield
        norm_back(middles.at[layer], vec[5:6, :], 5, layer, True)
        swap = net.push(low.at[0, :, pl.ds(pl.multiple_of((1 - core) * 640, 128), 640)], grad_o_far.at[layer], to_core,
                        swapped)
        yield

        def copies_out(i, slot):
            return [pltpu.make_async_copy(attn_full.at[layer, 3, tile(i, 256), :], wide_w.at[slot, pl.ds(0, 256), :],
                                          lsem.at[slot])]

        def body_out(i, slot):
            big[pl.ds(pl.multiple_of(3840 + i * 256, 256), 256), :] = dot(
                wide_w[slot, :256, :], low[0], NT).astype(BF16)

        streams(5, copies_out, body_out)
        swap.wait()
        fetch((grad_o_far.at[layer], low.at[1, :, pl.ds(0, 640)]), (lse_all.at[layer], lse))

        def small_spot(whole):
            def spot(pc, pa, pb):
                return whole.at[pl.ds(pl.multiple_of((pa * 2 + pb) * 80, 16), 80),
                                pl.ds(pl.multiple_of(pc * 640, 128), 640)]
            return spot

        weight_gradient(
            320, lambda i: rows_of(context_t, i), lambda i: rows_of(context_far, i),
            [(lambda: low[0, :, pl.ds(pl.multiple_of(core * 640, 128), 640)], lambda: low[1, :, :640], 1.0,
              [(0, order_of(8), 0)])],
        )
        send_item(order_of(8), small_spot(out_out.at[layer]))
        yield

        def copies_head(h, slot):
            at = pl.ds(pl.multiple_of(h * 80, 16), 80)
            return [
                pltpu.make_async_copy(qkv.at[layer, :, at, :], heads_in.at[slot, pl.ds(0, 3)], lsem.at[slot]),
                pltpu.make_async_copy(far.at[layer, :, at, :], heads_in.at[slot, pl.ds(3, 2)], lsem.at[slot]),
            ]

        def body_head(h, slot):
            at = pl.ds(pl.multiple_of(h * 80, 16), 80)
            at_k = pl.ds(pl.multiple_of(1280 + h * 80, 16), 80)
            at_v = pl.ds(pl.multiple_of(2560 + h * 80, 16), 80)
            query, norm = heads_in[slot, 0], lse[h]
            grad = big[pl.ds(pl.multiple_of(3840 + h * 80, 16), 80), :]
            halves, delta = [], None
            for k, v, mask, target in ((1, 2, 0, big.at[at_v, :]), (3, 4, 1, dfar.at[1, at, :])):
                p = jnp.exp(dot(heads_in[slot, k], query, TN) + masks[mask] - norm)
                dp = dot(heads_in[slot, v], grad, TN)
                part = jnp.sum(p * dp, axis=0, keepdims=True)
                delta = part if delta is None else delta + part
                target[...] = dot(grad, p.astype(BF16), NT).astype(BF16)
                halves.append((p, dp))
            total_ = None
            for (p, dp), k, target in zip(halves, (1, 3), (big.at[at_k, :], dfar.at[0, at, :])):
                ds = (p * (dp - delta)).astype(BF16)
                part = dot(heads_in[slot, k], ds)
                total_ = part if total_ is None else total_ + part
                target[...] = dot(query, ds, NT).astype(BF16)
            big[at, :] = total_.astype(BF16)

        swap = []
        for part in range(4):
            streams(4, lambda i, slot: copies_head(i + 4 * part, slot), lambda i, slot: body_head(i + 4 * part, slot))
            if part % 2 == 1:
                rows = pl.ds(320 * (2 * (part // 2)), 640)
                swap.append(net.push(dfar.at[:, rows, :], grad_kv_far.at[layer, :, rows, :], to_core,
                                     swapped_half.at[part // 2]))
            yield
        for copy in swap:
            copy.wait()

        def copies_far(i, slot):
            return [pltpu.make_async_copy(grad_kv_far.at[layer, :, tile(i, 128), :], far_in.at[slot], lsem.at[slot])]

        def body_far(i, slot):
            at = tile(i, 128)
            query = big[at, :].T
            gp[:, at] = query
            sums[layer, 20:21, at] = jnp.sum(query.astype(F32), axis=0, keepdims=True) * scale
            for which in range(2):
                rows = pl.ds(pl.multiple_of(1280 + which * 1280 + i * 128, 128), 128)
                both = (big[rows, :].astype(F32) + far_in[slot, which].astype(F32)).astype(BF16).T
                gp[:, pl.ds(pl.multiple_of(1280 + which * 1280 + i * 128, 128), 128)] = both
                if which == 1:
                    sums[layer, 21:22, at] = jnp.sum(both.astype(F32), axis=0, keepdims=True)

        streams(10, copies_far, body_far)
        swap = [
            net.push(gp.at[:, pl.ds(pl.multiple_of(t * 1280 + (1 - core) * 640, 128), 640)], grad_far.at[layer, t],
                     to_core, swapped)
            for t in range(3)
        ]
        yield

        def copies_back(i, slot):
            return [pltpu.make_async_copy(attn_full.at[layer, i // 5, tile(i % 5, 256), :],
                                          wide_w.at[slot, pl.ds(0, 256), :], lsem.at[slot])]

        def body_back(i, slot):
            at = tile(i % 5, 256)
            out = dot(gp[:, pl.ds(pl.multiple_of((i // 5) * 1280, 128), 1280)], wide_w[slot, :256, :], NT)

            @pl.when(i < 5)
            def _():
                gh[:, at] = out * scale

            @pl.when(i >= 5)
            def _():
                gh[:, at] += out

        streams(5, copies_back, body_back)
        for copy in swap:
            copy.wait()
        fetch(*[(grad_far.at[layer, t], gs.at[:, pl.ds(t * 640, 640)]) for t in range(3)])
        for group in ((0, 1), (2,)):
            weight_gradient(
                320, lambda i: rows_of(normed_t, i), lambda i: rows_of(normed_far, i),
                [(lambda t=t: gp[:, pl.ds(pl.multiple_of(t * 1280 + core * 640, 128), 640)],
                  lambda t=t: gs[:, t * 640 : t * 640 + 640], scale if t == 0 else 1.0,
                  [(t % 2, order_of(9 + t), 0)]) for t in group],
            )
            for t in group:
                send_item(order_of(9 + t), small_spot(qkv_out.at[layer, t]))
            yield
        streams(10, lambda i, slot: copies_back(i + 5, slot), lambda i, slot: body_back(i + 5, slot))
        yield
        norm_back(states.at[layer], vec[0:1, :], 18, layer, False)
        if layer == 0:
            returned.extend(give_back(low.at[0], grad_out, 2))
        yield

    sum_programs = [sum_program(0, 1, 0, 24), sum_program(1, 0, 0, 16), sum_program(2, 0, 16, 8)]
    segments = itertools.chain.from_iterable(work(layer) for layer in reversed(range(layers)))
    for action in PLAN:
        if action == -1:
            next(segments)
        elif action < 0:
            next(sum_programs[-2 - action])
        else:
            advance(action)
    for copy in returned:
        copy.wait()
    assert next(segments, None) is None and all(s == 7 for s in stage)
    net.drain()


def backward_all(cotangent, final, weights, kept, vectors, masks):
    any_ = pl.BlockSpec(memory_space=pl.ANY)
    vmem = pl.BlockSpec(memory_space=pltpu.VMEM)
    layers = vectors.shape[0]
    t = TOKENS

    def hbm(shape, dtype=BF16):
        return jax.ShapeDtypeStruct((layers,) + shape, dtype)

    out_shape = (
        jax.ShapeDtypeStruct(cotangent.shape, BF16), jax.ShapeDtypeStruct(cotangent.shape, BF16),
        hbm((1280, 1280)), hbm((320, 5120)), hbm((320, 1280)), hbm((3, 320, 1280)),
        hbm((24, 1280), F32),
        hbm((t, 1280)), hbm((t, 2560)), hbm((t, 640)), hbm((3, t, 640)), hbm((2, 1280, t)),
    )
    v = pltpu.VMEM
    items = ITEMS_A_LAYER * layers
    return pl.pallas_call(
        functools.partial(backward_kernel, layers),
        out_shape=out_shape,
        in_specs=[any_] * 19 + [vmem] * 2,
        out_specs=(any_,) * 6 + (vmem,) + (any_,) * 5,
        scratch_shapes=[
            v((t, 1280), F32), v((2, t, 1280), BF16), v((t, 5120), BF16), v((t, 2560), BF16), v((t, 1280), F32),
            v((2, 64, 1280), F32), v((5120, t), BF16), v((2, 1280, t), BF16), v((2, 5, 80, t), BF16), v((2, 2, 128, t), BF16),
            v((H, 1, t), F32), v((2, 512, 1280), BF16), v((2, t, 512), BF16), v((2, 2, 640, t), BF16),
            v((XRING, 2, 4, 2, 80, 640), BF16), v((RING, 4, 2, 80, 640), BF16), v((RING, 6, 80, 640), BF16),
            v((RING, 3, 80, 640), BF16), v((RING, 80, 640), BF16),
            v((layers, 4, 24, 1280), F32), v((layers, 6, 24, 1280), F32),
            pltpu.SemaphoreType.DMA, pltpu.SemaphoreType.DMA((2,)), pltpu.SemaphoreType.DMA,
            pltpu.SemaphoreType.DMA((2,)),
            pltpu.SemaphoreType.DMA((RING, 4)), pltpu.SemaphoreType.DMA((RING,)), pltpu.SemaphoreType.DMA((3, 4)),
            pltpu.SemaphoreType.DMA((4,)), pltpu.SemaphoreType.DMA((4,)), pltpu.SemaphoreType.DMA,
            pltpu.SemaphoreType.DMA((items * 12 + 16 * layers + 8,)),
        ],
        compiler_params=pltpu.CompilerParams(collective_id=2, has_side_effects=True, vmem_limit_bytes=63 << 20),
        name="backward_all",
    )(cotangent, final, *weights, *kept, vectors, masks)


def plane_shards(
    inputs, lengths, cotangent, attn_gain, attn_shift, query_weight, query_bias, key_weight,
    value_weight, value_bias, out_weight, out_bias, mlp_gain, mlp_shift, up_weight, up_bias,
    down_weight, down_bias,
):
    z = lax.axis_index("shard")
    layers = attn_gain.shape[0]
    rows = jnp.concatenate(
        [attn_gain, attn_shift, query_bias, value_bias, out_bias, mlp_gain, mlp_shift, down_bias], axis=1
    ).reshape(layers, 8, 320)
    part = jnp.zeros((layers, 24, 1280), BF16)
    part = lax.dynamic_update_slice(part, rows, (0, 0, z * 320))
    wide = lax.dynamic_update_slice(jnp.zeros((layers, 5120), BF16), up_bias, (0, z * 1280)).reshape(layers, 10, 512)
    part = lax.dynamic_update_slice(part, wide, (0, 8, 0))
    spread = jnp.broadcast_to(lengths.astype(F32)[:, None, None], (2, 8, 128))
    results = forward_all(
        inputs, cotangent, (query_weight, key_weight, value_weight, out_weight, up_weight, down_weight), part, spread
    )
    weights, kept = results[:3], list(results[3:17])
    cotangent, final, table, masks = results[17:]
    kept[8] = kept[8].reshape(layers, 4, 2, 640, -1)
    output, grad, down_grad, up_grad, out_grad, qkv_grad, small = backward_all(
        cotangent, final, weights, kept, table, masks
    )[:7]
    input_grad = grad.astype(F32)
    small_rows = jnp.concatenate([small[:, 18:22], small[:, 4:8]], axis=1)
    sums = jnp.concatenate([small_rows.reshape(layers, -1), small[:, 8:18, :512].reshape(layers, -1)], axis=1)
    vec = pick(sums[:, :10240].reshape(layers, 8, 4, 320), z, 2)
    up_bias_grad = pick(sums[:, 10240:].reshape(layers, 4, 1280), z, 1)

    query_grad, key_grad, value_grad = [qkv_grad[:, i].astype(F32) for i in range(3)]
    out_grad, up_grad, down_grad = out_grad.astype(F32), up_grad.astype(F32), down_grad.astype(F32)
    return (
        output, input_grad, vec[:, 0], vec[:, 1], query_grad, vec[:, 2], key_grad, value_grad,
        vec[:, 3], out_grad, vec[:, 4], vec[:, 5], vec[:, 6], up_grad, up_bias_grad, down_grad,
        vec[:, 7],
    )


def pick_body(mesh):
    if mesh.shape["rep"] == 8 and mesh.shape["shard"] == 4:
        return plane_shards
    return general_shards


def solution(mesh):
    body = pick_body(mesh)
    placed = (
        P("rep", "shard", None),
        P("rep"),
        P("rep", "shard", None),
        P(None, "shard"),
        P(None, "shard"),
        P(None, "shard", None),
        P(None, "shard"),
        P(None, "shard", None),
        P(None, "shard", None),
        P(None, "shard"),
        P(None, "shard", None),
        P(None, "shard"),
        P(None, "shard"),
        P(None, "shard"),
        P(None, "shard", None),
        P(None, "shard"),
        P(None, "shard", None),
        P(None, "shard"),
    )
    return jax.shard_map(
        body,
        mesh=mesh,
        in_specs=placed,
        out_specs=(
            P("rep", "shard", None),
            P("rep", "shard", None),
            P(None, "shard"),
            P(None, "shard"),
            P(None, "shard", None),
            P(None, "shard"),
            P(None, "shard", None),
            P(None, "shard", None),
            P(None, "shard"),
            P(None, "shard", None),
            P(None, "shard"),
            P(None, "shard"),
            P(None, "shard"),
            P(None, "shard", None),
            P(None, "shard"),
            P(None, "shard", None),
            P(None, "shard"),
        ),
        check_vma=False,
    )
```
